32 devices in a mesh: dp: 4 (over y, x), row: 2 (over core), col: 4 (over z).
Axes of the slice: x: 2, y: 2, z: 4, core: 2. Of those that a mesh axis runs over, the one named last changes fastest.
Arguments:
- inputs: bfloat16 [32768, 1024], P(('dp', 'col'), 'row'), may hold values from -6 to 6
- w_query: bfloat16 [1024, 1024], P(('dp', 'col'), 'row'), may hold values from -0.1875 to 0.1875
- w_key: bfloat16 [1024, 1024], P(('dp', 'col'), 'row'), may hold values from -0.1875 to 0.1875
- w_value: bfloat16 [1024, 1024], P(('dp', 'col'), 'row'), may hold values from -0.1875 to 0.1875
- w_out: bfloat16 [1024, 1024], P('row', ('dp', 'col')), may hold values from -3 to 3
- w_gate: bfloat16 [1024, 2816], P(('dp', 'col'), 'row'), may hold values from -0.1875 to 0.1875
- w_up: bfloat16 [1024, 2816], P(('dp', 'col'), 'row'), may hold values from -0.1875 to 0.1875
- w_down: bfloat16 [2816, 1024], P('row', ('dp', 'col')), may hold values from -0.109375 to 0.109375
- norm_one: bfloat16 [1024], P(('dp', 'col')), may hold values from 0.5 to 1.5
- norm_two: bfloat16 [1024], P(('dp', 'col')), may hold values from 0.5 to 1.5
- cache_keys: bfloat16 [32, 512, 1024], P(('dp', 'col'), None, 'row'), may hold values from -6 to 6
- cache_values: bfloat16 [32, 512, 1024], P(('dp', 'col'), None, 'row'), may hold values from -6 to 6
- own_index: int32 [32, 2, 2], P(('dp', 'col')), may hold values from 0 to 3
- partner_index: int32 [32, 2, 2], P(('dp', 'col')), may hold values from 0 to 3
- picture_start: int32 [32, 2], P(('dp', 'col')), may hold values from 0 to 768, as said below
- partner_seq: int32 [32], P(('dp', 'col')), may hold values from 0 to 31, as said below
- cotangent: bfloat16 [32768, 1024], P(('dp', 'col'), 'row'), may hold values from -6 to 6
Outputs:
- output: bfloat16 [32768, 1024], P(('dp', 'col'), 'row')
- input_grad: bfloat16 [32768, 1024], P(('dp', 'col'), 'row')
- grad_query: float32 [1024, 1024], P(('dp', 'col'), 'row')
- grad_key: float32 [1024, 1024], P(('dp', 'col'), 'row')
- grad_value: float32 [1024, 1024], P(('dp', 'col'), 'row')
- grad_out: float32 [1024, 1024], P('row', ('dp', 'col'))
- grad_gate: float32 [1024, 2816], P(('dp', 'col'), 'row')
- grad_up: float32 [1024, 2816], P(('dp', 'col'), 'row')
- grad_down: float32 [2816, 1024], P('row', ('dp', 'col'))
- grad_norm_one: float32 [1024], P(('dp', 'col'))
- grad_norm_two: float32 [1024], P(('dp', 'col'))
The draws below stay inside these ranges and needn't reach their ends.
Inputs may be any that keep to these rules, and one draw needn't show every extreme that they name: partner_seq[s] = (s + k * 4 * 2) mod 32 for some whole k from 1 to 3, drawn for each sequence s. `picture_start`: each sequence has two picture spans of 256 tokens; the first starts at or before 1024 // 2 - 256, the second at or after 1024 // 2.
All inputs are finite; a program needn't handle non-finite values.
Results may differ from the reference program's by a relative error of at most 0.019.
Values may be sent and summed in bfloat16 or wider, within the bound.
A program may use at most 256 MiB of HBM per device.

```python
import jax
import jax.numpy as jnp
from jax import lax

D = 1024
HEADS = 8
HEAD_DIM = 128
FF = 2816
SEQ_LEN = 1024
QROWS = 512
PIC = 256
MEM_BLK = 128
CACHE_BLK = 4
OWN_K = 2
PART_K = 2
SEQ_DEV = 2
SEQS = 32
TOKENS = 32768
QBLKS = 2
CACHE_ROWS = 512
MEMROWS = 512
REPLICAS = 4
COLUMNS = 4


def draw_partner_seq(key, part):
    sequence = jnp.arange(SEQS, dtype=jnp.int32)
    offsets = jax.random.randint(key, (SEQS,), 1, REPLICAS, dtype=jnp.int32)
    return (sequence + offsets * (COLUMNS * SEQ_DEV)) % SEQS


def draw_picture_start(key, part):
    early_key, late_key = jax.random.split(key)
    halfway = SEQ_LEN // 2
    early_start = jax.random.randint(early_key, (SEQS, 1), 0, halfway - PIC + 1, dtype=jnp.int32)
    late_start = jax.random.randint(late_key, (SEQS, 1), halfway, SEQ_LEN - PIC + 1, dtype=jnp.int32)
    return jnp.concatenate([early_start, late_start], axis=1)


def with_ends(values, rng, least, top_value):
    shape = values.shape
    index_at = [jax.random.randint(jax.random.fold_in(rng, axis), (), 0, shape[axis]) for axis in range(len(shape))]
    values = values.at[tuple(index_at)].set(least)
    longest = shape.index(max(shape))
    index_at[longest] = (index_at[longest] + 1) % shape[longest]
    return values.at[tuple(index_at)].set(top_value)


def spiked(result, rng, source, target, shards_of, factor):
    owner, partner = [(jnp.arange(result.shape[position]) // (result.shape[position] // shards_of)).reshape([-1 if axis == position else 1 for axis in range(result.ndim)]) for position in (source, target)]
    chosen = jax.random.permutation(rng, shards_of)[partner]
    strong = (owner == chosen) | (owner == (partner + shards_of // 2) % shards_of)
    return jnp.where(strong, factor * result, result)


def level_of(rng, shape, shards, smallest, high):
    loudness = 1.0
    for position, blocks in shards:
        steps = jax.random.uniform(jax.random.fold_in(jax.random.fold_in(rng, 6), position), (blocks,), jnp.float32, smallest / len(shards), high / len(shards))
        loudness = loudness * jnp.repeat(jnp.exp(steps), shape[position] // blocks).reshape((-1,) + (1,) * (len(shape) - 1 - position))
    return loudness


def gaussian(key, extent, spread, bound, cuts=(), held_as=jnp.bfloat16):
    result = spread * jax.random.normal(key, extent, jnp.float32)
    if cuts:
        result = result * level_of(key, extent, cuts, -0.22, 0.18)
    return jnp.clip(result, -bound, bound).astype(held_as)


def heavy_noise(key, shape, spread, most, shards, heavy, kind=jnp.bfloat16):
    result = spread * jax.random.normal(key, shape, jnp.float32)
    if shards:
        result = result * level_of(key, shape, shards, -0.22, 0.18)
    return jnp.clip(spiked(result, jax.random.fold_in(key, 3), *heavy), -most, most).astype(kind)


def setup_inputs(seed: int = 0) -> dict:
    keys = jax.random.split(jax.random.key(seed), 18)
    return {
        "inputs": gaussian(keys[0], (TOKENS, D), 1.0, 6.0, ((0, 16), (1, 2))),
        "w_query": gaussian(keys[1], (D, D), D ** -0.5, 0.1875, ((0, 16), (1, 2))),
        "w_key": gaussian(keys[2], (D, D), D ** -0.5, 0.1875, ((0, 16), (1, 2))),
        "w_value": gaussian(keys[3], (D, D), D ** -0.5, 0.1875, ((0, 16), (1, 2))),
        "w_out": gaussian(keys[4], (D, D), (max(D // 256, 1)) ** -0.5, 3.0, ((0, 2), (1, 16))),
        "w_gate": gaussian(keys[5], (D, FF), D ** -0.5, 0.1875, ((0, 16), (1, 2))),
        "w_up": gaussian(keys[6], (D, FF), D ** -0.5, 0.1875, ((0, 16), (1, 2))),
        "w_down": gaussian(keys[7], (FF, D), FF ** -0.5, 0.109375, ((0, 2), (1, 16))),
        "norm_one": jnp.clip(1.0 + 0.1 * jax.random.normal(keys[8], (D,), jnp.float32), 0.5, 1.5).astype(jnp.bfloat16),
        "norm_two": jnp.clip(1.0 + 0.1 * jax.random.normal(keys[9], (D,), jnp.float32), 0.5, 1.5).astype(jnp.bfloat16),
        "cache_keys": gaussian(keys[10], (SEQS, CACHE_ROWS, D), 1.0, 6.0, ((0, 16), (2, 2))),
        "cache_values": gaussian(keys[11], (SEQS, CACHE_ROWS, D), 1.0, 6.0, ((0, 16), (2, 2))),
        "own_index": with_ends(jax.random.randint(keys[12], (SEQS, QBLKS, OWN_K), 0, CACHE_BLK), jax.random.fold_in(keys[12], 1), 0, CACHE_BLK - 1).astype(jnp.int32),
        "partner_index": with_ends(jax.random.randint(keys[13], (SEQS, QBLKS, PART_K), 0, CACHE_BLK), jax.random.fold_in(keys[13], 1), 0, CACHE_BLK - 1).astype(jnp.int32),
        "picture_start": draw_picture_start(jax.random.fold_in(keys[17], 71), 0),
        "partner_seq": draw_partner_seq(jax.random.fold_in(keys[17], 71), 0),
        "cotangent": heavy_noise(keys[16], (TOKENS, D), 1.0, 6.0, ((0, 16), (1, 2)), (0, 1, 16, 2.0)),
    }


@jax.custom_vjp
def low(v):
    return lax.optimization_barrier(v.astype(jnp.bfloat16)).astype(jnp.float32)

@jax.custom_vjp
def low_back(v):
    return v

def low_keep(v):
    return (low(v), None)

def low_pass(kept, grad):
    return (grad,)

def back_keep(v):
    return (v, None)

def back_low(kept, grad):
    return (low(grad),)
low.defvjp(low_keep, low_pass)
low_back.defvjp(back_keep, back_low)
EPSILON = 1e-05
HIGHEST = lax.Precision.HIGHEST

def matmul(former, latter):
    return jnp.dot(former, latter, precision=HIGHEST, preferred_element_type=jnp.float32)

def rmsnorm(values, gain):
    return values * lax.rsqrt(lax.optimization_barrier(jnp.mean(values * values, axis=-1, keepdims=True)) + EPSILON) * gain

def rotary_tables(amount):
    frequency = 10000.0 ** (-2.0 * jnp.arange(HEAD_DIM // 2, dtype=jnp.float32) / HEAD_DIM)
    positions = (jnp.arange(amount, dtype=jnp.int32) % SEQ_LEN).astype(jnp.float32)
    angles = positions[:, None] * frequency[None, :]
    return (jnp.concatenate([jnp.cos(angles)] * 2, axis=1), jnp.concatenate([jnp.sin(angles)] * 2, axis=1))

def rotate(values, cosine_table, sine_table):
    halfwidth = values.shape[-1] // 2
    turned = jnp.concatenate([-values[..., halfwidth:], values[..., :halfwidth]], axis=-1)
    return values * cosine_table[:, None, :] + turned * sine_table[:, None, :]

def picture_mask(starts):
    positions = jnp.arange(SEQ_LEN, dtype=jnp.int32)
    inside = (positions[None, :] >= starts[:, None]) & (positions[None, :] < starts[:, None] + PIC)
    shared = jnp.any(inside[:, :, None] & inside[:, None, :], axis=0)
    return (positions[None, :] <= positions[:, None]) | shared

def attend_sequence(bundle):
    queries, key_rows, value_rows, mem_keys, mem_values, starts = bundle
    allowed = picture_mask(starts)
    scaling = HEAD_DIM ** (-0.5)
    blocks = []
    for qblock in range(QBLKS):
        row_span = slice(qblock * QROWS, (qblock + 1) * QROWS)
        key_all = jnp.concatenate([key_rows, mem_keys[qblock]], axis=0)
        value_all = jnp.concatenate([value_rows, mem_values[qblock]], axis=0)
        scores = low_back(jnp.einsum('qhd,khd->hqk', queries[row_span], key_all, precision=HIGHEST) * scaling)
        visible = jnp.concatenate([allowed[row_span], jnp.ones((QROWS, MEMROWS), dtype=jnp.bool_)], axis=1)
        scores = jnp.where(visible[None], scores, -1e+30)
        shares = jax.nn.softmax(scores, axis=-1)
        blocks.append(jnp.einsum('hqk,khd->qhd', low(shares), value_all, precision=HIGHEST))
    return jnp.concatenate(blocks, axis=0)

def memory_blocks(storage, sequence, chosen):
    cache_table = storage[sequence].astype(jnp.float32).reshape(CACHE_BLK, MEM_BLK, D)
    return cache_table[chosen]

def reference(inputs, w_query, w_key, w_value, w_out, w_gate, w_up, w_down, norm_one, norm_two, cache_keys, cache_values, own_index, partner_index, picture_start, partner_seq, cotangent):
    groups = SEQS // 2
    cosine_table, sine_table = rotary_tables(2 * SEQ_LEN)
    selves = jnp.arange(SEQS, dtype=jnp.int32).reshape(groups, 2)

    def memory(storage, own_chosen, far_chosen, own_seqs, far_seqs):
        near_blocks = jax.vmap(memory_blocks, in_axes=(None, 0, 0))(storage, own_seqs, own_chosen)
        far_blocks = jax.vmap(memory_blocks, in_axes=(None, 0, 0))(storage, far_seqs, far_chosen)
        joined = jnp.concatenate([near_blocks, far_blocks], axis=2)
        return joined.reshape(2, QBLKS, MEMROWS, HEADS, HEAD_DIM)

    def forward(inputs_f, weights):
        weight_query, weight_key, weight_value, weight_out, weight_gate, weight_up, weight_down, gain_one, gain_two = weights

        def group_layer(bundle):
            tokens, own_chosen, far_chosen, starts, own_seqs, far_seqs = bundle
            normed_one = low(rmsnorm(tokens, gain_one))
            queries = low(rotate(low_back(matmul(normed_one, weight_query)).reshape(-1, HEADS, HEAD_DIM), cosine_table, sine_table))
            key_rows = low(rotate(low_back(matmul(normed_one, weight_key)).reshape(-1, HEADS, HEAD_DIM), cosine_table, sine_table))
            value_rows = low(low_back(matmul(normed_one, weight_value))).reshape(-1, HEADS, HEAD_DIM)
            mem_keys = memory(cache_keys, own_chosen, far_chosen, own_seqs, far_seqs)
            mem_values = memory(cache_values, own_chosen, far_chosen, own_seqs, far_seqs)
            shaped = (2, SEQ_LEN, HEADS, HEAD_DIM)
            attended = lax.map(jax.checkpoint(attend_sequence), (queries.reshape(shaped), key_rows.reshape(shaped), value_rows.reshape(shaped), mem_keys, mem_values, starts))
            mixture = low(low_back(attended.reshape(-1, D)))
            hidden = tokens + low_back(matmul(mixture, weight_out))
            normed_two = low(rmsnorm(hidden, gain_two))
            gating = low_back(matmul(normed_two, weight_gate))
            upward = low_back(matmul(normed_two, weight_up))
            active = low(jax.nn.silu(gating) * upward)
            return hidden + low_back(matmul(active, weight_down))
        packed = (inputs_f.reshape(groups, 2 * SEQ_LEN, D), own_index.reshape(groups, 2, QBLKS, OWN_K), partner_index.reshape(groups, 2, QBLKS, PART_K), picture_start.reshape(groups, 2, 2), selves, partner_seq.reshape(groups, 2))
        return lax.map(jax.checkpoint(group_layer), packed).reshape(TOKENS, D)
    weights = tuple((matrix.astype(jnp.float32) for matrix in (w_query, w_key, w_value, w_out, w_gate, w_up, w_down, norm_one, norm_two)))
    outputs, pullback = jax.vjp(forward, inputs.astype(jnp.float32), weights)
    grad_inputs, grad_weights = pullback(cotangent.astype(jnp.float32))
    return (outputs.astype(jnp.bfloat16), grad_inputs.astype(jnp.bfloat16), grad_weights[0], grad_weights[1], grad_weights[2], grad_weights[3], grad_weights[4], grad_weights[5], grad_weights[6], grad_weights[7], grad_weights[8])
```

```python
import functools
import math

import jax
import jax.numpy as jnp
from jax import lax
from jax.experimental import pallas as pl
from jax.experimental.pallas import tpu as pltpu
from jax.sharding import PartitionSpec as P

HEAD_DIM = 128
SEQ_LEN = 1024
QROWS = 512
PIC = 256
MEM_BLK = 128
OWN_K = 2
PART_K = 2
SEQ_DEV = 2
QBLKS = 2
EPSILON = 1e-05
NEG = -1e30
CHUNK = 256
LANES = 128

BF = jnp.bfloat16
F32 = jnp.float32
LOG2E = math.log2(math.e)


def nn(a, b):
    return jnp.dot(a, b, preferred_element_type=F32)


def nt(a, b):
    return lax.dot_general(a, b, (((1,), (1,)), ((), ())), preferred_element_type=F32)


def tn(a, b):
    return lax.dot_general(a, b, (((0,), (0,)), ((), ())), preferred_element_type=F32)


def rotary_tables():
    half = HEAD_DIM // 2
    frequency = 10000.0 ** (-2.0 * jnp.arange(half, dtype=F32) / HEAD_DIM)
    angles = jnp.arange(SEQ_LEN, dtype=jnp.int32).astype(F32)[:, None] * frequency[None, :]
    cosine, sine = jnp.cos(angles), jnp.sin(angles)
    return jnp.concatenate([cosine, cosine], axis=1), jnp.concatenate([-sine, sine], axis=1)


def whole(shape):
    return pl.BlockSpec(shape, lambda *_: (0,) * len(shape))


def params(limit=60):
    return pltpu.CompilerParams(
        vmem_limit_bytes=limit * 1024 * 1024, dimension_semantics=None
    )


def chunks(total, body, size=CHUNK):
    def step(i, carry):
        body(pl.ds(pl.multiple_of(i * size, size), size))
        return carry

    lax.fori_loop(0, total // size, step, 0)


def qkv_kernel(x_ref, gain_ref, w_ref, cos_ref, sin_ref, out_ref, n1_ref):
    part = pl.program_id(0)
    model = x_ref.shape[1]

    @pl.when((part == 0) & (pl.program_id(1) == 0))
    def _():
        def norm(rows):
            x = x_ref[rows, :].astype(F32)
            inverse = lax.rsqrt(jnp.mean(x * x, axis=1, keepdims=True) + EPSILON)
            n1_ref[rows, :] = (x * inverse * gain_ref[...]).astype(BF)

        chunks(x_ref.shape[0], norm)

    def project(rows):
        y = nn(n1_ref[rows, :], w_ref[...].reshape(model, -1))
        cosine, sine = cos_ref[rows, :], sin_ref[rows, :]
        for h in range(y.shape[1] // HEAD_DIM):
            lanes = slice(h * HEAD_DIM, (h + 1) * HEAD_DIM)
            u = y[:, lanes]
            turned = u * cosine + pltpu.roll(u, HEAD_DIM // 2, 1) * sine
            out_ref[0, rows, lanes] = jnp.where(part < 2, turned, u).astype(BF)

    chunks(x_ref.shape[0], project)


def project_qkv(x, gain, gathered, cosine, sine):
    tokens, model = x.shape
    groups, halves, rows, _ = gathered.shape
    half = model // halves
    return pl.pallas_call(
        qkv_kernel,
        grid=(3, halves),
        in_specs=[
            whole(x.shape),
            whole(gain.shape),
            pl.BlockSpec((groups, None, rows, half), lambda m, h: (0, h, 0, m)),
            whole(cosine.shape),
            whole(sine.shape),
        ],
        out_specs=pl.BlockSpec((1, tokens, half), lambda m, h: (m, 0, h)),
        out_shape=jax.ShapeDtypeStruct((3, tokens, model), BF),
        scratch_shapes=[pltpu.VMEM((tokens, model), BF)],
        compiler_params=params(),
        name="project_qkv",
    )(x, gain, gathered, cosine, sine)


def fill_memory(idx_ref, near_ref, far_ref, mem_ref):
    for b in range(QBLKS):
        for j in range(OWN_K):
            start = pl.multiple_of(idx_ref[1 + b * OWN_K + j] * MEM_BLK, MEM_BLK)
            mem_ref[b, j * MEM_BLK : (j + 1) * MEM_BLK, :] = near_ref[pl.ds(start, MEM_BLK), :]
        for j in range(PART_K):
            k = QBLKS * OWN_K + b * PART_K + j
            start = pl.multiple_of(idx_ref[1 + k] * MEM_BLK, MEM_BLK)
            at = (OWN_K + j) * MEM_BLK
            mem_ref[b, at : at + MEM_BLK, :] = far_ref[pl.ds(start, MEM_BLK), :]


def masked(scores, start, first):
    keys, queries = scores.shape
    at = first + lax.broadcasted_iota(jnp.int32, (1, queries), 1)
    limit = jnp.where((at >= start) & (at < start + PIC), start + PIC - 1, at)
    key = lax.broadcasted_iota(jnp.int32, (keys, queries), 0)
    return jnp.where(key <= limit, scores, NEG)


def key_parts(b, k_ref, v_ref, kmem_ref, vmem_ref):
    parts = []
    for i in range(b + 1):
        rows = slice(i * QROWS, (i + 1) * QROWS)
        parts.append((k_ref[0, rows, :], v_ref[0, rows, :], i == b, rows))
    parts.append((kmem_ref[b], vmem_ref[b], False, None))
    return parts


def attend_kernel(
    idx_ref, q_ref, k_ref, v_ref, nk_ref, nv_ref, fk_ref, fv_ref, out_ref, lse_ref, kmem_ref, vmem_ref
):
    fill_memory(idx_ref, nk_ref, fk_ref, kmem_ref)
    fill_memory(idx_ref, nv_ref, fv_ref, vmem_ref)
    scale = LOG2E / math.sqrt(HEAD_DIM)
    base = 1 + QBLKS * (OWN_K + PART_K)
    for b in range(QBLKS):
        start = idx_ref[base + b] - b * QROWS

        def body(i, carry, b=b, start=start):
            first = pl.multiple_of(i * CHUNK, CHUNK)
            rows = pl.ds(pl.multiple_of(b * QROWS + first, CHUNK), CHUNK)
            q = q_ref[0, rows, :]
            parts = key_parts(b, k_ref, v_ref, kmem_ref, vmem_ref)
            scores = []
            for k, _, diagonal, _ in parts:
                s = nt(k, q)
                scores.append(masked(s, start, first) if diagonal else s)
            top = functools.reduce(
                jnp.maximum, [jnp.max(s, axis=0, keepdims=True) for s in scores]
            )
            shift = top * scale
            total = jnp.zeros_like(top)
            acc = jnp.zeros((HEAD_DIM, CHUNK), F32)
            for s, (_, v, _, _) in zip(scores, parts):
                e = jnp.exp2(s * scale - shift)
                total = total + jnp.sum(e, axis=0, keepdims=True)
                acc = acc + tn(v, e.astype(BF))
            out_ref[rows, :] = jnp.transpose(acc / total).astype(BF)
            lse_ref[0, :, rows] = shift + jnp.log2(total)
            return carry

        lax.fori_loop(0, QROWS // CHUNK, body, 0)


def head_specs(tokens, cache_rows):
    column = lambda m: pl.BlockSpec((1, tokens, HEAD_DIM), lambda h, idx: (m, 0, h))
    near = pl.BlockSpec((cache_rows, HEAD_DIM), lambda h, idx: (0, h))
    far = pl.BlockSpec((None, cache_rows, HEAD_DIM), lambda h, idx: (idx[0], 0, h))
    return [column(0), column(1), column(2), near, near, far, far]


def attend(idx, qkv, near_k, near_v, far_k, far_v):
    _, tokens, model = qkv.shape
    heads = model // HEAD_DIM
    memory = (QBLKS, (OWN_K + PART_K) * MEM_BLK, HEAD_DIM)
    return pl.pallas_call(
        attend_kernel,
        grid_spec=pltpu.PrefetchScalarGridSpec(
            num_scalar_prefetch=1,
            grid=(heads,),
            in_specs=head_specs(tokens, near_k.shape[0]),
            out_specs=[
                pl.BlockSpec((tokens, HEAD_DIM), lambda h, idx: (0, h)),
                pl.BlockSpec((1, 1, tokens), lambda h, idx: (h, 0, 0)),
            ],
            scratch_shapes=[pltpu.VMEM(memory, BF), pltpu.VMEM(memory, BF)],
        ),
        out_shape=[
            jax.ShapeDtypeStruct((tokens, model), BF),
            jax.ShapeDtypeStruct((heads, 1, tokens), F32),
        ],
        compiler_params=params(),
        name="attend",
    )(idx, qkv, qkv, qkv, near_k, near_v, far_k, far_v)


def attend_back_kernel(
    idx_ref,
    q_ref,
    k_ref,
    v_ref,
    nk_ref,
    nv_ref,
    fk_ref,
    fv_ref,
    o_ref,
    do_ref,
    lse_ref,
    cos_ref,
    sin_ref,
    grad_ref,
    kmem_ref,
    vmem_ref,
    dk_ref,
    dv_ref,
):
    fill_memory(idx_ref, nk_ref, fk_ref, kmem_ref)
    fill_memory(idx_ref, nv_ref, fv_ref, vmem_ref)
    scale = LOG2E / math.sqrt(HEAD_DIM)
    plain = 1.0 / math.sqrt(HEAD_DIM)
    base = 1 + QBLKS * (OWN_K + PART_K)

    def unturn(g, rows):
        return g * cos_ref[rows, :] - pltpu.roll(g, HEAD_DIM // 2, 1) * sin_ref[rows, :]

    dk_ref[...] = jnp.zeros_like(dk_ref)
    dv_ref[...] = jnp.zeros_like(dv_ref)
    for b in range(QBLKS):
        start = idx_ref[base + b] - b * QROWS

        def body(i, carry, b=b, start=start):
            first = pl.multiple_of(i * CHUNK, CHUNK)
            rows = pl.ds(pl.multiple_of(b * QROWS + first, CHUNK), CHUNK)
            q = q_ref[0, rows, :]
            do = do_ref[rows, :]
            lse = lse_ref[0, :, rows]
            dots = jnp.transpose(do.astype(F32) * o_ref[rows, :].astype(F32))
            dot = jnp.sum(dots, axis=0, keepdims=True)
            dq = jnp.zeros((HEAD_DIM, CHUNK), F32)
            for k, v, diagonal, keys in key_parts(b, k_ref, v_ref, kmem_ref, vmem_ref):
                s = nt(k, q)
                if diagonal:
                    s = masked(s, start, first)
                share = jnp.exp2(s * scale - lse)
                ds = (share * (nt(v, do) - dot)).astype(BF)
                if keys is not None:
                    dv_ref[keys, :] += nn(share.astype(BF), do)
                    dk_ref[keys, :] += nn(ds, q)
                dq = dq + tn(k, ds)
            grad_ref[0, rows, :] = unturn(jnp.transpose(dq) * plain, rows).astype(BF)
            return carry

        lax.fori_loop(0, QROWS // CHUNK, body, 0)

    def finish(rows):
        grad_ref[1, rows, :] = unturn(dk_ref[rows, :] * plain, rows).astype(BF)
        grad_ref[2, rows, :] = dv_ref[rows, :].astype(BF)

    chunks(dk_ref.shape[0], finish)


def attend_back(idx, qkv, near_k, near_v, far_k, far_v, attended, grad, lse, cosine, sine):
    _, tokens, model = qkv.shape
    heads = model // HEAD_DIM
    memory = (QBLKS, (OWN_K + PART_K) * MEM_BLK, HEAD_DIM)
    column = pl.BlockSpec((tokens, HEAD_DIM), lambda h, idx: (0, h))
    return pl.pallas_call(
        attend_back_kernel,
        grid_spec=pltpu.PrefetchScalarGridSpec(
            num_scalar_prefetch=1,
            grid=(heads,),
            in_specs=head_specs(tokens, near_k.shape[0])
            + [
                column,
                column,
                pl.BlockSpec((1, 1, tokens), lambda h, idx: (h, 0, 0)),
                whole(cosine.shape),
                whole(sine.shape),
            ],
            out_specs=pl.BlockSpec((3, tokens, HEAD_DIM), lambda h, idx: (0, 0, h)),
            scratch_shapes=[
                pltpu.VMEM(memory, BF),
                pltpu.VMEM(memory, BF),
                pltpu.VMEM((tokens, HEAD_DIM), F32),
                pltpu.VMEM((tokens, HEAD_DIM), F32),
            ],
        ),
        out_shape=jax.ShapeDtypeStruct((3, tokens, model), BF),
        compiler_params=params(),
        name="attend_back",
    )(idx, qkv, qkv, qkv, near_k, near_v, far_k, far_v, attended, grad, lse, cosine, sine)


def split_store(me, value, mine_ref, other_ref, index):
    half = value.shape[1] // 2
    low, high = value[:, :half], value[:, half:]
    mine_ref[index] = jnp.where(me == 0, low, high)
    other_ref[index] = jnp.where(me == 0, high, low)


def feed_kernel(
    me_ref,
    x_ref,
    att_ref,
    cot_ref,
    gain_ref,
    wo_ref,
    wg_ref,
    wu_ref,
    wd_ref,
    out_ref,
    ghid_ref,
    gatt_ref,
    mine_ref,
    other_ref,
    omine_ref,
    oother_ref,
    gn2_ref,
    hid_ref,
    n2_ref,
    n2t_ref,
    cott_ref,
    acc_ref,
    dn_ref,
    a_ref,
    dg_ref,
    du_ref,
):
    tokens, model = x_ref.shape
    half = model // 2
    step = pl.program_id(0)
    me = me_ref[0]

    def joined(ref):
        return jnp.concatenate(
            [ref[:, 0].reshape(model, LANES), ref[:, 1].reshape(model, LANES)], axis=1
        )

    def wo_half(h):
        return wo_ref[:, h].reshape(model, half)

    @pl.when(step == 0)
    def _():
        def start(rows):
            att = att_ref[rows, :]
            hidden = x_ref[rows, :].astype(F32)
            for h in range(2):
                hidden = hidden + nt(att[:, h * half : (h + 1) * half], wo_half(h))
            hid_ref[rows, :] = hidden
            inverse = lax.rsqrt(jnp.mean(hidden * hidden, axis=1, keepdims=True) + EPSILON)
            n2_ref[rows, :] = (hidden * inverse * gain_ref[...]).astype(BF)
            n2t_ref[:, rows] = jnp.transpose(n2_ref[rows, :])
            cott_ref[:, rows] = jnp.transpose(cot_ref[rows, :])
            acc_ref[rows, :] = jnp.zeros((CHUNK, model), F32)
            dn_ref[rows, :] = jnp.zeros((CHUNK, model), F32)

        chunks(tokens, start)

    def forward_back(rows):
        n2 = n2_ref[rows, :]
        gating = nn(n2, joined(wg_ref))
        upward = nn(n2, joined(wu_ref))
        gactive = nn(cot_ref[rows, :], joined(wd_ref))
        sigmoid = 1.0 / (1.0 + jnp.exp(-gating))
        silu = gating * sigmoid
        a_ref[rows, :] = (silu * upward).astype(BF)
        dg_ref[rows, :] = (gactive * upward * (sigmoid + silu * (1.0 - sigmoid))).astype(BF)
        du_ref[rows, :] = (gactive * silu).astype(BF)
        acc_ref[rows, :] += nt(a_ref[rows, :], joined(wd_ref))
        dn_ref[rows, :] += nt(dg_ref[rows, :], joined(wg_ref)) + nt(du_ref[rows, :], joined(wu_ref))

    chunks(tokens, forward_back)

    def weights(rows):
        n2t = n2t_ref[rows, :]
        split_store(me, nn(n2t, dg_ref[...]).astype(BF), mine_ref, other_ref, (0, rows))
        split_store(me, nn(n2t, du_ref[...]).astype(BF), mine_ref, other_ref, (1, rows))
        split_store(me, nn(cott_ref[rows, :], a_ref[...]).astype(BF), mine_ref, other_ref, (2, rows))

    chunks(model, weights)

    @pl.when(step == pl.num_programs(0) - 1)
    def _():
        gn2_ref[...] = jnp.zeros_like(gn2_ref)

        def finish(rows):
            hidden = hid_ref[rows, :]
            out_ref[rows, :] = (hidden + acc_ref[rows, :]).astype(BF)
            inverse = lax.rsqrt(jnp.mean(hidden * hidden, axis=1, keepdims=True) + EPSILON)
            normal = hidden * inverse
            dn = dn_ref[rows, :]
            gn2_ref[...] += jnp.sum(dn * normal, axis=0, keepdims=True)
            scaled = dn * gain_ref[...]
            inward = inverse * (scaled - normal * jnp.mean(scaled * normal, axis=1, keepdims=True))
            ghid = cot_ref[rows, :].astype(F32) + inward
            ghid_ref[rows, :] = ghid
            gmix = ghid.astype(BF)
            n2t_ref[:, rows] = jnp.transpose(gmix)
            for h in range(2):
                gatt_ref[rows, h * half : (h + 1) * half] = nn(gmix, wo_half(h)).astype(BF)

        chunks(tokens, finish)

        def out_weight(rows):
            split_store(me, nn(n2t_ref[rows, :], att_ref[...]).astype(BF), omine_ref, oother_ref, (rows,))

        chunks(model, out_weight)


def feed(me, x, attended, cotangent, gain, gathered, o_at, g_at, u_at, d_at, units):
    tokens, model = x.shape
    groups, halves, rows, _ = gathered.shape
    half = model // halves
    tile = lambda at: pl.BlockSpec(
        (groups, halves, rows, LANES), lambda j, me: (0, 0, 0, at // LANES + j)
    )
    grads = pl.BlockSpec((3, model, LANES), lambda j, me: (0, 0, j))
    full = lambda dtype: jax.ShapeDtypeStruct((tokens, model), dtype)
    big = lambda dtype: pltpu.VMEM((tokens, model), dtype)
    small = pltpu.VMEM((tokens, 2 * LANES), BF)
    steps = units // LANES
    return pl.pallas_call(
        feed_kernel,
        grid_spec=pltpu.PrefetchScalarGridSpec(
            num_scalar_prefetch=1,
            grid=(steps,),
            in_specs=[
                whole(x.shape),
                whole(x.shape),
                whole(x.shape),
                whole(gain.shape),
                pl.BlockSpec((groups, halves, rows, half), lambda j, me: (0, 0, 0, o_at // half)),
                tile(g_at),
                tile(u_at),
                tile(d_at),
            ],
            out_specs=[
                whole(x.shape),
                whole(x.shape),
                whole(x.shape),
                grads,
                grads,
                whole((model, half)),
                whole((model, half)),
                whole(gain.shape),
            ],
            scratch_shapes=[big(F32), big(BF), big(BF), big(BF), big(F32), big(F32), small, small, small],
        ),
        out_shape=[
            full(BF),
            full(F32),
            full(BF),
            jax.ShapeDtypeStruct((3, model, units), BF),
            jax.ShapeDtypeStruct((3, model, units), BF),
            jax.ShapeDtypeStruct((model, half), BF),
            jax.ShapeDtypeStruct((model, half), BF),
            jax.ShapeDtypeStruct(gain.shape, F32),
        ],
        compiler_params=params(),
        name="feed",
    )(me, x, attended, cotangent, gain, gathered, gathered, gathered, gathered)


def back_kernel(
    me_ref,
    x_ref,
    gain_ref,
    w_ref,
    g_ref,
    ghid_ref,
    grad_ref,
    mine_ref,
    other_ref,
    gn1_ref,
    n1t_ref,
    dn_ref,
):
    tokens, model = x_ref.shape
    part, h = pl.program_id(0), pl.program_id(1)
    me = me_ref[0]

    def normal_of(rows):
        x = x_ref[rows, :].astype(F32)
        inverse = lax.rsqrt(jnp.mean(x * x, axis=1, keepdims=True) + EPSILON)
        return x * inverse, inverse

    @pl.when((part == 0) & (h == 0))
    def _():
        def start(rows):
            normal, _ = normal_of(rows)
            n1t_ref[:, rows] = jnp.transpose((normal * gain_ref[...]).astype(BF))
            dn_ref[rows, :] = jnp.zeros((CHUNK, model), F32)

        chunks(tokens, start)

    def inward(rows):
        dn_ref[rows, :] += nt(g_ref[0, rows, :], w_ref[...].reshape(model, -1))

    chunks(tokens, inward)

    def weights(rows):
        value = nn(n1t_ref[rows, :], g_ref[0]).astype(BF)

        @pl.when(h == me)
        def _():
            mine_ref[0, rows, :] = value

        @pl.when(h != me)
        def _():
            other_ref[0, rows, :] = value

    chunks(model, weights)

    @pl.when((part == pl.num_programs(0) - 1) & (h == pl.num_programs(1) - 1))
    def _():
        gn1_ref[...] = jnp.zeros_like(gn1_ref)

        def finish(rows):
            normal, inverse = normal_of(rows)
            dn = dn_ref[rows, :]
            gn1_ref[...] += jnp.sum(dn * normal, axis=0, keepdims=True)
            scaled = dn * gain_ref[...]
            back = inverse * (scaled - normal * jnp.mean(scaled * normal, axis=1, keepdims=True))
            grad_ref[rows, :] = (ghid_ref[rows, :] + back).astype(BF)

        chunks(tokens, finish)


def back(me, x, gain, gathered, grads, ghid):
    tokens, model = x.shape
    groups, halves, rows, _ = gathered.shape
    half = model // halves
    part = pl.BlockSpec((1, model, half), lambda m, h, me: (m, 0, 0))
    return pl.pallas_call(
        back_kernel,
        grid_spec=pltpu.PrefetchScalarGridSpec(
            num_scalar_prefetch=1,
            grid=(3, halves),
            in_specs=[
                whole(x.shape),
                whole(gain.shape),
                pl.BlockSpec((groups, None, rows, half), lambda m, h, me: (0, h, 0, m)),
                pl.BlockSpec((1, tokens, half), lambda m, h, me: (m, 0, h)),
                whole(x.shape),
            ],
            out_specs=[whole(x.shape), part, part, whole(gain.shape)],
            scratch_shapes=[pltpu.VMEM((model, tokens), BF), pltpu.VMEM((tokens, model), F32)],
        ),
        out_shape=[
            jax.ShapeDtypeStruct((tokens, model), BF),
            jax.ShapeDtypeStruct((3, model, half), BF),
            jax.ShapeDtypeStruct((3, model, half), BF),
            jax.ShapeDtypeStruct(gain.shape, F32),
        ],
        compiler_params=params(),
        name="back",
    )(me, x, gain, gathered, grads, ghid)


def swap(value, axis_name):
    return lax.ppermute(value, axis_name, [(0, 1), (1, 0)])


class Lines:
    def __init__(self):
        dp = lax.axis_size("dp")
        self.nx = math.isqrt(dp)
        self.ny = dp // self.nx
        self.nz = lax.axis_size("col")
        d = lax.axis_index("dp")
        self.at = {"x": d % self.nx, "y": d // self.nx, "z": lax.axis_index("col")}
        self.size = {"x": self.nx, "y": self.ny, "z": self.nz}

    def shift(self, value, line, by, sources):
        if line == "z":
            pairs = [(s, s + by) for s in sources]
            return lax.ppermute(value, "col", pairs)
        pairs = []
        for y in range(self.ny):
            for x in range(self.nx):
                if (x if line == "x" else y) in sources:
                    to = (y, x + by) if line == "x" else (y + by, x)
                    pairs.append((y * self.nx + x, to[0] * self.nx + to[1]))
        return lax.ppermute(value, "dp", pairs)

    def both(self, value, line):
        if line == "z":
            return swap(value, "col")
        pairs = []
        for y in range(self.ny):
            for x in range(self.nx):
                to = (y, 1 - x) if line == "x" else (1 - y, x)
                pairs.append((y * self.nx + x, to[0] * self.nx + to[1]))
        return lax.ppermute(value, "dp", pairs)

    def reduce_scatter(self, value, axis, line):
        n, at = self.size[line], self.at[line]
        take = lambda j: lax.dynamic_index_in_dim(value, j, axis, keepdims=False)
        mine = take(at)
        if n == 1:
            return mine
        if n == 2:
            return (mine.astype(F32) + self.both(take(1 - at), line).astype(F32)).astype(BF)
        total = mine.astype(F32)
        for sign in (1, -1):
            carried = None
            for step in range(1, n):
                place = at + sign * (n - step)
                own = take(jnp.clip(place, 0, n - 1))
                if carried is not None:
                    own = (own.astype(F32) + carried.astype(F32)).astype(BF)
                sources = range(0, step) if sign > 0 else range(n - step, n)
                carried = self.shift(own, line, sign, list(sources))
            total = total + carried.astype(F32)
        return total.astype(BF)


def reduce_gradients(lines, mine, other):
    parts, rows, columns = mine.shape
    value = (mine.astype(F32) + swap(other, "row").astype(F32)).astype(BF)
    block = rows // (lines.nx * lines.ny * lines.nz)
    value = value.reshape(parts, lines.ny, lines.nx, lines.nz, 2, block // 2, columns)
    low, high = value[:, :, :, :, 0], value[:, :, :, :, 1]
    low = lines.reduce_scatter(lines.reduce_scatter(low, 2, "x"), 1, "y")
    high = lines.reduce_scatter(lines.reduce_scatter(high, 1, "y"), 1, "x")
    value = jnp.stack([low, high], axis=2).reshape(parts, lines.nz, block, columns)
    return lines.reduce_scatter(value, 1, "z").astype(F32)


def pick_sequence(value, me, axis):
    mine = lax.dynamic_index_in_dim(value, me, 0, keepdims=False)
    got = swap(lax.dynamic_index_in_dim(value, 1 - me, 0, keepdims=False), "row")
    return jnp.where(
        me == 0,
        jnp.concatenate([mine, got], axis=axis),
        jnp.concatenate([got, mine], axis=axis),
    )


def halves_back(value, me):
    half = value.shape[1] // 2
    low, high = value[:, :half], value[:, half:]
    mine = jnp.where(me == 0, low, high)
    got = swap(jnp.where(me == 0, high, low), "row")
    return jnp.where(
        me == 0,
        jnp.concatenate([mine, got], axis=0),
        jnp.concatenate([got, mine], axis=0),
    )


def on_device(
    inputs,
    w_query,
    w_key,
    w_value,
    w_out,
    w_gate,
    w_up,
    w_down,
    norm_one,
    norm_two,
    cache_keys,
    cache_values,
    own_index,
    partner_index,
    picture_start,
    partner_seq,
    cotangent,
):
    lines = Lines()
    me = lax.axis_index("row")
    columns = lax.axis_size("col")
    dp = lax.axis_size("dp")
    half = inputs.shape[1]
    model = 2 * half
    units = w_gate.shape[1]
    rows = w_query.shape[0]
    everywhere = ("dp", "col", "row")
    me_arg = me.reshape(1).astype(jnp.int32)

    x = pick_sequence(inputs.reshape(SEQ_DEV, SEQ_LEN, half), me, 1)
    gains = jnp.pad(jnp.stack([norm_one, norm_two], axis=1), ((0, 0), (0, LANES - 2)))
    first = jnp.concatenate([w_query, w_key, w_value, gains], axis=1)
    second = jnp.concatenate([w_out.T, w_gate, w_up, w_down.T], axis=1)
    shape = (dp * columns, 2, rows)
    first = lax.all_gather(first, everywhere, axis=0, tiled=True).reshape(*shape, -1)
    second = lax.all_gather(second, everywhere, axis=0, tiled=True).reshape(*shape, -1)
    gains = first[:, 0, :, 3 * half : 3 * half + 2].reshape(model, 2).astype(F32)
    gain_one, gain_two = gains[:, 0].reshape(1, model), gains[:, 1].reshape(1, model)
    caches = jnp.concatenate([cache_keys, cache_values], axis=1)
    near = pick_sequence(caches, me, 1)
    cot = pick_sequence(cotangent.reshape(SEQ_DEV, SEQ_LEN, half), me, 1)
    cache_rows = cache_keys.shape[1]
    far = lax.all_gather(near, "dp", axis=0)
    near_k, near_v = near[:cache_rows], near[cache_rows:]
    far_k, far_v = far[:, :cache_rows], far[:, cache_rows:]

    pick = lambda table: lax.dynamic_index_in_dim(table, me, 0, keepdims=False).reshape(-1)
    source = lax.dynamic_index_in_dim(partner_seq, me, 0) // SEQ_DEV // columns
    idx = jnp.concatenate([source, pick(own_index), pick(partner_index), pick(picture_start)])
    cosine, sine = rotary_tables()

    qkv = project_qkv(x, gain_one, first, cosine, sine)
    attended, lse = attend(idx, qkv, near_k, near_v, far_k, far_v)
    o_at, g_at = 0, half
    u_at, d_at = g_at + units, g_at + 2 * units
    out, ghid, gatt, mine, other, omine, oother, gn2 = feed(
        me_arg, x, attended, cot, gain_two, second, o_at, g_at, u_at, d_at, units
    )
    feed_grads = reduce_gradients(lines, mine, other)
    grads = attend_back(
        idx, qkv, near_k, near_v, far_k, far_v, attended, gatt, lse, cosine, sine
    )
    input_grad, pmine, pother, gn1 = back(me_arg, x, gain_one, first, grads, ghid)
    pmine = jnp.concatenate([pmine, omine[None]], axis=0)
    pother = jnp.concatenate([pother, oother[None]], axis=0)
    model_grads = reduce_gradients(lines, pmine, pother)
    norms = lax.psum_scatter(
        jnp.stack([gn1[0], gn2[0]], axis=1), ("dp", "col"), scatter_dimension=0, tiled=True
    )
    norms = lax.psum(norms, "row")
    return (
        halves_back(out, me),
        halves_back(input_grad, me),
        model_grads[0],
        model_grads[1],
        model_grads[2],
        model_grads[3].T,
        feed_grads[0],
        feed_grads[1],
        feed_grads[2].T,
        norms[:, 0],
        norms[:, 1],
    )


def solution(mesh):
    tokens = P(("dp", "col"), "row")
    down = P("row", ("dp", "col"))
    gain = P(("dp", "col"))
    cache = P(("dp", "col"), None, "row")
    index = P(("dp", "col"), None, None)
    weights = (tokens, tokens, tokens, down, tokens, tokens, down)
    return jax.shard_map(
        on_device,
        mesh=mesh,
        in_specs=(tokens,)
        + weights
        + (gain, gain, cache, cache, index, index, P(("dp", "col"), None), gain, tokens),
        out_specs=(tokens, tokens) + weights + (gain, gain),
        check_vma=False,
    )
```

```python
import functools
import math

import jax
import jax.numpy as jnp
from jax import lax
from jax.experimental import pallas as pl
from jax.experimental.pallas import tpu as pltpu
from jax.sharding import PartitionSpec as P

HEAD_DIM = 128
SEQ_LEN = 1024
QROWS = 512
PIC = 256
MEM_BLK = 128
OWN_K = 2
PART_K = 2
SEQ_DEV = 2
QBLKS = 2
EPSILON = 1e-05
NEG = -1e30
CHUNK = 256
LANES = 128

BF = jnp.bfloat16
F32 = jnp.float32
LOG2E = math.log2(math.e)
MESH = pl.DeviceIdType.MESH


def nn(a, b):
    return jnp.dot(a, b, preferred_element_type=F32)


def nt(a, b):
    return lax.dot_general(a, b, (((1,), (1,)), ((), ())), preferred_element_type=F32)


def tn(a, b):
    return lax.dot_general(a, b, (((0,), (0,)), ((), ())), preferred_element_type=F32)


def rotary_tables():
    half = HEAD_DIM // 2
    frequency = 10000.0 ** (-2.0 * jnp.arange(half, dtype=F32) / HEAD_DIM)
    angles = jnp.arange(SEQ_LEN, dtype=jnp.int32).astype(F32)[:, None] * frequency[None, :]
    cosine, sine = jnp.cos(angles), jnp.sin(angles)
    return jnp.concatenate([cosine, cosine], axis=1), jnp.concatenate([-sine, sine], axis=1)


def whole(shape):
    return pl.BlockSpec(shape, lambda *_: (0,) * len(shape))


def once(shape):
    return pl.BlockSpec(shape, lambda *_: (0,) * len(shape), pipeline_mode=pl.Buffered(1))


def params(limit=60):
    return pltpu.CompilerParams(
        vmem_limit_bytes=limit * 1024 * 1024
    )


def chunks(total, body, size=CHUNK):
    def step(i, carry):
        body(pl.ds(pl.multiple_of(i * size, size), size))
        return carry

    lax.fori_loop(0, total // size, step, 0)


class Place:
    def __init__(self, nz):
        dp, self.me, self.z = lax.axis_index("dp"), lax.axis_index("row"), lax.axis_index("col")
        self.x, self.y, self.nz = dp % 2, dp // 2, nz
        self.core = (dp, 1 - self.me, self.z)
        self.next_x = (self.y * 2 + 1 - self.x, self.me, self.z)
        self.next_y = ((1 - self.y) * 2 + self.x, self.me, self.z)
        self.above = (dp, self.me, self.z + 1)
        self.below = (dp, self.me, self.z - 1)
        self.has_above = self.z < nz - 1
        self.has_below = self.z > 0

    def barrier(self):
        semaphore = pltpu.get_barrier_semaphore()

        def signal(device):
            pl.semaphore_signal(semaphore, inc=1, device_id=device, device_id_type=MESH)

        for device in (self.core, self.next_x, self.next_y):
            signal(device)
        if self.nz > 1:
            pl.when(self.has_above)(lambda: signal(self.above))
            pl.when(self.has_below)(lambda: signal(self.below))
        more = (self.nz > 1) * (self.has_above.astype(jnp.int32) + self.has_below.astype(jnp.int32))
        pl.semaphore_wait(semaphore, 3 + more)


def remote(source, target, sent, arrived, device):
    return pltpu.make_async_remote_copy(
        src_ref=source,
        dst_ref=target,
        send_sem=sent,
        recv_sem=arrived,
        device_id=device,
        device_id_type=MESH,
    )


def comm_params(number, limit=60):
    return pltpu.CompilerParams(
        vmem_limit_bytes=limit * 1024 * 1024, collective_id=number, has_side_effects=True
    )


HBM = pl.BlockSpec(memory_space=pl.ANY)


def gather_kernel(
    nz,
    w_ref,
    x_ref,
    cot_ref,
    ck_ref,
    cv_ref,
    out_ref,
    xs_ref,
    cots_ref,
    near_ref,
    wbuf,
    xbuf,
    cbuf,
    local,
    csent,
    carrived,
    sent_z,
    sent_xy,
    sent_diag,
    wsent,
    arrived_z,
    arrived_xy,
    arrived_diag,
    warrived,
):
    at = Place(nz)
    me, x, y, z = at.me, at.x, at.y, at.z
    tokens = xs_ref.shape[1]
    keys = ck_ref.shape[1]
    rows = w_ref.shape[0]
    part = rows // 2
    pending = []

    def go(copy, when=None):
        if when is None:
            copy.start()
            pending.append((None, copy))
        else:
            pl.when(when)(copy.start)
            pending.append((when, copy))

    own = out_ref.at[y, x, z, me]
    near_span = [near_ref.at[me, pl.ds(0, keys)], near_ref.at[me, pl.ds(keys, keys)]]
    keep = [
        (w_ref, wbuf, own),
        (x_ref.at[me], xbuf.at[0], xs_ref.at[me]),
        (cot_ref.at[me], xbuf.at[1], cots_ref.at[me]),
        (ck_ref.at[me], cbuf.at[0], near_span[0]),
        (cv_ref.at[me], cbuf.at[1], near_span[1]),
    ]
    loads = [pltpu.make_async_copy(a, b, local.at[i]) for i, (a, b, _) in enumerate(keep)]
    stores = [pltpu.make_async_copy(b, c, local.at[5 + i]) for i, (_, b, c) in enumerate(keep)]
    for copy in loads:
        copy.start()
    at.barrier()
    exchange = [
        remote(x_ref.at[1 - me], xs_ref.at[me], csent.at[0], carrived.at[0], at.core),
        remote(ck_ref.at[1 - me], near_ref.at[me, pl.ds(0, keys)], csent.at[1], carrived.at[1], at.core),
        remote(cv_ref.at[1 - me], near_ref.at[me, pl.ds(keys, keys)], csent.at[2], carrived.at[2], at.core),
        remote(cot_ref.at[1 - me], cots_ref.at[me], csent.at[3], carrived.at[3], at.core),
    ]

    def block(yy, xx, zz, half=None):
        ref = out_ref.at[yy, xx, zz, me]
        return ref if half is None else ref.at[pl.ds(half * part, part)]

    def core(ref, kind, zz, when=None):
        go(remote(ref, ref, wsent.at[kind, zz], warrived.at[kind, zz], at.core), when)

    def along_z(ref, zz, up, when):
        to = at.above if up else at.below
        go(remote(ref, ref, sent_z.at[int(up), zz], arrived_z.at[zz], to), when)

    def across(ref, zz, when=None):
        go(remote(ref, ref, sent_xy.at[0, zz], arrived_xy.at[0, zz], at.next_x), when)
        go(remote(ref, ref, sent_xy.at[1, zz], arrived_xy.at[1, zz], at.next_y), when)
        core(ref, 0, zz, when)

    loads[0].wait()
    stores[0].start()
    stores[0].wait()
    along_z(own, z, True, at.has_above)
    along_z(own, z, False, at.has_below)
    across(own, z)
    for copy in exchange:
        go(copy)
    for load, store in zip(loads[1:], stores[1:]):
        load.wait()
        store.start()

    def arrive_across(zz, when=None):
        def body():
            ref = block(y, 1 - x, zz)
            remote(ref, ref, sent_xy.at[0, zz], arrived_xy.at[0, zz], at.next_x).wait_recv()
            ref = block(1 - y, x, zz)
            remote(ref, ref, sent_xy.at[1, zz], arrived_xy.at[1, zz], at.next_y).wait_recv()

        body() if when is None else pl.when(when)(body)
        ref = block(y, 1 - x, zz, 0)
        go(remote(ref, ref, sent_diag.at[0, zz], arrived_diag.at[0, zz], at.next_y), when)
        ref = block(1 - y, x, zz, 1)
        go(remote(ref, ref, sent_diag.at[1, zz], arrived_diag.at[1, zz], at.next_x), when)
        core(block(y, 1 - x, zz), 1, zz, when)
        core(block(1 - y, x, zz), 2, zz, when)

    for step in range(1, nz):
        for up in (True, False):
            zz = z - step if up else z + step
            valid = zz >= 0 if up else zz < nz
            zc = jnp.clip(zz, 0, nz - 1)
            ref = block(y, x, zc)

            def wait(ref=ref, zc=zc, up=up):
                to = at.below if up else at.above
                remote(ref, ref, sent_z.at[int(up), zc], arrived_z.at[zc], to).wait_recv()

            pl.when(valid)(wait)
            along_z(ref, zc, up, valid & (at.has_above if up else at.has_below))
            across(ref, zc, valid)
        if step == 1:
            arrive_across(z)
        else:
            arrive_across(jnp.clip(z - step + 1, 0, nz - 1), z - step + 1 >= 0)
            arrive_across(jnp.clip(z + step - 1, 0, nz - 1), z + step - 1 < nz)
    if nz == 1:
        arrive_across(z)
    else:
        arrive_across(jnp.clip(z - nz + 1, 0, nz - 1), z - nz + 1 >= 0)
        arrive_across(jnp.clip(z + nz - 1, 0, nz - 1), z + nz - 1 < nz)
    for zz in range(nz):
        for half in range(2):
            ref = block(1 - y, 1 - x, zz, half)
            back = at.next_y if half == 0 else at.next_x
            remote(ref, ref, sent_diag.at[half, zz], arrived_diag.at[half, zz], back).wait_recv()
            core(ref, 3 + half, zz)
    for copy in stores[1:]:
        copy.wait()
    for copy in exchange:
        copy.wait_recv()
    for zz in range(nz):
        for kind, ref in enumerate(
            (
                out_ref.at[y, x, zz, 1 - me],
                out_ref.at[y, 1 - x, zz, 1 - me],
                out_ref.at[1 - y, x, zz, 1 - me],
                out_ref.at[1 - y, 1 - x, zz, 1 - me, pl.ds(0, part)],
                out_ref.at[1 - y, 1 - x, zz, 1 - me, pl.ds(part, part)],
            )
        ):
            remote(ref, ref, wsent.at[kind, zz], warrived.at[kind, zz], at.core).wait_recv()
    for when, copy in pending:
        copy.wait_send() if when is None else pl.when(when)(copy.wait_send)


def gather(w, x, cot, cache_keys, cache_values, nz):
    dma = pltpu.SemaphoreType.DMA
    _, tokens, half = x.shape
    keys = cache_keys.shape[1]
    full = jax.ShapeDtypeStruct((2, tokens, half), BF)
    return pl.pallas_call(
        functools.partial(gather_kernel, nz),
        in_specs=[HBM] * 5,
        out_specs=[HBM] * 4,
        out_shape=[
            jax.ShapeDtypeStruct((2, 2, nz, 2) + w.shape, BF),
            full,
            full,
            jax.ShapeDtypeStruct((2, 2 * keys, half), BF),
        ],
        scratch_shapes=[
            pltpu.VMEM(w.shape, BF),
            pltpu.VMEM(x.shape, BF),
            pltpu.VMEM((2, keys, half), BF),
            dma((10,)),
            dma((4,)),
            dma((4,)),
            dma((2, nz)),
            dma((2, nz)),
            dma((2, nz)),
            dma((5, nz)),
            dma((nz,)),
            dma((2, nz)),
            dma((2, nz)),
            dma((5, nz)),
        ],
        compiler_params=comm_params(0),
        name="gather",
    )(w, x, cot, cache_keys, cache_values)


class Sums:
    BUFFERS = 12

    @staticmethod
    def scratch(parts, rows, tiles, nz):
        dma = pltpu.SemaphoreType.DMA
        slab, block = rows // 4, rows // 4 // nz
        hops = max(nz - 1, 1)
        return [
            pltpu.VMEM((2, parts, rows, LANES), BF),
            pltpu.VMEM((2, parts, rows, LANES), BF),
            pltpu.VMEM((tiles, parts, rows, LANES), BF),
            pltpu.VMEM((tiles, 2, parts, slab // 2, LANES), BF),
            pltpu.VMEM((tiles, 2, parts, slab, LANES), BF),
            pltpu.VMEM((tiles, 2, hops, parts, block, LANES), BF),
            dma((tiles,)),
            dma((tiles,)),
            dma((tiles, 4)),
            dma((tiles, 4)),
            dma((tiles, 2, hops)),
            dma((tiles, 2, hops)),
        ]

    def __init__(self, at, refs):
        (
            self.mine,
            self.other,
            self.total,
            self.diag,
            self.side,
            self.hop,
            self.core_sent,
            self.core_arrived,
            self.sent,
            self.arrived,
            self.hop_sent,
            self.hop_arrived,
        ) = refs
        self.at = at
        self.tiles, _, self.rows, _ = self.total.shape
        self.slab = self.rows // 4
        self.block = self.slab // at.nz
        self.last = at.nz + 2

    def span(self, y, x, first=0, size=None):
        start = pl.multiple_of((y * 2 + x) * self.slab + first, self.block)
        return pl.ds(start, self.slab if size is None else size)

    def core_copy(self, j):
        return remote(
            self.other.at[j % 2],
            self.total.at[j],
            self.core_sent.at[j],
            self.core_arrived.at[j],
            self.at.core,
        )

    def diag_copies(self, j):
        at, part = self.at, self.slab // 2
        y, x = 1 - at.y, 1 - at.x
        return [
            remote(
                self.total.at[j, :, self.span(y, x, i * part, part)],
                self.diag.at[j, i],
                self.sent.at[j, i],
                self.arrived.at[j, i],
                device,
            )
            for i, device in enumerate((at.next_x, at.next_y))
        ]

    def side_copies(self, j):
        at = self.at
        return [
            remote(
                self.total.at[j, :, span],
                self.side.at[j, i],
                self.sent.at[j, 2 + i],
                self.arrived.at[j, 2 + i],
                device,
            )
            for i, (span, device) in enumerate(
                ((self.span(at.y, 1 - at.x), at.next_x), (self.span(1 - at.y, at.x), at.next_y))
            )
        ]

    def hop_copy(self, j, t, up):
        at = self.at
        place = at.z + (at.nz - t) if up else at.z - (at.nz - t)
        place = jnp.clip(place, 0, at.nz - 1)
        return remote(
            self.total.at[j, :, self.span(at.y, at.x, place * self.block, self.block)],
            self.hop.at[j, int(up), t - 1],
            self.hop_sent.at[j, int(up), t - 1],
            self.hop_arrived.at[j, int(up), t - 1],
            at.above if up else at.below,
        )

    def sends(self, t, up):
        at = self.at
        return at.has_above & (at.z < t) if up else at.has_below & (at.nz - 1 - at.z < t)

    def receives(self, t, up):
        at = self.at
        return at.has_below & (at.z <= t) if up else at.has_above & (at.nz - 1 - at.z <= t)

    def add(self, j, span, value):
        self.total[j, :, span, :] = (
            self.total[j, :, span, :].astype(F32) + value.astype(F32)
        ).astype(BF)

    def start(self, j):
        self.core_copy(j).start()

    def after_core(self, j):
        self.core_copy(j).wait()

        def body(rows):
            self.add(j, rows, self.mine[j % 2, :, rows, :])

        chunks(self.rows, body)
        for copy in self.diag_copies(j):
            copy.start()

    def after_diag(self, j):
        at, part = self.at, self.slab // 2
        for copy in self.diag_copies(j):
            copy.wait()
        self.add(j, self.span(1 - at.y, at.x, 0, part), self.diag[j, 0])
        self.add(j, self.span(at.y, 1 - at.x, part, part), self.diag[j, 1])
        for copy in self.side_copies(j):
            copy.start()

    def after_side(self, j):
        at = self.at
        for copy in self.side_copies(j):
            copy.wait()
        span = self.span(at.y, at.x)
        self.total[j, :, span, :] = (
            self.total[j, :, span, :].astype(F32)
            + self.side[j, 0].astype(F32)
            + self.side[j, 1].astype(F32)
        ).astype(BF)
        self.hop_start(j, 1)

    def hop_start(self, j, t):
        if t < self.at.nz:
            for up in (True, False):
                pl.when(self.sends(t, up))(self.hop_copy(j, t, up).start)

    def after_hop(self, j, t):
        at = self.at
        for up in (True, False):
            pl.when(self.sends(t, up))(self.hop_copy(j, t, up).wait_send)

            @pl.when(self.receives(t, up))
            def _(up=up):
                self.hop_copy(j, t, up).wait_recv()
                if t < at.nz - 1:
                    place = at.z - 1 + (at.nz - t) if up else at.z + 1 - (at.nz - t)
                    place = jnp.clip(place, 0, at.nz - 1)
                    span = self.span(at.y, at.x, place * self.block, self.block)
                    self.add(j, span, self.hop[j, int(up), t - 1])

        self.hop_start(j, t + 1)

    def result(self, j):
        at = self.at
        value = self.total[j, :, self.span(at.y, at.x, at.z * self.block, self.block), :].astype(F32)
        if at.nz > 1:
            for up, there in ((True, at.has_below), (False, at.has_above)):
                got = self.hop[j, int(up), at.nz - 2].astype(F32)
                value = value + jnp.where(there, got, 0.0)
        return value

    def advance(self, step, store):
        def on(behind, body):
            j = step - behind
            pl.when((j >= 0) & (j < self.tiles))(lambda: body(jnp.clip(j, 0, self.tiles - 1)))

        for t in range(self.at.nz - 1, 0, -1):
            on(3 + t, functools.partial(self.after_hop, t=t))
        on(self.last, lambda j: store(self.result(j)))
        on(3, self.after_side)
        on(2, self.after_diag)

    def meet(self, step):
        j = step - 1
        pl.when((j >= 0) & (j < self.tiles))(lambda: self.after_core(jnp.clip(j, 0, self.tiles - 1)))


class Unsummed:
    class Tile:
        def __init__(self, ref):
            self.ref = ref

        def __setitem__(self, index, value):
            self.ref[index[1:]] = value

    def __init__(self, mine, other):
        self.mine, self.other = Unsummed.Tile(mine), Unsummed.Tile(other)

    def start(self, j):
        pass

    def advance(self, step, store):
        pass

    def meet(self, step):
        pass


def features(ref, rows):
    return jnp.concatenate([ref[0, rows, :], ref[1, rows, :]], axis=1)


def pair(ref, model):
    return jnp.concatenate(
        [ref[:, 0].reshape(model, LANES), ref[:, 1].reshape(model, LANES)], axis=1
    )


def normal_of(x):
    inverse = lax.rsqrt(jnp.mean(x * x, axis=1, keepdims=True) + EPSILON)
    return x * inverse, inverse


def norm_back(normal, inverse, gain, grad):
    scaled = grad * gain
    return inverse * (scaled - normal * jnp.mean(scaled * normal, axis=1, keepdims=True))


def qkv_kernel(x_ref, gain_ref, w_ref, cos_ref, sin_ref, out_ref, n1_ref):
    part = pl.program_id(0)
    tokens, model = n1_ref.shape

    @pl.when((part == 0) & (pl.program_id(1) == 0))
    def _():
        def norm(rows):
            normal, _ = normal_of(features(x_ref, rows).astype(F32))
            n1_ref[rows, :] = (normal * gain_ref[...]).astype(BF)

        chunks(tokens, norm)

    def project(rows):
        y = nn(n1_ref[rows, :], w_ref[...].reshape(model, -1))
        cosine, sine = cos_ref[rows, :], sin_ref[rows, :]
        for h in range(y.shape[1] // HEAD_DIM):
            lanes = slice(h * HEAD_DIM, (h + 1) * HEAD_DIM)
            u = y[:, lanes]
            turned = u * cosine + pltpu.roll(u, HEAD_DIM // 2, 1) * sine
            out_ref[rows, lanes] = jnp.where(part < 2, turned, u).astype(BF)

    chunks(tokens, project)


def project_qkv(x, gain, gathered, cosine, sine):
    halves, tokens, half = x.shape
    groups, _, rows, _ = gathered.shape
    return pl.pallas_call(
        qkv_kernel,
        grid=(3, halves),
        in_specs=[
            whole(x.shape),
            whole(gain.shape),
            pl.BlockSpec((groups, None, rows, half), lambda m, h: (0, h, 0, m)),
            whole(cosine.shape),
            whole(sine.shape),
        ],
        out_specs=pl.BlockSpec((None, None, tokens, half), lambda m, h: (m, h, 0, 0)),
        out_shape=jax.ShapeDtypeStruct((3, halves, tokens, half), BF),
        scratch_shapes=[pltpu.VMEM((tokens, halves * half), BF)],
        compiler_params=params(),
        name="project_qkv",
    )(x, gain, gathered, cosine, sine)


def fill_memory(idx_ref, near_ref, far_ref, offset, mem_ref):
    for b in range(QBLKS):
        for j in range(OWN_K + PART_K):
            ref, at = (near_ref, b * OWN_K + j) if j < OWN_K else (far_ref, QBLKS * OWN_K + b * PART_K + j - OWN_K)
            start = pl.multiple_of(idx_ref[at] * MEM_BLK, MEM_BLK) + offset
            mem_ref[b, j * MEM_BLK : (j + 1) * MEM_BLK, :] = ref[pl.ds(start, MEM_BLK), :]


def masked(scores, start, first):
    keys, queries = scores.shape
    at = first + lax.broadcasted_iota(jnp.int32, (1, queries), 1)
    limit = jnp.where((at >= start) & (at < start + PIC), start + PIC - 1, at)
    key = lax.broadcasted_iota(jnp.int32, (keys, queries), 0)
    return jnp.where(key <= limit, scores, NEG)


def attend_kernel(
    idx_ref, q_ref, k_ref, v_ref, near_ref, far_ref, out_ref, lse_ref, kmem_ref, vmem_ref
):
    keys = near_ref.shape[0] // 2
    fill_memory(idx_ref, near_ref, far_ref, 0, kmem_ref)
    fill_memory(idx_ref, near_ref, far_ref, keys, vmem_ref)
    scale = LOG2E / math.sqrt(HEAD_DIM)
    base = QBLKS * (OWN_K + PART_K)
    for b in range(QBLKS):
        start = idx_ref[base + b] - b * QROWS

        def body(i, carry, b=b, start=start):
            first = pl.multiple_of(i * CHUNK, CHUNK)
            rows = pl.ds(pl.multiple_of(b * QROWS + first, CHUNK), CHUNK)
            q = q_ref[rows, :]
            parts = []
            for n in range(b + 1):
                span = slice(n * QROWS, (n + 1) * QROWS)
                s = nt(k_ref[span, :], q)
                parts.append((masked(s, start, first) if n == b else s, v_ref[span, :]))
            parts.append((nt(kmem_ref[b], q), vmem_ref[b]))
            top = functools.reduce(
                jnp.maximum, [jnp.max(s, axis=0, keepdims=True) for s, _ in parts]
            )
            shift = top * scale
            total = jnp.zeros_like(top)
            acc = jnp.zeros((HEAD_DIM, CHUNK), F32)
            for s, v in parts:
                e = jnp.exp2(s * scale - shift)
                total = total + jnp.sum(e, axis=0, keepdims=True)
                acc = acc + tn(v, e.astype(BF))
            out_ref[rows, :] = jnp.transpose(acc / total).astype(BF)
            lse_ref[:, rows] = shift + jnp.log2(total)
            return carry

        lax.fori_loop(0, QROWS // CHUNK, body, 0)


def attend(idx, qkv, near, far):
    _, halves, tokens, half = qkv.shape
    here = half // HEAD_DIM
    cached = near.shape[1]
    memory = (OWN_K + PART_K) * MEM_BLK
    column = lambda m: pl.BlockSpec(
        (None, None, tokens, HEAD_DIM), lambda h, idx: (m, h // here, 0, h % here)
    )
    cache = pl.BlockSpec((None, cached, HEAD_DIM), lambda h, idx: (h // here, 0, h % here))
    chosen = pl.BlockSpec((None, QBLKS, memory, HEAD_DIM), lambda h, idx: (h // here, 0, 0, h % here))
    chosen_shape = jax.ShapeDtypeStruct((halves, QBLKS, memory, half), BF)
    return pl.pallas_call(
        attend_kernel,
        grid_spec=pltpu.PrefetchScalarGridSpec(
            num_scalar_prefetch=1,
            grid=(halves * here,),
            in_specs=[column(0), column(1), column(2), cache, cache],
            out_specs=[
                pl.BlockSpec((None, tokens, HEAD_DIM), lambda h, idx: (h // here, 0, h % here)),
                pl.BlockSpec((None, None, 1, tokens), lambda h, idx: (h // here, h % here, 0, 0)),
                chosen,
                chosen,
            ],
        ),
        out_shape=[
            jax.ShapeDtypeStruct((halves, tokens, half), BF),
            jax.ShapeDtypeStruct((halves, here, 1, tokens), F32),
            chosen_shape,
            chosen_shape,
        ],
        compiler_params=params(),
        name="attend",
    )(idx, qkv, qkv, qkv, near, far)


def split_store(me, value, mine_ref, other_ref, index):
    low, high = value[:, :LANES], value[:, LANES:]
    mine_ref[index] = jnp.where(me == 0, low, high)
    other_ref[index] = jnp.where(me == 0, high, low)


def send_halves(at, buffer, out_ref, local, sent, arrived):
    tokens = buffer.shape[1]
    rows = pl.ds(pl.multiple_of(at.me * tokens, tokens), tokens)
    return (
        pltpu.make_async_copy(buffer.at[at.me], out_ref.at[rows], local),
        remote(buffer.at[1 - at.me], out_ref.at[rows], sent, arrived, at.core),
    )


def feed_kernel(
    nz,
    steps,
    x_ref,
    att_ref,
    cot_ref,
    gain_ref,
    wo_ref,
    wg_ref,
    wu_ref,
    wd_ref,
    ghid_ref,
    gn2_ref,
    *refs,
):
    if nz:
        out_ref, grad_ref, *refs = refs
    else:
        result_ref, mine_ref, other_ref, *refs = refs
    hid_ref, n2_ref, n2t_ref, cott_ref, acc_ref, dn_ref, a_ref, dg_ref, du_ref, *refs = refs
    tokens, model = hid_ref.shape
    half = model // 2
    step = pl.program_id(0)
    me = lax.axis_index("row")
    copies = []
    if nz:
        at = Place(nz)
        result_ref, local, sent, arrived, *refs = refs
        sums = Sums(at, refs)
        copies = send_halves(at, result_ref, out_ref, local.at[0], sent.at[0], arrived.at[0])
    else:
        sums = Unsummed(mine_ref, other_ref)

    def wo_half(h):
        return wo_ref[:, h].reshape(model, half)

    @pl.when(step == 0)
    def _():
        if nz:
            at.barrier()

        def start(rows):
            hidden = features(x_ref, rows).astype(F32)
            for h in range(2):
                hidden = hidden + nt(att_ref[h, rows, :], wo_half(h))
            hid_ref[rows, :] = hidden
            normal, _ = normal_of(hidden)
            n2_ref[rows, :] = (normal * gain_ref[...]).astype(BF)
            n2t_ref[:, rows] = jnp.transpose(n2_ref[rows, :])
            cott_ref[:, rows] = jnp.transpose(features(cot_ref, rows))
            acc_ref[rows, :] = jnp.zeros((CHUNK, model), F32)
            dn_ref[rows, :] = jnp.zeros((CHUNK, model), F32)

        chunks(tokens, start)

    def store(value):
        grad_ref[...] = value

    sums.advance(step, store)

    def forward_back(rows):
        n2 = n2_ref[rows, :]
        gating = nn(n2, pair(wg_ref, model))
        upward = nn(n2, pair(wu_ref, model))
        gactive = nn(features(cot_ref, rows), pair(wd_ref, model))
        sigmoid = 1.0 / (1.0 + jnp.exp(-gating))
        silu = gating * sigmoid
        a_ref[rows, :] = (silu * upward).astype(BF)
        dg_ref[rows, :] = (gactive * upward * (sigmoid + silu * (1.0 - sigmoid))).astype(BF)
        du_ref[rows, :] = (gactive * silu).astype(BF)
        acc_ref[rows, :] += nt(a_ref[rows, :], pair(wd_ref, model))
        dn_ref[rows, :] += nt(dg_ref[rows, :], pair(wg_ref, model)) + nt(
            du_ref[rows, :], pair(wu_ref, model)
        )

    @pl.when(step < steps)
    def _():
        chunks(tokens, forward_back)

    sums.meet(step)

    @pl.when(step < steps)
    def _():
        slot = step % 2

        def weights(rows):
            n2t = n2t_ref[rows, :]
            for p, value in enumerate(
                (nn(n2t, dg_ref[...]), nn(n2t, du_ref[...]), nn(cott_ref[rows, :], a_ref[...]))
            ):
                split_store(me, value.astype(BF), sums.mine, sums.other, (slot, p, rows))

        chunks(model, weights)
        sums.start(step)

    @pl.when(step == (steps if nz else steps - 1))
    def _():
        gn2_ref[...] = jnp.zeros_like(gn2_ref)

        def finish(rows):
            hidden = hid_ref[rows, :]
            result = (hidden + acc_ref[rows, :]).astype(BF)
            result_ref[0, rows, :] = result[:, :half]
            result_ref[1, rows, :] = result[:, half:]
            normal, inverse = normal_of(hidden)
            dn = dn_ref[rows, :]
            gn2_ref[...] += jnp.sum(dn * normal, axis=0, keepdims=True)
            ghid_ref[rows, :] = features(cot_ref, rows).astype(F32) + norm_back(
                normal, inverse, gain_ref[...], dn
            )

        chunks(tokens, finish)
        for copy in copies:
            copy.start()

    if nz:

        @pl.when(step == pl.num_programs(0) - 1)
        def _():
            for copy in copies:
                copy.wait()


def feed(x, attended, cotangent, gain, gathered, o_at, g_at, u_at, d_at, units, nz):
    halves, tokens, half = x.shape
    model = halves * half
    groups, _, rows, _ = gathered.shape
    steps = units // LANES
    tile = lambda at: pl.BlockSpec(
        (groups, halves, rows, LANES),
        lambda j: (0, 0, 0, at // LANES + jnp.minimum(j, steps - 1)),
    )
    big = lambda dtype: pltpu.VMEM((tokens, model), dtype)
    small = pltpu.VMEM((tokens, 2 * LANES), BF)
    last = nz + 2 if nz else 0
    dma = pltpu.SemaphoreType.DMA((1,))
    if nz:
        out_specs = [
            HBM,
            pl.BlockSpec((3, rows, LANES), lambda j: (0, 0, jnp.clip(j - last, 0, steps - 1))),
        ]
        out_shape = [
            jax.ShapeDtypeStruct((halves * tokens, half), BF),
            jax.ShapeDtypeStruct((3, rows, units), F32),
        ]
        more = [pltpu.VMEM(x.shape, BF), dma, dma, dma] + Sums.scratch(3, model, steps, nz)
    else:
        grads = pl.BlockSpec((3, model, LANES), lambda j: (0, 0, j))
        out_specs = [once(x.shape), grads, grads]
        grads = jax.ShapeDtypeStruct((3, model, units), BF)
        out_shape = [jax.ShapeDtypeStruct(x.shape, BF), grads, grads]
        more = []
    return pl.pallas_call(
        functools.partial(feed_kernel, nz, steps),
        grid=(steps + last,),
        in_specs=[
            once(x.shape),
            once(x.shape),
            once(x.shape),
            once(gain.shape),
            pl.BlockSpec(
                (groups, halves, rows, half),
                lambda j: (0, 0, 0, o_at // half),
                pipeline_mode=pl.Buffered(1),
            ),
            tile(g_at),
            tile(u_at),
            tile(d_at),
        ],
        out_specs=[once((tokens, model)), once(gain.shape)] + out_specs,
        out_shape=[
            jax.ShapeDtypeStruct((tokens, model), F32),
            jax.ShapeDtypeStruct(gain.shape, F32),
        ]
        + out_shape,
        scratch_shapes=[big(F32), big(BF), big(BF), big(BF), big(F32), big(F32), small, small, small]
        + more,
        compiler_params=comm_params(1) if nz else params(),
        name="feed",
    )(x, attended, cotangent, gain, gathered, gathered, gathered, gathered)


def back_kernel(
    nz,
    steps,
    starts_ref,
    qkv_ref,
    kmem_ref,
    vmem_ref,
    att_ref,
    lse_ref,
    wo_ref,
    wq_ref,
    wk_ref,
    wv_ref,
    x_ref,
    gain_ref,
    ghid_ref,
    gn2_ref,
    cos_ref,
    sin_ref,
    *refs,
):
    if nz:
        out_ref, grad_ref, norms_ref, *refs = refs
    else:
        result_ref, mine_ref, other_ref, gn1_ref, *refs = refs
    gmix_ref, gmixt_ref, n1t_ref, dn_ref, gatt_ref, g_ref, dk_ref, dv_ref, *refs = refs
    tokens, model = ghid_ref.shape
    half = model // 2
    step = pl.program_id(0)
    me = lax.axis_index("row")
    copies = []
    if nz:
        at = Place(nz)
        result_ref, local, sent, arrived, *refs = refs
        sums = Sums(at, refs[: Sums.BUFFERS])
        norm_sums = Sums(at, refs[Sums.BUFFERS :])
        copies = send_halves(at, result_ref, out_ref, local.at[0], sent.at[0], arrived.at[0])
    else:
        sums = Unsummed(mine_ref, other_ref)
    scale = LOG2E / math.sqrt(HEAD_DIM)
    plain = 1.0 / math.sqrt(HEAD_DIM)

    @pl.when(step == 0)
    def _():
        if nz:
            at.barrier()

        def start(rows):
            normal, _ = normal_of(features(x_ref, rows).astype(F32))
            n1t_ref[:, rows] = jnp.transpose((normal * gain_ref[...]).astype(BF))
            gmix_ref[rows, :] = ghid_ref[rows, :].astype(BF)
            gmixt_ref[:, rows] = jnp.transpose(gmix_ref[rows, :])
            dn_ref[rows, :] = jnp.zeros((CHUNK, model), F32)

        chunks(tokens, start)

    def store(value):
        grad_ref[...] = value

    sums.advance(step, store)

    def unturn(g, rows):
        return g * cos_ref[rows, :] - pltpu.roll(g, HEAD_DIM // 2, 1) * sin_ref[rows, :]

    def one_head(hh, carry):
        dk_ref[...] = jnp.zeros_like(dk_ref)
        dv_ref[...] = jnp.zeros_like(dv_ref)
        for b in range(QBLKS):
            start = starts_ref[b] - b * QROWS

            def body(i, carry, b=b, start=start):
                first = pl.multiple_of(i * CHUNK, CHUNK)
                rows = pl.ds(pl.multiple_of(b * QROWS + first, CHUNK), CHUNK)
                q = qkv_ref[0, hh, rows, :]
                do = gatt_ref[hh, rows, :]
                lse = lse_ref[hh, 0, :, rows]
                dots = jnp.transpose(do.astype(F32) * att_ref[hh, rows, :].astype(F32))
                dot = jnp.sum(dots, axis=0, keepdims=True)
                dq = jnp.zeros((HEAD_DIM, CHUNK), F32)
                for n in range(b + 2):
                    span = slice(n * QROWS, (n + 1) * QROWS)
                    if n <= b:
                        k, v = qkv_ref[1, hh, span, :], qkv_ref[2, hh, span, :]
                    else:
                        k, v = kmem_ref[hh, b], vmem_ref[hh, b]
                    s = nt(k, q)
                    if n == b:
                        s = masked(s, start, first)
                    share = jnp.exp2(s * scale - lse)
                    ds = (share * (nt(v, do) - dot)).astype(BF)
                    if n <= b:
                        dv_ref[span, :] += nn(share.astype(BF), do)
                        dk_ref[span, :] += nn(ds, q)
                    dq = dq + tn(k, ds)
                g_ref[0, hh, rows, :] = unturn(jnp.transpose(dq) * plain, rows).astype(BF)
                return carry

            lax.fori_loop(0, QROWS // CHUNK, body, 0)

        def finish(rows):
            g_ref[1, hh, rows, :] = unturn(dk_ref[rows, :] * plain, rows).astype(BF)
            g_ref[2, hh, rows, :] = dv_ref[rows, :].astype(BF)

        chunks(tokens, finish)
        return carry

    @pl.when(step < steps)
    def _():
        def grad_attended(rows):
            value = nn(gmix_ref[rows, :], pair(wo_ref, model)).astype(BF)
            gatt_ref[0, rows, :] = value[:, :LANES]
            gatt_ref[1, rows, :] = value[:, LANES:]

        chunks(tokens, grad_attended)
        lax.fori_loop(0, 2, one_head, 0)

    sums.meet(step)

    @pl.when(step < steps)
    def _():
        slot = step % 2

        def weights(rows):
            n1t = n1t_ref[rows, :]
            for p in range(3):
                value = nn(n1t, jnp.concatenate([g_ref[p, 0], g_ref[p, 1]], axis=1))
                split_store(me, value.astype(BF), sums.mine, sums.other, (slot, p, rows))
            value = nn(gmixt_ref[rows, :], jnp.concatenate([att_ref[0], att_ref[1]], axis=1))
            split_store(me, value.astype(BF), sums.mine, sums.other, (slot, 3, rows))

        chunks(model, weights)
        sums.start(step)

        def inward(rows):
            total = dn_ref[rows, :]
            for p, ref in enumerate((wq_ref, wk_ref, wv_ref)):
                g = jnp.concatenate([g_ref[p, 0, rows, :], g_ref[p, 1, rows, :]], axis=1)
                total = total + nt(g, pair(ref, model))
            dn_ref[rows, :] = total

        chunks(tokens, inward)

    @pl.when(step == (steps if nz else steps - 1))
    def _():
        def finish(rows, carry):
            normal, inverse = normal_of(features(x_ref, rows).astype(F32))
            dn = dn_ref[rows, :]
            value = (ghid_ref[rows, :] + norm_back(normal, inverse, gain_ref[...], dn)).astype(BF)
            result_ref[0, rows, :] = value[:, :half]
            result_ref[1, rows, :] = value[:, half:]
            return carry + jnp.sum(dn * normal, axis=0, keepdims=True)

        gn1 = lax.fori_loop(
            0,
            tokens // CHUNK,
            lambda i, c: finish(pl.ds(pl.multiple_of(i * CHUNK, CHUNK), CHUNK), c),
            jnp.zeros((1, model), F32),
        )
        for copy in copies:
            copy.start()
        if not nz:
            gn1_ref[...] = gn1
            return
        row = lax.broadcasted_iota(jnp.int32, (LANES, model), 0)
        both = jnp.where(row == 0, gn1, jnp.where(row == 1, gn2_ref[...], 0.0))
        column = jnp.transpose(both).astype(BF)
        norm_sums.mine[0, 0] = column
        norm_sums.other[0, 0] = column
        norm_sums.start(0)

    if nz:

        def store_norms(value):
            norms_ref[...] = value[0]

        norm_sums.advance(step - steps, store_norms)
        norm_sums.meet(step - steps)

        @pl.when(step == pl.num_programs(0) - 1)
        def _():
            for copy in copies:
                copy.wait()


def back(starts, qkv, kmem, vmem, attended, lse, first, second, o_at, x, gain, ghid, gn2, cosine, sine, nz):
    halves, tokens, half = x.shape
    model = halves * half
    groups, _, rows, _ = first.shape
    steps = half // HEAD_DIM
    memory = kmem.shape[2]
    now = lambda j: jnp.minimum(j, steps - 1)
    tile = lambda at: pl.BlockSpec(
        (groups, halves, rows, LANES), lambda j: (0, 0, 0, at // LANES + now(j))
    )
    chosen = pl.BlockSpec((halves, QBLKS, memory, HEAD_DIM), lambda j: (0, 0, 0, now(j)))
    big = lambda dtype: pltpu.VMEM((tokens, model), dtype)
    last = nz + 2 if nz else 0
    dma = pltpu.SemaphoreType.DMA((1,))
    if nz:
        out_specs = [
            HBM,
            pl.BlockSpec((4, rows, LANES), lambda j: (0, 0, jnp.clip(j - last, 0, steps - 1))),
            once((rows, LANES)),
        ]
        out_shape = [
            jax.ShapeDtypeStruct((halves * tokens, half), BF),
            jax.ShapeDtypeStruct((4, rows, half), F32),
            jax.ShapeDtypeStruct((rows, LANES), F32),
        ]
        more = (
            [pltpu.VMEM(x.shape, BF), dma, dma, dma]
            + Sums.scratch(4, model, steps, nz)
            + Sums.scratch(1, model, 1, nz)
        )
    else:
        grads = pl.BlockSpec((4, model, LANES), lambda j: (0, 0, j))
        out_specs = [once(x.shape), grads, grads, once(gain.shape)]
        grads = jax.ShapeDtypeStruct((4, model, half), BF)
        out_shape = [jax.ShapeDtypeStruct(x.shape, BF), grads, grads]
        out_shape.append(jax.ShapeDtypeStruct(gain.shape, F32))
        more = []
    return pl.pallas_call(
        functools.partial(back_kernel, nz, steps),
        grid=(steps + last + (1 if nz else 0),),
        in_specs=[
            pl.BlockSpec(memory_space=pltpu.SMEM),
            pl.BlockSpec((3, halves, tokens, HEAD_DIM), lambda j: (0, 0, 0, now(j))),
            chosen,
            chosen,
            pl.BlockSpec((halves, tokens, HEAD_DIM), lambda j: (0, 0, now(j))),
            pl.BlockSpec((halves, 1, 1, tokens), lambda j: (0, now(j), 0, 0)),
            tile(o_at),
            tile(0),
            tile(half),
            tile(2 * half),
            once(x.shape),
            once(gain.shape),
            once(ghid.shape),
            once(gain.shape),
            once(cosine.shape),
            once(sine.shape),
        ],
        out_specs=out_specs,
        out_shape=out_shape,
        scratch_shapes=[big(BF), big(BF), big(BF), big(F32)]
        + [
            pltpu.VMEM((halves, tokens, HEAD_DIM), BF),
            pltpu.VMEM((3, halves, tokens, HEAD_DIM), BF),
            pltpu.VMEM((tokens, HEAD_DIM), F32),
            pltpu.VMEM((tokens, HEAD_DIM), F32),
        ]
        + more,
        compiler_params=comm_params(2) if nz else params(),
        name="back",
    )(
        starts,
        qkv,
        kmem,
        vmem,
        attended,
        lse,
        second,
        first,
        first,
        first,
        x,
        gain,
        ghid,
        gn2,
        cosine,
        sine,
    )


def exchange(value, line):
    step = 1 if line == "x" else 2
    return lax.ppermute(value, "dp", [(d, d ^ step) for d in range(4)])


def partner_cache(near, source):
    along_x, along_y = exchange(near, "x"), exchange(near, "y")
    corner = jnp.stack([exchange(along_x[0], "y"), exchange(along_y[1], "x")])
    which = source ^ lax.axis_index("dp")
    return jnp.where(which == 1, along_x, jnp.where(which == 2, along_y, corner))


def swap(value):
    return lax.ppermute(value, "row", [(0, 1), (1, 0)])


def in_order(mine, got, me):
    return jnp.where(me == 0, jnp.stack([mine, got]), jnp.stack([got, mine]))


def own_sequence(value, me):
    take = lambda i: lax.dynamic_index_in_dim(value, i, 0, keepdims=False)
    return in_order(take(me), swap(take(1 - me)), me)


def own_features(value, me):
    return own_sequence(value, me).reshape(-1, value.shape[2])


def summed(mine, other):
    total = mine.astype(F32) + swap(other).astype(F32)
    return lax.psum_scatter(total, ("dp", "col"), scatter_dimension=1, tiled=True)


def on_device(
    inputs,
    w_query,
    w_key,
    w_value,
    w_out,
    w_gate,
    w_up,
    w_down,
    norm_one,
    norm_two,
    cache_keys,
    cache_values,
    own_index,
    partner_index,
    picture_start,
    partner_seq,
    cotangent,
):
    me = lax.axis_index("row")
    nz = lax.axis_size("col")
    chips = lax.axis_size("dp") * nz
    half = inputs.shape[1]
    model = 2 * half
    units = w_gate.shape[1]
    rows = w_query.shape[0]

    gains = jnp.pad(jnp.stack([norm_one, norm_two], axis=1), ((0, 0), (0, LANES - 2)))
    first = jnp.concatenate([w_query, w_key, w_value, gains], axis=1)
    second = jnp.concatenate([w_out.T, w_gate, w_up, w_down.T], axis=1)
    second = lax.all_gather(second, ("dp", "col", "row"), axis=0, tiled=True)
    second = second.reshape(chips, 2, rows, -1)
    tokens = inputs.reshape(SEQ_DEV, SEQ_LEN, half)
    upstream = cotangent.reshape(SEQ_DEV, SEQ_LEN, half)
    lines = lax.axis_size("dp") == 4
    if lines:
        first, x, cot, near = gather(first, tokens, upstream, cache_keys, cache_values, nz)
    else:
        first = lax.all_gather(first, ("dp", "col", "row"), axis=0, tiled=True)
        x, cot = own_sequence(tokens, me), own_sequence(upstream, me)
        near = own_sequence(jnp.concatenate([cache_keys, cache_values], axis=1), me)
    first = first.reshape(chips, 2, rows, -1)
    gains = first[:, 0, :, 3 * half : 3 * half + 2].reshape(model, 2).astype(F32)
    gain_one, gain_two = gains[:, 0].reshape(1, model), gains[:, 1].reshape(1, model)

    pick = lambda table: lax.dynamic_index_in_dim(table, me, 0, keepdims=False).reshape(-1)
    source = lax.dynamic_index_in_dim(partner_seq, me, 0, keepdims=False) // SEQ_DEV // nz
    starts = pick(picture_start)
    idx = jnp.concatenate([pick(own_index), pick(partner_index), starts])
    cosine, sine = rotary_tables()

    if lines:
        far = partner_cache(near, source)
    else:
        far = lax.dynamic_index_in_dim(lax.all_gather(near, "dp", axis=0), source, 0, keepdims=False)
    qkv = project_qkv(x, gain_one, first, cosine, sine)
    attended, lse, kmem, vmem = attend(idx, qkv, near, far)
    o_at, g_at = 0, half
    u_at, d_at = g_at + units, g_at + 2 * units
    hops = nz if lines else 0
    ghid, gn2, *fed = feed(
        x, attended, cot, gain_two, second, o_at, g_at, u_at, d_at, units, hops
    )
    backed = back(
        starts, qkv, kmem, vmem, attended, lse, first, second, o_at, x, gain_one, ghid, gn2, cosine, sine, hops
    )
    if lines:
        out, feed_grads = fed
        input_grad, model_grads, norms = backed
    else:
        out, input_grad = own_features(fed[0], me), own_features(backed[0], me)
        feed_grads, model_grads = summed(*fed[1:]), summed(*backed[1:3])
        norms = jnp.concatenate([backed[3], gn2], axis=0).T
        norms = lax.psum_scatter(norms, ("dp", "col"), scatter_dimension=0, tiled=True)
        norms = lax.psum(norms, "row")
    return (
        out,
        input_grad,
        model_grads[0],
        model_grads[1],
        model_grads[2],
        model_grads[3].T,
        feed_grads[0],
        feed_grads[1],
        feed_grads[2].T,
        norms[:, 0],
        norms[:, 1],
    )


def solution(mesh):
    tokens = P(("dp", "col"), "row")
    down = P("row", ("dp", "col"))
    gain = P(("dp", "col"))
    cache = P(("dp", "col"), None, "row")
    index = P(("dp", "col"), None, None)
    weights = (tokens, tokens, tokens, down, tokens, tokens, down)
    return jax.shard_map(
        on_device,
        mesh=mesh,
        in_specs=(tokens,)
        + weights
        + (gain, gain, cache, cache, index, index, P(("dp", "col"), None), gain, tokens),
        out_specs=(tokens, tokens) + weights + (gain, gain),
        check_vma=False,
    )
```

```python
import functools
import math

import jax
import jax.numpy as jnp
from jax import lax
from jax.experimental import pallas as pl
from jax.experimental.pallas import tpu as pltpu
from jax.sharding import PartitionSpec as P

HEAD_DIM = 128
SEQ_LEN = 1024
QROWS = 512
PIC = 256
MEM_BLK = 128
OWN_K = 2
PART_K = 2
SEQ_DEV = 2
QBLKS = 2
EPSILON = 1e-05
NEG = -1e30
CHUNK = 256
LANES = 128

BF = jnp.bfloat16
F32 = jnp.float32
LATE = 3
LOG2E = math.log2(math.e)
MESH = pl.DeviceIdType.MESH


def nn(a, b):
    return jnp.dot(a, b, preferred_element_type=F32)


def nt(a, b):
    return lax.dot_general(a, b, (((1,), (1,)), ((), ())), preferred_element_type=F32)


def tn(a, b):
    return lax.dot_general(a, b, (((0,), (0,)), ((), ())), preferred_element_type=F32)


def rotary_tables():
    half = HEAD_DIM // 2
    frequency = 10000.0 ** (-2.0 * jnp.arange(half, dtype=F32) / HEAD_DIM)
    angles = jnp.arange(SEQ_LEN, dtype=jnp.int32).astype(F32)[:, None] * frequency[None, :]
    cosine, sine = jnp.cos(angles), jnp.sin(angles)
    return jnp.concatenate([cosine, cosine], axis=1), jnp.concatenate([-sine, sine], axis=1)


def whole(shape):
    return pl.BlockSpec(shape, lambda *_: (0,) * len(shape))


def once(shape):
    return pl.BlockSpec(shape, lambda *_: (0,) * len(shape), pipeline_mode=pl.Buffered(1))


def params(limit=60):
    return pltpu.CompilerParams(
        vmem_limit_bytes=limit * 1024 * 1024
    )


def chunks(total, body, size=CHUNK):
    def step(i, carry):
        body(pl.ds(pl.multiple_of(i * size, size), size))
        return carry

    if total == size:
        body(pl.ds(0, size))
    else:
        lax.fori_loop(0, total // size, step, 0)


class Place:
    def __init__(self, nz):
        dp, self.me, self.z = lax.axis_index("dp"), lax.axis_index("row"), lax.axis_index("col")
        self.x, self.y, self.nz = dp % 2, dp // 2, nz
        self.core = (dp, 1 - self.me, self.z)
        self.next_x = (self.y * 2 + 1 - self.x, self.me, self.z)
        self.next_y = ((1 - self.y) * 2 + self.x, self.me, self.z)
        self.above = (dp, self.me, lax.rem(self.z + 1, nz))
        self.below = (dp, self.me, lax.rem(self.z + nz - 1, nz))
        self.has_above = self.z < nz - 1
        self.has_below = self.z > 0

    def corner(self):
        return ((1 - self.y) * 2 + 1 - self.x, self.me, self.z)

    def level(self, by):
        return (self.y * 2 + self.x, self.me, lax.rem(self.z + by, self.nz))

    def levels(self):
        return [self.level(by) for by in range(1, self.nz)]

    def plane(self):
        devices = []
        for by in range(1, 8):
            place = lax.rem(self.y * 4 + self.x * 2 + self.me + by, 8)
            devices.append((place // 2, place % 2, self.z))
        return devices

    def barrier(self, devices):
        semaphore = pltpu.get_barrier_semaphore()
        for device in devices:
            pl.semaphore_signal(semaphore, inc=1, device_id=device, device_id_type=MESH)
        pl.semaphore_wait(semaphore, len(devices))


def remote(source, target, sent, arrived, device):
    return pltpu.make_async_remote_copy(
        src_ref=source,
        dst_ref=target,
        send_sem=sent,
        recv_sem=arrived,
        device_id=device,
        device_id_type=MESH,
    )


def comm_params(number, limit=60):
    return pltpu.CompilerParams(
        vmem_limit_bytes=limit * 1024 * 1024, collective_id=number, has_side_effects=True
    )


HBM = pl.BlockSpec(memory_space=pl.ANY)


def gather_kernel(
    nz,
    w_ref,
    x_ref,
    cot_ref,
    ck_ref,
    cv_ref,
    out_ref,
    xs_ref,
    cots_ref,
    near_ref,
    wbuf,
    xbuf,
    cbuf,
    local,
    csent,
    carrived,
    sent_z,
    sent_xy,
    sent_diag,
    wsent,
    arrived_z,
    arrived_xy,
    arrived_diag,
    warrived,
):
    at = Place(nz)
    me, x, y, z = at.me, at.x, at.y, at.z
    tokens = xs_ref.shape[1]
    keys = ck_ref.shape[1]
    rows = w_ref.shape[0]
    part = rows // 2
    pending = []

    def go(copy, when=None):
        if when is None:
            copy.start()
            pending.append((None, copy))
        else:
            pl.when(when)(copy.start)
            pending.append((when, copy))

    own = out_ref.at[y, x, z, me]
    near_span = [near_ref.at[me, pl.ds(0, keys)], near_ref.at[me, pl.ds(keys, keys)]]
    keep = [
        (w_ref, wbuf, own),
        (x_ref.at[me], xbuf.at[0], xs_ref.at[me]),
        (cot_ref.at[me], xbuf.at[1], cots_ref.at[me]),
        (ck_ref.at[me], cbuf.at[0], near_span[0]),
        (cv_ref.at[me], cbuf.at[1], near_span[1]),
    ]
    loads = [pltpu.make_async_copy(a, b, local.at[i]) for i, (a, b, _) in enumerate(keep)]
    stores = [pltpu.make_async_copy(b, c, local.at[5 + i]) for i, (_, b, c) in enumerate(keep)]
    for copy in loads:
        copy.start()
    at.barrier([at.core, at.next_x, at.next_y, at.above, at.below])
    exchange = [
        remote(x_ref.at[1 - me], xs_ref.at[me], csent.at[0], carrived.at[0], at.core),
        remote(ck_ref.at[1 - me], near_ref.at[me, pl.ds(0, keys)], csent.at[1], carrived.at[1], at.core),
        remote(cv_ref.at[1 - me], near_ref.at[me, pl.ds(keys, keys)], csent.at[2], carrived.at[2], at.core),
        remote(cot_ref.at[1 - me], cots_ref.at[me], csent.at[3], carrived.at[3], at.core),
    ]

    def block(yy, xx, zz, half=None):
        ref = out_ref.at[yy, xx, zz, me]
        return ref if half is None else ref.at[pl.ds(half * part, part)]

    def core(ref, kind, zz, when=None):
        go(remote(ref, ref, wsent.at[kind, zz], warrived.at[kind, zz], at.core), when)

    def along_z(ref, zz, up, when):
        to = at.above if up else at.below
        go(remote(ref, ref, sent_z.at[int(up), zz], arrived_z.at[zz], to), when)

    def across(ref, zz, when=None):
        go(remote(ref, ref, sent_xy.at[0, zz], arrived_xy.at[0, zz], at.next_x), when)
        go(remote(ref, ref, sent_xy.at[1, zz], arrived_xy.at[1, zz], at.next_y), when)
        core(ref, 0, zz, when)

    loads[0].wait()
    stores[0].start()
    stores[0].wait()
    along_z(own, z, True, at.has_above)
    along_z(own, z, False, at.has_below)
    across(own, z)
    for copy in exchange:
        go(copy)
    for load, store in zip(loads[1:], stores[1:]):
        load.wait()
        store.start()

    def arrive_across(zz, when=None):
        def body():
            ref = block(y, 1 - x, zz)
            remote(ref, ref, sent_xy.at[0, zz], arrived_xy.at[0, zz], at.next_x).wait_recv()
            ref = block(1 - y, x, zz)
            remote(ref, ref, sent_xy.at[1, zz], arrived_xy.at[1, zz], at.next_y).wait_recv()

        body() if when is None else pl.when(when)(body)
        ref = block(y, 1 - x, zz, 0)
        go(remote(ref, ref, sent_diag.at[0, zz], arrived_diag.at[0, zz], at.next_y), when)
        ref = block(1 - y, x, zz, 1)
        go(remote(ref, ref, sent_diag.at[1, zz], arrived_diag.at[1, zz], at.next_x), when)
        core(block(y, 1 - x, zz), 1, zz, when)
        core(block(1 - y, x, zz), 2, zz, when)

    for step in range(1, nz):
        for up in (True, False):
            zz = z - step if up else z + step
            valid = zz >= 0 if up else zz < nz
            zc = jnp.clip(zz, 0, nz - 1)
            ref = block(y, x, zc)

            def wait(ref=ref, zc=zc, up=up):
                to = at.below if up else at.above
                remote(ref, ref, sent_z.at[int(up), zc], arrived_z.at[zc], to).wait_recv()

            pl.when(valid)(wait)
            along_z(ref, zc, up, valid & (at.has_above if up else at.has_below))
            across(ref, zc, valid)
        if step == 1:
            arrive_across(z)
        else:
            arrive_across(jnp.clip(z - step + 1, 0, nz - 1), z - step + 1 >= 0)
            arrive_across(jnp.clip(z + step - 1, 0, nz - 1), z + step - 1 < nz)
    if nz == 1:
        arrive_across(z)
    else:
        arrive_across(jnp.clip(z - nz + 1, 0, nz - 1), z - nz + 1 >= 0)
        arrive_across(jnp.clip(z + nz - 1, 0, nz - 1), z + nz - 1 < nz)
    for zz in range(nz):
        for half in range(2):
            ref = block(1 - y, 1 - x, zz, half)
            back = at.next_y if half == 0 else at.next_x
            remote(ref, ref, sent_diag.at[half, zz], arrived_diag.at[half, zz], back).wait_recv()
            core(ref, 3 + half, zz)
    for copy in stores[1:]:
        copy.wait()
    for copy in exchange:
        copy.wait_recv()
    for zz in range(nz):
        for kind, ref in enumerate(
            (
                out_ref.at[y, x, zz, 1 - me],
                out_ref.at[y, 1 - x, zz, 1 - me],
                out_ref.at[1 - y, x, zz, 1 - me],
                out_ref.at[1 - y, 1 - x, zz, 1 - me, pl.ds(0, part)],
                out_ref.at[1 - y, 1 - x, zz, 1 - me, pl.ds(part, part)],
            )
        ):
            remote(ref, ref, wsent.at[kind, zz], warrived.at[kind, zz], at.core).wait_recv()
    for when, copy in pending:
        copy.wait_send() if when is None else pl.when(when)(copy.wait_send)


def gather(w, x, cot, cache_keys, cache_values, nz):
    dma = pltpu.SemaphoreType.DMA
    _, tokens, half = x.shape
    keys = cache_keys.shape[1]
    full = jax.ShapeDtypeStruct((2, tokens, half), BF)
    return pl.pallas_call(
        functools.partial(gather_kernel, nz),
        in_specs=[HBM] * 5,
        out_specs=[HBM] * 4,
        out_shape=[
            jax.ShapeDtypeStruct((2, 2, nz, 2) + w.shape, BF),
            full,
            full,
            jax.ShapeDtypeStruct((2, 2 * keys, half), BF),
        ],
        scratch_shapes=[
            pltpu.VMEM(w.shape, BF),
            pltpu.VMEM(x.shape, BF),
            pltpu.VMEM((2, keys, half), BF),
            dma((10,)),
            dma((4,)),
            dma((4,)),
            dma((2, nz)),
            dma((2, nz)),
            dma((2, nz)),
            dma((5, nz)),
            dma((nz,)),
            dma((2, nz)),
            dma((2, nz)),
            dma((5, nz)),
        ],
        compiler_params=comm_params(0),
        name="gather",
    )(w, x, cot, cache_keys, cache_values)


class Sums:
    BUFFERS = 10

    @staticmethod
    def last(halved):
        return 4 if halved else 3

    @staticmethod
    def scratch(parts, rows, tiles, nz, halved, taken=False):
        dma = pltpu.SemaphoreType.DMA
        slab = rows // 4
        pairs = pltpu.VMEM((1, 1, 16, LANES) if taken else (2, parts, rows, LANES), BF)
        return [
            pairs,
            pairs,
            pltpu.VMEM((tiles, parts, rows, LANES), BF),
            pltpu.VMEM((tiles, 2, parts, slab // 2, LANES) if halved else (tiles, 1, parts, slab, LANES), BF),
            pltpu.VMEM((tiles, 2, parts, slab, LANES), BF),
            pltpu.VMEM((tiles, nz - 1, parts, slab // nz, LANES), BF),
            dma((tiles, 5)),
            dma((tiles, 5)),
            dma((tiles, nz - 1)),
            dma((tiles, nz - 1)),
        ]

    def __init__(self, at, halved, refs, left=0):
        (
            self.mine,
            self.other,
            self.total,
            self.diag,
            self.side,
            self.hop,
            self.sent,
            self.arrived,
            self.hop_sent,
            self.hop_arrived,
        ) = refs
        self.at, self.halved = at, halved
        self.tiles, _, self.rows, _ = self.total.shape
        self.left, self.early = left, self.tiles - left
        self.slab = self.rows // 4
        self.block = self.slab // at.nz

    def span(self, y, x, first=0, size=None):
        start = pl.multiple_of((y * 2 + x) * self.slab + first, self.block)
        return pl.ds(start, self.slab if size is None else size)

    def copy(self, j, span, target, index, device):
        return remote(
            self.total.at[j, :, span], target, self.sent.at[j, index], self.arrived.at[j, index], device
        )

    def core_copy(self, j):
        return remote(
            self.other.at[j % 2],
            self.total.at[j],
            self.sent.at[j, 0],
            self.arrived.at[j, 0],
            self.at.core,
        )

    def diag_copies(self, j):
        at, part = self.at, self.slab // 2
        y, x = 1 - at.y, 1 - at.x
        if not self.halved:
            return [self.copy(j, self.span(y, x), self.diag.at[j, 0], 1, at.corner())]
        return [
            self.copy(j, self.span(y, x, i * part, part), self.diag.at[j, i], 1 + i, device)
            for i, device in enumerate((at.next_x, at.next_y))
        ]

    def side_copies(self, j):
        at = self.at
        return [
            self.copy(j, self.span(at.y, 1 - at.x), self.side.at[j, 0], 3, at.next_x),
            self.copy(j, self.span(1 - at.y, at.x), self.side.at[j, 1], 4, at.next_y),
        ]

    def hop_copies(self, j):
        at = self.at
        copies = []
        for by in range(1, at.nz):
            device = at.level(by)
            copies.append(
                remote(
                    self.total.at[j, :, self.span(at.y, at.x, device[2] * self.block, self.block)],
                    self.hop.at[j, by - 1],
                    self.hop_sent.at[j, by - 1],
                    self.hop_arrived.at[j, by - 1],
                    device,
                )
            )
        return copies

    def add(self, j, span, *values):
        total = self.total[j, :, span, :].astype(F32)
        for value in values:
            total = total + value.astype(F32)
        self.total[j, :, span, :] = total.astype(BF)

    def start(self, j):
        self.core_copy(j).start()

    def after_core(self, j):
        self.core_copy(j).wait()

        def body(rows):
            self.add(j, rows, self.mine[j % 2, :, rows, :])

        chunks(self.rows, body)

    def begin(self, j):
        for copy in self.diag_copies(j):
            copy.start()
        if not self.halved:
            for copy in self.side_copies(j):
                copy.start()

    def after_diag(self, j):
        at, part = self.at, self.slab // 2
        for copy in self.diag_copies(j):
            copy.wait()
        self.add(j, self.span(1 - at.y, at.x, 0, part), self.diag[j, 0])
        self.add(j, self.span(at.y, 1 - at.x, part, part), self.diag[j, 1])
        for copy in self.side_copies(j):
            copy.start()

    def after_side(self, j):
        at = self.at
        for copy in self.side_copies(j):
            copy.wait()
        values = [self.side[j, 0], self.side[j, 1]]
        if not self.halved:
            for copy in self.diag_copies(j):
                copy.wait()
            values.append(self.diag[j, 0])
        self.add(j, self.span(at.y, at.x), *values)
        for copy in self.hop_copies(j):
            copy.start()

    def result(self, j):
        at = self.at
        for copy in self.hop_copies(j):
            copy.wait()
        value = self.total[j, :, self.span(at.y, at.x, at.z * self.block, self.block), :].astype(F32)
        for by in range(at.nz - 1):
            value = value + self.hop[j, by].astype(F32)
        return value

    def advance(self, step, store, leave=None, taken=False):
        def on(behind, body, first, last):
            j = step - behind
            pl.when((j >= first) & (j < last))(lambda: body(jnp.clip(j, first, last - 1)))

        def summed(j):
            self.after_core(j)
            self.begin(j)

        def left(j):
            self.after_core(j)
            leave(self.total[j])

        if not taken:
            on(1, summed, 0, self.early)
        if self.left:
            on(1, left, self.early, self.tiles)
        if self.halved:
            on(2, self.after_diag, 0, self.early)
        on(self.last(self.halved) - 1, self.after_side, 0, self.early)
        on(self.last(self.halved), lambda j: store(self.result(j)), 0, self.early)


class Norms:
    BUFFERS = 7

    @staticmethod
    def scratch(model, nz):
        dma = pltpu.SemaphoreType.DMA
        return [
            pltpu.VMEM((4, 8, model // 4), F32),
            pltpu.VMEM((8, 8, model // 4), F32),
            pltpu.VMEM((nz, 8, LANES), F32),
            dma((7,)),
            dma((7,)),
            dma((nz - 1,)),
            dma((nz - 1,)),
        ]

    def __init__(self, at, refs):
        self.at = at
        self.own, self.parts, self.level, self.sent, self.arrived, self.hop_sent, self.hop_arrived = refs

    def plane_copies(self):
        at = self.at
        me = at.y * 4 + at.x * 2 + at.me
        return [
            remote(self.own.at[device[0]], self.parts.at[me], self.sent.at[i], self.arrived.at[i], device)
            for i, device in enumerate(at.plane())
        ]

    def hop_copies(self):
        at = self.at
        me = at.y * 4 + at.x * 2 + at.me
        copies = []
        for by in range(1, at.nz):
            device = at.level(by)
            lanes = pl.ds(pl.multiple_of(device[2] // 2 * LANES, LANES), LANES)
            copies.append(
                remote(
                    self.own.at[0, :, lanes],
                    self.level.at[at.z],
                    self.hop_sent.at[by - 1],
                    self.hop_arrived.at[by - 1],
                    device,
                )
            )
        return copies

    def start(self, rows):
        at = self.at
        width = self.own.shape[2]
        for d in range(4):
            self.own[d] = rows[:, d * width : (d + 1) * width]
        self.parts[at.y * 4 + at.x * 2 + at.me] = self.own[at.y * 2 + at.x]
        for copy in self.plane_copies():
            copy.start()

    def after_plane(self):
        at = self.at
        for copy in self.plane_copies():
            copy.wait()
        total = self.parts[0]
        for i in range(1, 8):
            total = total + self.parts[i]
        self.own[0] = total
        lanes = pl.ds(pl.multiple_of(at.z // 2 * LANES, LANES), LANES)
        self.level[at.z] = self.own[0, :, lanes]
        for copy in self.hop_copies():
            copy.start()

    def result(self):
        for copy in self.hop_copies():
            copy.wait()
        total = self.level[0]
        for i in range(1, self.at.nz):
            total = total + self.level[i]
        return total


class Unsummed:
    class Tile:
        def __init__(self, ref):
            self.ref = ref

        def __setitem__(self, index, value):
            self.ref[index[1:]] = value

    def __init__(self, mine, other):
        self.mine, self.other = Unsummed.Tile(mine), Unsummed.Tile(other)

    def start(self, j):
        pass

    def advance(self, step, store, leave=None):
        pass


def features(ref, rows):
    return jnp.concatenate([ref[0, rows, :], ref[1, rows, :]], axis=1)


def pair(ref, model):
    return jnp.concatenate(
        [ref[:, 0].reshape(model, LANES), ref[:, 1].reshape(model, LANES)], axis=1
    )


def normal_of(x):
    inverse = lax.rsqrt(jnp.mean(x * x, axis=1, keepdims=True) + EPSILON)
    return x * inverse, inverse


def norm_back(normal, inverse, gain, grad):
    scaled = grad * gain
    return inverse * (scaled - normal * jnp.mean(scaled * normal, axis=1, keepdims=True))


def qkv_kernel(x_ref, gain_ref, w_ref, cos_ref, sin_ref, out_ref, n1_ref):
    part = pl.program_id(0)
    tokens, model = n1_ref.shape

    @pl.when((part == 0) & (pl.program_id(1) == 0))
    def _():
        def norm(rows):
            normal, _ = normal_of(features(x_ref, rows).astype(F32))
            n1_ref[rows, :] = (normal * gain_ref[...]).astype(BF)

        chunks(tokens, norm)

    def project(rows):
        y = nn(n1_ref[rows, :], w_ref[...].reshape(model, -1))
        cosine, sine = cos_ref[rows, :], sin_ref[rows, :]
        for h in range(y.shape[1] // HEAD_DIM):
            lanes = slice(h * HEAD_DIM, (h + 1) * HEAD_DIM)
            u = y[:, lanes]
            turned = u * cosine + pltpu.roll(u, HEAD_DIM // 2, 1) * sine
            out_ref[rows, lanes] = jnp.where(part < 2, turned, u).astype(BF)

    chunks(tokens, project, tokens)


def project_qkv(x, gain, gathered, cosine, sine):
    halves, tokens, half = x.shape
    groups, _, rows, _ = gathered.shape
    return pl.pallas_call(
        qkv_kernel,
        grid=(3, halves),
        in_specs=[
            whole(x.shape),
            whole(gain.shape),
            pl.BlockSpec((groups, None, rows, half), lambda m, h: (0, h, 0, m)),
            whole(cosine.shape),
            whole(sine.shape),
        ],
        out_specs=pl.BlockSpec((None, None, tokens, half), lambda m, h: (m, h, 0, 0)),
        out_shape=jax.ShapeDtypeStruct((3, halves, tokens, half), BF),
        scratch_shapes=[pltpu.VMEM((tokens, halves * half), BF)],
        compiler_params=params(),
        name="project_qkv",
    )(x, gain, gathered, cosine, sine)


def fill_memory(idx_ref, near_ref, far_ref, offset, mem_ref):
    for b in range(QBLKS):
        for j in range(OWN_K + PART_K):
            ref, at = (near_ref, b * OWN_K + j) if j < OWN_K else (far_ref, QBLKS * OWN_K + b * PART_K + j - OWN_K)
            start = pl.multiple_of(idx_ref[at] * MEM_BLK, MEM_BLK) + offset
            mem_ref[b, j * MEM_BLK : (j + 1) * MEM_BLK, :] = ref[pl.ds(start, MEM_BLK), :]


def masked(scores, start, first):
    keys, queries = scores.shape
    at = first + lax.broadcasted_iota(jnp.int32, (1, queries), 1)
    limit = jnp.where((at >= start) & (at < start + PIC), start + PIC - 1, at)
    key = lax.broadcasted_iota(jnp.int32, (keys, queries), 0)
    return jnp.where(key <= limit, scores, NEG)


def attend_kernel(
    idx_ref, q_ref, k_ref, v_ref, near_ref, far_ref, out_ref, lse_ref, kmem_ref, vmem_ref
):
    keys = near_ref.shape[0] // 2
    fill_memory(idx_ref, near_ref, far_ref, 0, kmem_ref)
    fill_memory(idx_ref, near_ref, far_ref, keys, vmem_ref)
    scale = LOG2E / math.sqrt(HEAD_DIM)
    base = QBLKS * (OWN_K + PART_K)
    for b in range(QBLKS):
        start = idx_ref[base + b] - b * QROWS

        def body(i, carry, b=b, start=start):
            first = pl.multiple_of(i * CHUNK, CHUNK)
            rows = pl.ds(pl.multiple_of(b * QROWS + first, CHUNK), CHUNK)
            q = q_ref[rows, :]
            parts = []
            for n in range(b + 1):
                span = slice(n * QROWS, (n + 1) * QROWS)
                s = nt(k_ref[span, :], q)
                parts.append((masked(s, start, first) if n == b else s, v_ref[span, :]))
            parts.append((nt(kmem_ref[b], q), vmem_ref[b]))
            top = functools.reduce(
                jnp.maximum, [jnp.max(s, axis=0, keepdims=True) for s, _ in parts]
            )
            shift = top * scale
            total = jnp.zeros_like(top)
            acc = jnp.zeros((HEAD_DIM, CHUNK), F32)
            for s, v in parts:
                e = jnp.exp2(s * scale - shift)
                total = total + jnp.sum(e, axis=0, keepdims=True)
                acc = acc + tn(v, e.astype(BF))
            out_ref[rows, :] = jnp.transpose(acc / total).astype(BF)
            lse_ref[:, rows] = shift + jnp.log2(total)
            return carry

        lax.fori_loop(0, QROWS // CHUNK, body, 0)


def attend(idx, qkv, near, far):
    _, halves, tokens, half = qkv.shape
    here = half // HEAD_DIM
    cached = near.shape[1]
    memory = (OWN_K + PART_K) * MEM_BLK
    column = lambda m: pl.BlockSpec(
        (None, None, tokens, HEAD_DIM), lambda h, idx: (m, h // here, 0, h % here)
    )
    cache = pl.BlockSpec((None, cached, HEAD_DIM), lambda h, idx: (h // here, 0, h % here))
    chosen = pl.BlockSpec((None, QBLKS, memory, HEAD_DIM), lambda h, idx: (h // here, 0, 0, h % here))
    chosen_shape = jax.ShapeDtypeStruct((halves, QBLKS, memory, half), BF)
    return pl.pallas_call(
        attend_kernel,
        grid_spec=pltpu.PrefetchScalarGridSpec(
            num_scalar_prefetch=1,
            grid=(halves * here,),
            in_specs=[column(0), column(1), column(2), cache, cache],
            out_specs=[
                pl.BlockSpec((None, tokens, HEAD_DIM), lambda h, idx: (h // here, 0, h % here)),
                pl.BlockSpec((None, None, 1, tokens), lambda h, idx: (h // here, h % here, 0, 0)),
                chosen,
                chosen,
            ],
        ),
        out_shape=[
            jax.ShapeDtypeStruct((halves, tokens, half), BF),
            jax.ShapeDtypeStruct((halves, here, 1, tokens), F32),
            chosen_shape,
            chosen_shape,
        ],
        compiler_params=params(),
        name="attend",
    )(idx, qkv, qkv, qkv, near, far)


def split_store(me, value, mine_ref, other_ref, index):
    low, high = value[:, :LANES], value[:, LANES:]
    mine_ref[index] = jnp.where(me == 0, low, high)
    other_ref[index] = jnp.where(me == 0, high, low)


def send_halves(at, buffer, out_ref, local, sent, arrived):
    tokens = buffer.shape[1]
    rows = pl.ds(pl.multiple_of(at.me * tokens, tokens), tokens)
    return (
        pltpu.make_async_copy(buffer.at[at.me], out_ref.at[rows], local),
        remote(buffer.at[1 - at.me], out_ref.at[rows], sent, arrived, at.core),
    )


def feed_kernel(
    nz,
    steps,
    x_ref,
    att_ref,
    cot_ref,
    gain_ref,
    wo_ref,
    wg_ref,
    wu_ref,
    wd_ref,
    ghid_ref,
    gn2_ref,
    *refs,
):
    if nz:
        out_ref, grad_ref, late_ref, *refs = refs
    else:
        result_ref, mine_ref, other_ref, *refs = refs
    hid_ref, n2_ref, n2t_ref, cott_ref, acc_ref, dn_ref, a_ref, dg_ref, du_ref, *refs = refs
    tokens, model = hid_ref.shape
    half = model // 2
    step = pl.program_id(0)
    me = lax.axis_index("row")
    copies = []
    if nz:
        at = Place(nz)
        result_ref, local, sent, arrived, *refs = refs
        sums = Sums(at, True, refs, LATE)
        copies = send_halves(at, result_ref, out_ref, local.at[0], sent.at[0], arrived.at[0])
    else:
        sums = Unsummed(mine_ref, other_ref)

    def wo_half(h):
        return wo_ref[:, h].reshape(model, half)

    @pl.when(step == 0)
    def _():
        if nz:
            at.barrier([at.core, at.next_x, at.next_y] + at.levels())

        def start(rows):
            hidden = features(x_ref, rows).astype(F32)
            for h in range(2):
                hidden = hidden + nt(att_ref[h, rows, :], wo_half(h))
            hid_ref[rows, :] = hidden
            normal, _ = normal_of(hidden)
            n2_ref[rows, :] = (normal * gain_ref[...]).astype(BF)
            n2t_ref[:, rows] = jnp.transpose(n2_ref[rows, :])
            cott_ref[:, rows] = jnp.transpose(features(cot_ref, rows))
            acc_ref[rows, :] = jnp.zeros((CHUNK, model), F32)
            dn_ref[rows, :] = jnp.zeros((CHUNK, model), F32)

        chunks(tokens, start)

    def store(value):
        grad_ref[...] = value

    def leave(value):
        late_ref[...] = value

    def forward_back(rows):
        n2 = n2_ref[rows, :]
        gating = nn(n2, pair(wg_ref, model))
        upward = nn(n2, pair(wu_ref, model))
        gactive = nn(features(cot_ref, rows), pair(wd_ref, model))
        sigmoid = 1.0 / (1.0 + jnp.exp(-gating))
        silu = gating * sigmoid
        a_ref[rows, :] = (silu * upward).astype(BF)
        dg_ref[rows, :] = (gactive * upward * (sigmoid + silu * (1.0 - sigmoid))).astype(BF)
        du_ref[rows, :] = (gactive * silu).astype(BF)
        acc_ref[rows, :] += nt(a_ref[rows, :], pair(wd_ref, model))
        dn_ref[rows, :] += nt(dg_ref[rows, :], pair(wg_ref, model)) + nt(
            du_ref[rows, :], pair(wu_ref, model)
        )

    @pl.when(step < steps)
    def _():
        chunks(tokens, forward_back, tokens)
        slot = step % 2

        def weights(rows):
            n2t = n2t_ref[rows, :]
            for p, value in enumerate(
                (nn(n2t, dg_ref[...]), nn(n2t, du_ref[...]), nn(cott_ref[rows, :], a_ref[...]))
            ):
                split_store(me, value.astype(BF), sums.mine, sums.other, (slot, p, rows))

        chunks(model, weights, model)
        sums.start(step)

    sums.advance(step, store, leave)

    @pl.when(step == (steps if nz else steps - 1))
    def _():
        gn2_ref[...] = jnp.zeros_like(gn2_ref)

        def finish(rows):
            hidden = hid_ref[rows, :]
            result = (hidden + acc_ref[rows, :]).astype(BF)
            result_ref[0, rows, :] = result[:, :half]
            result_ref[1, rows, :] = result[:, half:]
            normal, inverse = normal_of(hidden)
            dn = dn_ref[rows, :]
            gn2_ref[...] += jnp.sum(dn * normal, axis=0, keepdims=True)
            ghid_ref[rows, :] = features(cot_ref, rows).astype(F32) + norm_back(
                normal, inverse, gain_ref[...], dn
            )

        chunks(tokens, finish)
        for copy in copies:
            copy.start()

    if nz:

        @pl.when(step == pl.num_programs(0) - 1)
        def _():
            for copy in copies:
                copy.wait()


def feed(x, attended, cotangent, gain, gathered, o_at, g_at, u_at, d_at, units, nz):
    halves, tokens, half = x.shape
    model = halves * half
    groups, _, rows, _ = gathered.shape
    steps = units // LANES
    tile = lambda at: pl.BlockSpec(
        (groups, halves, rows, LANES),
        lambda j: (0, 0, 0, at // LANES + jnp.minimum(j, steps - 1)),
    )
    big = lambda dtype: pltpu.VMEM((tokens, model), dtype)
    small = pltpu.VMEM((tokens, 2 * LANES), BF)
    early = steps - LATE
    last = Sums.last(True)
    dma = pltpu.SemaphoreType.DMA((1,))
    if nz:
        out_specs = [
            HBM,
            pl.BlockSpec((3, rows, LANES), lambda j: (0, 0, jnp.clip(j - last, 0, early - 1))),
            pl.BlockSpec((3, model, LANES), lambda j: (0, 0, jnp.clip(j - 1 - early, 0, LATE - 1))),
        ]
        out_shape = [
            jax.ShapeDtypeStruct((halves * tokens, half), BF),
            jax.ShapeDtypeStruct((3, rows, early * LANES), F32),
            jax.ShapeDtypeStruct((3, model, LATE * LANES), BF),
        ]
        more = [pltpu.VMEM(x.shape, BF), dma, dma, dma] + Sums.scratch(3, model, steps, nz, True)
    else:
        grads = pl.BlockSpec((3, model, LANES), lambda j: (0, 0, j))
        out_specs = [once(x.shape), grads, grads]
        grads = jax.ShapeDtypeStruct((3, model, units), BF)
        out_shape = [jax.ShapeDtypeStruct(x.shape, BF), grads, grads]
        more = []
    return pl.pallas_call(
        functools.partial(feed_kernel, nz, steps),
        grid=(max(steps + 1, early + last) if nz else steps,),
        in_specs=[
            once(x.shape),
            once(x.shape),
            once(x.shape),
            once(gain.shape),
            pl.BlockSpec(
                (groups, halves, rows, half),
                lambda j: (0, 0, 0, o_at // half),
                pipeline_mode=pl.Buffered(1),
            ),
            tile(g_at),
            tile(u_at),
            tile(d_at),
        ],
        out_specs=[once((tokens, model)), once(gain.shape)] + out_specs,
        out_shape=[
            jax.ShapeDtypeStruct((tokens, model), F32),
            jax.ShapeDtypeStruct(gain.shape, F32),
        ]
        + out_shape,
        scratch_shapes=[big(F32), big(BF), big(BF), big(BF), big(F32), big(F32), small, small, small]
        + more,
        compiler_params=comm_params(1) if nz else params(),
        name="feed",
    )(x, attended, cotangent, gain, gathered, gathered, gathered, gathered)


def back_kernel(
    nz,
    steps,
    starts_ref,
    qkv_ref,
    kmem_ref,
    vmem_ref,
    att_ref,
    lse_ref,
    wo_ref,
    wq_ref,
    wk_ref,
    wv_ref,
    x_ref,
    gain_ref,
    ghid_ref,
    gn2_ref,
    cos_ref,
    sin_ref,
    *refs,
):
    if nz:
        left_ref, out_ref, grad_ref, late_ref, norms_ref, *refs = refs
    else:
        result_ref, mine_ref, other_ref, gn1_ref, *refs = refs
    gmix_ref, gmixt_ref, n1t_ref, dn_ref, gatt_ref, g_ref, dk_ref, dv_ref, *refs = refs
    tokens, model = ghid_ref.shape
    half = model // 2
    step = pl.program_id(0)
    me = lax.axis_index("row")
    copies = []
    if nz:
        at = Place(nz)
        result_ref, local, sent, arrived, *refs = refs
        sums = Sums(at, False, refs[: Sums.BUFFERS])
        late = Sums(at, True, refs[Sums.BUFFERS : 2 * Sums.BUFFERS])
        norms = Norms(at, refs[2 * Sums.BUFFERS :])
        copies = send_halves(at, result_ref, out_ref, local.at[0], sent.at[0], arrived.at[0])
    else:
        sums = Unsummed(mine_ref, other_ref)
    scale = LOG2E / math.sqrt(HEAD_DIM)
    plain = 1.0 / math.sqrt(HEAD_DIM)

    @pl.when(step == 0)
    def _():
        if nz:
            at.barrier(at.plane() + at.levels())

        def start(rows):
            normal, _ = normal_of(features(x_ref, rows).astype(F32))
            n1t_ref[:, rows] = jnp.transpose((normal * gain_ref[...]).astype(BF))
            gmix_ref[rows, :] = ghid_ref[rows, :].astype(BF)
            gmixt_ref[:, rows] = jnp.transpose(gmix_ref[rows, :])
            dn_ref[rows, :] = jnp.zeros((CHUNK, model), F32)

        chunks(tokens, start)

    def store(value):
        grad_ref[...] = value

    def store_late(value):
        late_ref[...] = value

    if nz:

        @pl.when(step < LATE)
        def _():
            late.total[step] = left_ref[...]
            late.begin(step)

    def unturn(g, rows):
        return g * cos_ref[rows, :] - pltpu.roll(g, HEAD_DIM // 2, 1) * sin_ref[rows, :]

    def one_head(hh, carry):
        dk_ref[...] = jnp.zeros_like(dk_ref)
        dv_ref[...] = jnp.zeros_like(dv_ref)
        for b in range(QBLKS):
            start = starts_ref[b] - b * QROWS

            def body(i, carry, b=b, start=start):
                first = pl.multiple_of(i * CHUNK, CHUNK)
                rows = pl.ds(pl.multiple_of(b * QROWS + first, CHUNK), CHUNK)
                q = qkv_ref[0, hh, rows, :]
                do = gatt_ref[hh, rows, :]
                lse = lse_ref[hh, 0, :, rows]
                dots = jnp.transpose(do.astype(F32) * att_ref[hh, rows, :].astype(F32))
                dot = jnp.sum(dots, axis=0, keepdims=True)
                dq = jnp.zeros((HEAD_DIM, CHUNK), F32)
                for n in range(b + 2):
                    span = slice(n * QROWS, (n + 1) * QROWS)
                    if n <= b:
                        k, v = qkv_ref[1, hh, span, :], qkv_ref[2, hh, span, :]
                    else:
                        k, v = kmem_ref[hh, b], vmem_ref[hh, b]
                    s = nt(k, q)
                    if n == b:
                        s = masked(s, start, first)
                    share = jnp.exp2(s * scale - lse)
                    ds = (share * (nt(v, do) - dot)).astype(BF)
                    if n <= b:
                        dv_ref[span, :] += nn(share.astype(BF), do)
                        dk_ref[span, :] += nn(ds, q)
                    dq = dq + tn(k, ds)
                g_ref[0, hh, rows, :] = unturn(jnp.transpose(dq) * plain, rows).astype(BF)
                return carry

            lax.fori_loop(0, QROWS // CHUNK, body, 0)

        def finish(rows):
            g_ref[1, hh, rows, :] = unturn(dk_ref[rows, :] * plain, rows).astype(BF)
            g_ref[2, hh, rows, :] = dv_ref[rows, :].astype(BF)

        chunks(tokens, finish)
        return carry

    @pl.when(step < steps)
    def _():
        def grad_attended(rows):
            value = nn(gmix_ref[rows, :], pair(wo_ref, model)).astype(BF)
            gatt_ref[0, rows, :] = value[:, :LANES]
            gatt_ref[1, rows, :] = value[:, LANES:]

        chunks(tokens, grad_attended, tokens)

    sums.advance(step, store)
    if nz:
        late.advance(step + 1, store_late, taken=True)

    @pl.when(step < steps)
    def _():
        lax.fori_loop(0, 2, one_head, 0)
        slot = step % 2

        def weights(rows):
            n1t = n1t_ref[rows, :]
            for p in range(3):
                value = nn(n1t, jnp.concatenate([g_ref[p, 0], g_ref[p, 1]], axis=1))
                split_store(me, value.astype(BF), sums.mine, sums.other, (slot, p, rows))
            value = nn(gmixt_ref[rows, :], jnp.concatenate([att_ref[0], att_ref[1]], axis=1))
            split_store(me, value.astype(BF), sums.mine, sums.other, (slot, 3, rows))

        chunks(model, weights, model)
        sums.start(step)

        def inward(rows):
            total = dn_ref[rows, :]
            for p, ref in enumerate((wq_ref, wk_ref, wv_ref)):
                g = jnp.concatenate([g_ref[p, 0, rows, :], g_ref[p, 1, rows, :]], axis=1)
                total = total + nt(g, pair(ref, model))
            dn_ref[rows, :] = total

        chunks(tokens, inward, tokens)

    @pl.when(step == (steps if nz else steps - 1))
    def _():
        def finish(rows, carry):
            normal, inverse = normal_of(features(x_ref, rows).astype(F32))
            dn = dn_ref[rows, :]
            value = (ghid_ref[rows, :] + norm_back(normal, inverse, gain_ref[...], dn)).astype(BF)
            result_ref[0, rows, :] = value[:, :half]
            result_ref[1, rows, :] = value[:, half:]
            return carry + jnp.sum(dn * normal, axis=0, keepdims=True)

        gn1 = lax.fori_loop(
            0,
            tokens // CHUNK,
            lambda i, c: finish(pl.ds(pl.multiple_of(i * CHUNK, CHUNK), CHUNK), c),
            jnp.zeros((1, model), F32),
        )
        for copy in copies:
            copy.start()
        if not nz:
            gn1_ref[...] = gn1
            return
        row = lax.broadcasted_iota(jnp.int32, (8, model), 0)
        norms.start(jnp.where(row == 0, gn1, jnp.where(row == 1, gn2_ref[...], 0.0)))

    if nz:

        @pl.when(step == steps + 1)
        def _():
            norms.after_plane()

        @pl.when(step == steps + 2)
        def _():
            norms_ref[...] = norms.result()

        @pl.when(step == pl.num_programs(0) - 1)
        def _():
            for copy in copies:
                copy.wait()


def back(starts, qkv, kmem, vmem, attended, lse, first, second, o_at, x, gain, ghid, gn2, cosine, sine, nz, *left):
    halves, tokens, half = x.shape
    model = halves * half
    groups, _, rows, _ = first.shape
    steps = half // HEAD_DIM
    memory = kmem.shape[2]
    now = lambda j: jnp.minimum(j, steps - 1)
    tile = lambda at: pl.BlockSpec(
        (groups, halves, rows, LANES), lambda j: (0, 0, 0, at // LANES + now(j))
    )
    chosen = pl.BlockSpec((halves, QBLKS, memory, HEAD_DIM), lambda j: (0, 0, 0, now(j)))
    big = lambda dtype: pltpu.VMEM((tokens, model), dtype)
    last = Sums.last(False)
    dma = pltpu.SemaphoreType.DMA((1,))
    if nz:
        out_specs = [
            HBM,
            pl.BlockSpec((4, rows, LANES), lambda j: (0, 0, jnp.clip(j - last, 0, steps - 1))),
            pl.BlockSpec((3, rows, LANES), lambda j: (0, 0, jnp.clip(j - last, 0, LATE - 1))),
            once((8, LANES)),
        ]
        out_shape = [
            jax.ShapeDtypeStruct((halves * tokens, half), BF),
            jax.ShapeDtypeStruct((4, rows, half), F32),
            jax.ShapeDtypeStruct((3, rows, LATE * LANES), F32),
            jax.ShapeDtypeStruct((8, LANES), F32),
        ]
        more = (
            [pltpu.VMEM(x.shape, BF), dma, dma, dma]
            + Sums.scratch(4, model, steps, nz, False)
            + Sums.scratch(3, model, LATE, nz, True, True)
            + Norms.scratch(model, nz)
        )
        left_spec = [pl.BlockSpec((3, model, LANES), lambda j: (0, 0, jnp.minimum(j, LATE - 1)))]
    else:
        grads = pl.BlockSpec((4, model, LANES), lambda j: (0, 0, j))
        out_specs = [once(x.shape), grads, grads, once(gain.shape)]
        grads = jax.ShapeDtypeStruct((4, model, half), BF)
        out_shape = [jax.ShapeDtypeStruct(x.shape, BF), grads, grads]
        out_shape.append(jax.ShapeDtypeStruct(gain.shape, F32))
        more = []
        left_spec = []
    return pl.pallas_call(
        functools.partial(back_kernel, nz, steps),
        grid=(steps + last if nz else steps,),
        in_specs=[
            pl.BlockSpec(memory_space=pltpu.SMEM),
            pl.BlockSpec((3, halves, tokens, HEAD_DIM), lambda j: (0, 0, 0, now(j))),
            chosen,
            chosen,
            pl.BlockSpec((halves, tokens, HEAD_DIM), lambda j: (0, 0, now(j))),
            pl.BlockSpec((halves, 1, 1, tokens), lambda j: (0, now(j), 0, 0)),
            tile(o_at),
            tile(0),
            tile(half),
            tile(2 * half),
            once(x.shape),
            once(gain.shape),
            once(ghid.shape),
            once(gain.shape),
            once(cosine.shape),
            once(sine.shape),
        ]
        + left_spec,
        out_specs=out_specs,
        out_shape=out_shape,
        scratch_shapes=[big(BF), big(BF), big(BF), big(F32)]
        + [
            pltpu.VMEM((halves, tokens, HEAD_DIM), BF),
            pltpu.VMEM((3, halves, tokens, HEAD_DIM), BF),
            pltpu.VMEM((tokens, HEAD_DIM), F32),
            pltpu.VMEM((tokens, HEAD_DIM), F32),
        ]
        + more,
        compiler_params=comm_params(2) if nz else params(),
        name="back",
    )(
        starts,
        qkv,
        kmem,
        vmem,
        attended,
        lse,
        second,
        first,
        first,
        first,
        x,
        gain,
        ghid,
        gn2,
        cosine,
        sine,
        *left,
    )


def exchange(value, line):
    step = 1 if line == "x" else 2
    return lax.ppermute(value, "dp", [(d, d ^ step) for d in range(4)])


def partner_cache(near, source):
    along_x, along_y = exchange(near, "x"), exchange(near, "y")
    corner = jnp.stack([exchange(along_x[0], "y"), exchange(along_y[1], "x")])
    which = source ^ lax.axis_index("dp")
    return jnp.where(which == 1, along_x, jnp.where(which == 2, along_y, corner))


def swap(value):
    return lax.ppermute(value, "row", [(0, 1), (1, 0)])


def in_order(mine, got, me):
    return jnp.where(me == 0, jnp.stack([mine, got]), jnp.stack([got, mine]))


def own_sequence(value, me):
    take = lambda i: lax.dynamic_index_in_dim(value, i, 0, keepdims=False)
    return in_order(take(me), swap(take(1 - me)), me)


def own_features(value, me):
    return own_sequence(value, me).reshape(-1, value.shape[2])


def summed(mine, other):
    total = mine.astype(F32) + swap(other).astype(F32)
    return lax.psum_scatter(total, ("dp", "col"), scatter_dimension=1, tiled=True)


def on_device(
    inputs,
    w_query,
    w_key,
    w_value,
    w_out,
    w_gate,
    w_up,
    w_down,
    norm_one,
    norm_two,
    cache_keys,
    cache_values,
    own_index,
    partner_index,
    picture_start,
    partner_seq,
    cotangent,
):
    me = lax.axis_index("row")
    nz = lax.axis_size("col")
    chips = lax.axis_size("dp") * nz
    half = inputs.shape[1]
    model = 2 * half
    units = w_gate.shape[1]
    rows = w_query.shape[0]

    gains = jnp.pad(jnp.stack([norm_one, norm_two], axis=1), ((0, 0), (0, LANES - 2)))
    first = jnp.concatenate([w_query, w_key, w_value, gains], axis=1)
    second = jnp.concatenate([w_out.T, w_gate, w_up, w_down.T], axis=1)
    second = lax.all_gather(second, ("dp", "col", "row"), axis=0, tiled=True)
    second = second.reshape(chips, 2, rows, -1)
    tokens = inputs.reshape(SEQ_DEV, SEQ_LEN, half)
    upstream = cotangent.reshape(SEQ_DEV, SEQ_LEN, half)
    lines = lax.axis_size("dp") == 4 and nz * rows == 2 * LANES and rows * 2 == LANES
    if lines:
        first, x, cot, near = gather(first, tokens, upstream, cache_keys, cache_values, nz)
    else:
        first = lax.all_gather(first, ("dp", "col", "row"), axis=0, tiled=True)
        x, cot = own_sequence(tokens, me), own_sequence(upstream, me)
        near = own_sequence(jnp.concatenate([cache_keys, cache_values], axis=1), me)
    first = first.reshape(chips, 2, rows, -1)
    gains = first[:, 0, :, 3 * half : 3 * half + 2].reshape(model, 2).astype(F32)
    gain_one, gain_two = gains[:, 0].reshape(1, model), gains[:, 1].reshape(1, model)

    pick = lambda table: lax.dynamic_index_in_dim(table, me, 0, keepdims=False).reshape(-1)
    source = lax.dynamic_index_in_dim(partner_seq, me, 0, keepdims=False) // SEQ_DEV // nz
    starts = pick(picture_start)
    idx = jnp.concatenate([pick(own_index), pick(partner_index), starts])
    cosine, sine = rotary_tables()

    if lines:
        far = partner_cache(near, source)
    else:
        far = lax.dynamic_index_in_dim(lax.all_gather(near, "dp", axis=0), source, 0, keepdims=False)
    qkv = project_qkv(x, gain_one, first, cosine, sine)
    attended, lse, kmem, vmem = attend(idx, qkv, near, far)
    o_at, g_at = 0, half
    u_at, d_at = g_at + units, g_at + 2 * units
    hops = nz if lines else 0
    ghid, gn2, *fed = feed(
        x, attended, cot, gain_two, second, o_at, g_at, u_at, d_at, units, hops
    )
    left = fed[2:] if lines else []
    backed = back(
        starts,
        qkv,
        kmem,
        vmem,
        attended,
        lse,
        first,
        second,
        o_at,
        x,
        gain_one,
        ghid,
        gn2,
        cosine,
        sine,
        hops,
        *left,
    )
    if lines:
        out, feed_grads, _ = fed
        input_grad, model_grads, late, norms = backed
        feed_grads = jnp.concatenate([feed_grads, late], axis=2)
        norms = lax.dynamic_slice_in_dim(norms[:2], lax.axis_index("col") % 2 * rows, rows, 1).T
    else:
        out, input_grad = own_features(fed[0], me), own_features(backed[0], me)
        feed_grads, model_grads = summed(*fed[1:]), summed(*backed[1:3])
        norms = jnp.concatenate([backed[3], gn2], axis=0).T
        norms = lax.psum_scatter(norms, ("dp", "col"), scatter_dimension=0, tiled=True)
        norms = lax.psum(norms, "row")
    return (
        out,
        input_grad,
        model_grads[0],
        model_grads[1],
        model_grads[2],
        model_grads[3].T,
        feed_grads[0],
        feed_grads[1],
        feed_grads[2].T,
        norms[:, 0],
        norms[:, 1],
    )


def solution(mesh):
    tokens = P(("dp", "col"), "row")
    down = P("row", ("dp", "col"))
    gain = P(("dp", "col"))
    cache = P(("dp", "col"), None, "row")
    index = P(("dp", "col"), None, None)
    weights = (tokens, tokens, tokens, down, tokens, tokens, down)
    return jax.shard_map(
        on_device,
        mesh=mesh,
        in_specs=(tokens,)
        + weights
        + (gain, gain, cache, cache, index, index, P(("dp", "col"), None), gain, tokens),
        out_specs=(tokens, tokens) + weights + (gain, gain),
        check_vma=False,
    )
```

```python
import functools
import math

import jax
import jax.numpy as jnp
from jax import lax
from jax.experimental import pallas as pl
from jax.experimental.pallas import tpu as pltpu
from jax.sharding import PartitionSpec as P

HEAD_DIM = 128
SEQ_LEN = 1024
QROWS = 512
PIC = 256
MEM_BLK = 128
OWN_K = 2
PART_K = 2
SEQ_DEV = 2
QBLKS = 2
EPSILON = 1e-05
NEG = -1e30
CHUNK = 256
LANES = 128

BF = jnp.bfloat16
F32 = jnp.float32
LATE = 3
LOG2E = math.log2(math.e)
MESH = pl.DeviceIdType.MESH


def nn(a, b):
    return jnp.dot(a, b, preferred_element_type=F32)


def nt(a, b):
    return lax.dot_general(a, b, (((1,), (1,)), ((), ())), preferred_element_type=F32)


def tn(a, b):
    return lax.dot_general(a, b, (((0,), (0,)), ((), ())), preferred_element_type=F32)


def rotary_tables():
    half = HEAD_DIM // 2
    frequency = 10000.0 ** (-2.0 * jnp.arange(half, dtype=F32) / HEAD_DIM)
    angles = jnp.arange(SEQ_LEN, dtype=jnp.int32).astype(F32)[:, None] * frequency[None, :]
    cosine, sine = jnp.cos(angles), jnp.sin(angles)
    return jnp.concatenate([cosine, cosine], axis=1), jnp.concatenate([-sine, sine], axis=1)


def whole(shape):
    return pl.BlockSpec(shape, lambda *_: (0,) * len(shape))


def once(shape):
    return pl.BlockSpec(shape, lambda *_: (0,) * len(shape), pipeline_mode=pl.Buffered(1))


def params(limit=60):
    return pltpu.CompilerParams(
        vmem_limit_bytes=limit * 1024 * 1024
    )


def chunks(total, body, size=CHUNK):
    def step(i, carry):
        body(pl.ds(pl.multiple_of(i * size, size), size))
        return carry

    if total == size:
        body(pl.ds(0, size))
    else:
        lax.fori_loop(0, total // size, step, 0)


class Place:
    def __init__(self, nz):
        dp, self.me, self.z = lax.axis_index("dp"), lax.axis_index("row"), lax.axis_index("col")
        self.x, self.y, self.nz = dp % 2, dp // 2, nz
        self.core = (dp, 1 - self.me, self.z)
        self.next_x = (self.y * 2 + 1 - self.x, self.me, self.z)
        self.next_y = ((1 - self.y) * 2 + self.x, self.me, self.z)
        self.above = (dp, self.me, lax.rem(self.z + 1, nz))
        self.below = (dp, self.me, lax.rem(self.z + nz - 1, nz))
        self.has_above = self.z < nz - 1
        self.has_below = self.z > 0

    def corner(self):
        return ((1 - self.y) * 2 + 1 - self.x, self.me, self.z)

    def level(self, by):
        return (self.y * 2 + self.x, self.me, lax.rem(self.z + by, self.nz))

    def levels(self):
        return [self.level(by) for by in range(1, self.nz)]

    def plane(self):
        devices = []
        for by in range(1, 8):
            place = lax.rem(self.y * 4 + self.x * 2 + self.me + by, 8)
            devices.append((place // 2, place % 2, self.z))
        return devices

    def barrier(self, devices):
        semaphore = pltpu.get_barrier_semaphore()
        for device in devices:
            pl.semaphore_signal(semaphore, inc=1, device_id=device, device_id_type=MESH)
        pl.semaphore_wait(semaphore, len(devices))


def remote(source, target, sent, arrived, device):
    return pltpu.make_async_remote_copy(
        src_ref=source,
        dst_ref=target,
        send_sem=sent,
        recv_sem=arrived,
        device_id=device,
        device_id_type=MESH,
    )


def comm_params(number, limit=60):
    return pltpu.CompilerParams(
        vmem_limit_bytes=limit * 1024 * 1024, collective_id=number, has_side_effects=True
    )


HBM = pl.BlockSpec(memory_space=pl.ANY)


class Sent:
    def __init__(self):
        self.copies = []

    def go(self, copy, when=None):
        if when is None:
            copy.start()
        else:
            pl.when(when)(copy.start)
        self.copies.append((when, copy))

    def wait(self):
        for when, copy in self.copies:
            copy.wait_send() if when is None else pl.when(when)(copy.wait_send)


class Spread:
    BUFFERS = 6

    @staticmethod
    def scratch(nz):
        dma = pltpu.SemaphoreType.DMA
        return [dma((4, nz)), dma((4, nz)), dma((2, 5, nz)), dma((5, nz)), dma((5, nz)), dma((5, nz))]

    def __init__(self, at, sent, source, target, refs):
        self.at, self.sent, self.source, self.target = at, sent, source, target
        (
            self.flat_sent,
            self.flat_arrived,
            self.line_sent,
            self.line_arrived,
            self.core_sent,
            self.core_arrived,
        ) = refs

    def block(self, place, zz, core=None):
        at = self.at
        y = at.y if place < 2 else 1 - at.y
        x = at.x if place in (0, 2) else 1 - at.x
        ref = self.target.at[y, x, zz, at.me if core is None else core]
        if place >= 3:
            part = self.source.shape[0] // 2
            ref = ref.at[pl.ds((place - 3) * part, part)]
        return ref

    def half(self, place, zz, piece):
        part = self.source.shape[0] // 2
        return self.block(place, zz).at[pl.ds(piece * part, part)]

    def own(self):
        return self.target.at[self.at.y, self.at.x, self.at.z, self.at.me]

    def flat(self, source, target, index, zz, device):
        return remote(source, target, self.flat_sent.at[index, zz], self.flat_arrived.at[index, zz], device)

    def sides(self, source, zz, when=None):
        target = self.block(0, zz)
        self.sent.go(self.flat(source, target, 0, zz, self.at.next_x), when)
        self.sent.go(self.flat(source, target, 1, zz, self.at.next_y), when)

    def from_side(self, index, zz, when=None):
        at = self.at
        place = 1 + index
        ref = self.block(place, zz)
        copy = self.flat(ref, ref, index, zz, (at.next_x, at.next_y)[index])
        copy.wait_recv() if when is None else pl.when(when)(copy.wait_recv)
        ref = self.half(place, zz, index)
        self.sent.go(self.flat(ref, ref, 2 + index, zz, (at.next_y, at.next_x)[index]), when)
        self.hand_over(place, zz, when)

    def from_across(self, index, zz):
        ref = self.block(3 + index, zz)
        self.flat(ref, ref, 2 + index, zz, (self.at.next_y, self.at.next_x)[index]).wait_recv()
        self.hand_over(3 + index, zz)

    def line(self, source, place, zz, up, when):
        at = self.at
        ref = self.block(place, zz)
        copy = remote(
            ref if source is None else source,
            ref,
            self.line_sent.at[int(up), place, zz],
            self.line_arrived.at[place, zz],
            at.above if up else at.below,
        )
        self.sent.go(copy, (at.has_above if up else at.has_below) & when)

    def both_ways(self, place, source=None):
        for up in (True, False):
            self.line(source, place, self.at.z, up, True)

    def from_line(self, step, up, place, onward):
        at = self.at
        zz = at.z - step if up else at.z + step
        valid = zz >= 0 if up else zz < at.nz
        zz = jnp.clip(zz, 0, at.nz - 1)
        ref = self.block(place, zz)
        copy = remote(
            ref,
            ref,
            self.line_sent.at[int(up), place, zz],
            self.line_arrived.at[place, zz],
            at.below if up else at.above,
        )
        pl.when(valid)(copy.wait_recv)
        self.line(None, place, zz, up, valid)
        if onward:
            self.sides(ref, zz, valid)
        self.hand_over(place, zz, valid)

    def hand_over(self, place, zz, when=None, source=None):
        ref = self.block(place, zz)
        copy = remote(
            ref if source is None else source,
            ref,
            self.core_sent.at[place, zz],
            self.core_arrived.at[place, zz],
            self.at.core,
        )
        self.sent.go(copy, when)

    def finish(self):
        for zz in range(self.at.nz):
            for place in range(5):
                ref = self.block(place, zz, 1 - self.at.me)
                remote(
                    ref,
                    ref,
                    self.core_sent.at[place, zz],
                    self.core_arrived.at[place, zz],
                    self.at.core,
                ).wait_recv()


    def begin_line(self):
        self.both_ways(0, self.source)

    def begin_sides(self):
        self.sides(self.source, self.at.z)
        self.hand_over(0, self.at.z, source=self.source)

    def sides_at(self, step):
        at = self.at
        if step == 0:
            for index in range(2):
                self.from_side(index, at.z)
            return
        for zz, valid in ((at.z - step, at.z >= step), (at.z + step, at.z + step < at.nz)):
            for index in range(2):
                self.from_side(index, jnp.clip(zz, 0, at.nz - 1), valid)

    def corners(self):
        for zz in range(self.at.nz):
            for index in range(2):
                self.from_across(index, zz)


    def plane(self, place):
        z = self.at.z
        if place < 3:
            self.from_side(place - 1, z)
        else:
            self.from_across(place - 3, z)
        self.both_ways(place)


def begin_kernel(
    nz,
    own_ref,
    partner_ref,
    starts_ref,
    seq_ref,
    w_ref,
    wa_ref,
    wb_ref,
    x_ref,
    cot_ref,
    ck_ref,
    cv_ref,
    first_ref,
    a_ref,
    b_ref,
    xs_ref,
    cots_ref,
    qkv_ref,
    att_out,
    kmem_out,
    vmem_out,
    lse_ref,
    cos_ref,
    sin_ref,
    all_ref,
    xv_ref,
    n1_ref,
    y_ref,
    cotbuf,
    near_ref,
    far_ref,
    stage_ref,
    kmem_ref,
    vmem_ref,
    att_ref,
    acc_ref,
    shift_ref,
    total_ref,
    loaded,
    stored,
    csent,
    carrived,
    far_sent,
    far_arrived,
    far_csent,
    far_carrived,
    *refs,
):
    at = Place(nz)
    me, x, y, z = at.me, at.x, at.y, at.z
    keys = ck_ref.shape[1]
    width = w_ref.shape[1]
    tokens, model = n1_ref.shape
    half = model // 2
    sent = Sent()
    n = Spread.BUFFERS
    first = Spread(at, sent, w_ref, all_ref, refs[:n])
    late = Spread(at, sent, wa_ref, a_ref, refs[n : 2 * n])
    wide = Spread(at, sent, wb_ref, b_ref, refs[2 * n :])
    span = [pl.ds(0, keys), pl.ds(keys, keys)]
    caches = (ck_ref, cv_ref)

    def local(source, target, semaphore):
        return pltpu.make_async_copy(source, target, semaphore)

    loads = [
        local(source, target, loaded.at[i])
        for i, (source, target) in enumerate(
            (
                (w_ref, first.own()),
                (x_ref.at[me], xv_ref.at[me]),
                (cot_ref.at[me], cotbuf),
                (ck_ref.at[me], near_ref.at[me, span[0]]),
                (cv_ref.at[me], near_ref.at[me, span[1]]),
                (wa_ref, late.own()),
                (wb_ref, wide.own()),
            )
        )
    ]
    stores = [
        local(source, target, stored.at[i])
        for i, (source, target) in enumerate(
            (
                (cotbuf, cots_ref.at[me]),
                (xv_ref, xs_ref),
                (all_ref, first_ref),
                (y_ref, qkv_ref),
                (kmem_ref, kmem_out),
                (vmem_ref, vmem_out),
                (att_ref, att_out),
            )
        )
    ]
    for copy in loads:
        copy.start()
    at.barrier([at.core, at.next_x, at.next_y, at.above, at.below])
    exchange = [
        remote(source, target, csent.at[i], carrived.at[i], at.core)
        for i, (source, target) in enumerate(
            (
                (x_ref.at[1 - me], xv_ref.at[me]),
                (ck_ref.at[1 - me], near_ref.at[me, span[0]]),
                (cv_ref.at[1 - me], near_ref.at[me, span[1]]),
                (cot_ref.at[1 - me], cots_ref.at[me]),
            )
        )
    ]

    def landing(source, turn, kv):
        return far_ref.at[source, me, span[kv]] if turn == 0 else stage_ref.at[source, kv]

    def cache_copy(line, turn, kv):
        index = (line, turn * 2 + kv)
        return remote(
            caches[kv].at[me if turn == 0 else 1 - me],
            landing(line, turn, kv),
            far_sent.at[index],
            far_arrived.at[index],
            (at.next_x, at.next_y)[line],
        )

    def corner_copy(turn, kv):
        source, device = (0, at.next_y) if turn == 0 else (1, at.next_x)
        index = (2, turn * 2 + kv)
        return remote(
            landing(source, turn, kv), landing(2, turn, kv), far_sent.at[index], far_arrived.at[index], device
        )

    def hand_over(source, kv):
        return remote(
            stage_ref.at[source, kv],
            far_ref.at[source, me, span[kv]],
            far_csent.at[source, kv],
            far_carrived.at[source, kv],
            at.core,
        )

    def from_lines(spread, step, places, onward):
        for place in places:
            for up in (True, False):
                spread.from_line(step, up, place, onward)


    first.begin_line()
    first.begin_sides()
    wide.begin_line()
    wide.begin_sides()
    sent.go(exchange[0])

    place_in = lax.broadcasted_iota(jnp.int32, (tokens, HEAD_DIM), 0).astype(F32)
    lane = lax.broadcasted_iota(jnp.int32, (1, HEAD_DIM), 1)
    turns = lax.rem(lane, HEAD_DIM // 2).astype(F32) * (-2.0 * math.log(10000.0) / HEAD_DIM)
    angles = place_in * jnp.exp(turns)
    cos_ref[...] = jnp.cos(angles)
    sin_ref[...] = jnp.where(lane < HEAD_DIM // 2, -1.0, 1.0) * jnp.sin(angles)

    from_lines(first, 1, (0,), True)
    wide.plane(1)
    wide.plane(2)
    first.sides_at(0)
    from_lines(first, 2, (0,), True)
    wide.plane(3)
    wide.plane(4)
    first.sides_at(1)
    from_lines(first, 3, (0,), True)
    first.sides_at(2)
    for turn in range(2):
        for kv in range(2):
            sent.go(cache_copy(0, turn, kv))
            sent.go(cache_copy(1, 1 - turn, kv))
    for copy in exchange[1:]:
        sent.go(copy)
    late.begin_line()
    late.begin_sides()
    first.sides_at(3)
    from_lines(wide, 1, range(3), False)
    loads[2].wait()
    stores[0].start()
    loads[1].wait()
    exchange[0].wait_recv()
    stores[1].start()
    first.corners()
    loads[0].wait()
    first.finish()
    stores[2].start()

    gains = all_ref[:, :, :, 0, :, pl.ds(width - LANES, LANES)].reshape(model, LANES).astype(F32)
    gain = jnp.transpose(gains)[0:1, :]

    def norm(rows):
        normal, _ = normal_of(features(xv_ref, rows).astype(F32))
        n1_ref[rows, :] = (normal * gain).astype(BF)

    chunks(tokens, norm)

    def project(i, carry):
        m, h = i // 2, i % 2
        lanes = pl.ds(pl.multiple_of(m * half, half), half)
        value = nn(n1_ref[...], all_ref[:, :, :, h, :, lanes].reshape(model, half))
        for head in range(half // HEAD_DIM):
            lanes = slice(head * HEAD_DIM, (head + 1) * HEAD_DIM)
            u = value[:, lanes]
            turned = u * cos_ref[...] + pltpu.roll(u, HEAD_DIM // 2, 1) * sin_ref[...]
            y_ref[m, h, :, lanes] = jnp.where(m < 2, turned, u).astype(BF)
        return carry

    lax.fori_loop(0, 6, project, 0)
    stores[3].start()


    for kv in range(2):
        cache_copy(0, 0, kv).wait_recv()
        sent.go(corner_copy(0, kv))
        cache_copy(1, 1, kv).wait_recv()
        sent.go(corner_copy(1, kv))
        sent.go(hand_over(1, kv))
    for copy in loads[3:5]:
        copy.wait()
    for copy in exchange[1:3]:
        copy.wait_recv()

    def choose(index_ref, first_row):
        for b in range(QBLKS):
            for j in range(OWN_K):
                index = index_ref[me, b, j]
                rows = pl.ds(first_row + j * MEM_BLK, MEM_BLK)
                for h in range(2):
                    for offset, ref in ((0, kmem_ref), (keys, vmem_ref)):
                        block = near_ref[h, pl.ds(offset, MEM_BLK), :]
                        for c in range(1, keys // MEM_BLK):
                            other = near_ref[h, pl.ds(offset + c * MEM_BLK, MEM_BLK), :]
                            block = jnp.where(index == c, other, block)
                        ref[h, b, rows, :] = block

    choose(own_ref, 0)
    heads = half // HEAD_DIM
    near_rows = slice(0, OWN_K * MEM_BLK)
    far_rows = slice(OWN_K * MEM_BLK, (OWN_K + PART_K) * MEM_BLK)

    def place(i):
        h, column = i // heads, i % heads
        return h, column, pl.ds(pl.multiple_of(column * HEAD_DIM, HEAD_DIM), HEAD_DIM)

    def without_partner(i, carry):
        h, column, lanes = place(i)

        def store(rows, shift, total, acc):
            acc_ref[i, :, rows] = acc
            shift_ref[i, :, rows] = shift
            total_ref[i, :, rows] = total

        attend_head(
            lambda m, rows: y_ref[m, h, rows, lanes],
            lambda b: (kmem_ref[h, b, near_rows, lanes], vmem_ref[h, b, near_rows, lanes]),
            [starts_ref[me, b] for b in range(QBLKS)],
            store,
        )
        return carry

    def with_partner(i, carry):
        h, column, lanes = place(i)
        for b in range(QBLKS):
            rows = pl.ds(b * QROWS, QROWS)
            shift, total, acc = attend_rows(
                [(kmem_ref[h, b, far_rows, lanes], vmem_ref[h, b, far_rows, lanes], None)],
                y_ref[0, h, rows, lanes],
            )
            before = shift_ref[i, :, rows]
            top = jnp.maximum(shift, before)
            now, then = jnp.exp2(shift - top), jnp.exp2(before - top)
            total = total * now + total_ref[i, :, rows] * then
            acc = acc * now + acc_ref[i, :, rows] * then
            att_ref[h, rows, lanes] = jnp.transpose(acc / total).astype(BF)
            lse_ref[h, column, :, rows] = top + jnp.log2(total)
        return carry

    lax.fori_loop(0, heads, without_partner, 0)
    from_lines(wide, 1, range(3, 5), False)
    from_lines(late, 1, (0,), True)
    from_lines(wide, 2, range(3), False)
    for kv in range(2):
        cache_copy(0, 1, kv).wait_recv()
        sent.go(hand_over(0, kv))
        cache_copy(1, 0, kv).wait_recv()
    lax.fori_loop(heads, 2 * heads, without_partner, 0)
    from_lines(wide, 2, range(3, 5), False)
    from_lines(late, 2, (0,), True)
    from_lines(late, 3, (0,), True)
    late.sides_at(0)
    for kv in range(2):
        corner_copy(1, kv).wait_recv()
        sent.go(hand_over(2, kv))
        corner_copy(0, kv).wait_recv()
    for source in range(3):
        for kv in range(2):
            remote(
                stage_ref.at[source, kv],
                far_ref.at[source, 1 - me, span[kv]],
                far_csent.at[source, kv],
                far_carrived.at[source, kv],
                at.core,
            ).wait_recv()
    source = seq_ref[me]
    across = (1 - y) * 2 + 1 - x
    near_y = (1 - y) * 2 + x
    at_most = SEQ_DEV * nz

    def comes_from(place):
        return (source >= place * at_most) & (source < (place + 1) * at_most)

    def take(i, carry):
        rows = pl.ds(pl.multiple_of(i * MEM_BLK, MEM_BLK), MEM_BLK)
        for h in range(2):
            block = jnp.where(comes_from(near_y), far_ref[1, h, rows, :], far_ref[0, h, rows, :])
            near_ref[h, rows, :] = jnp.where(comes_from(across), far_ref[2, h, rows, :], block)
        return carry

    lax.fori_loop(0, 2 * keys // MEM_BLK, take, 0)
    choose(partner_ref, OWN_K * MEM_BLK)
    stores[4].start()
    stores[5].start()
    lax.fori_loop(0, 2 * heads, with_partner, 0)
    stores[6].start()
    late.sides_at(1)
    from_lines(wide, 3, range(5), False)
    late.sides_at(2)
    late.sides_at(3)

    late.corners()
    late.finish()
    wide.finish()
    exchange[3].wait_recv()
    for copy in loads[5:]:
        copy.wait()
    for copy in stores:
        copy.wait()
    sent.wait()


def begin(own, partner, starts, seq, w, wa, wb, x, cot, cache_keys, cache_values, nz):
    dma = pltpu.SemaphoreType.DMA
    _, tokens, half = x.shape
    keys = cache_keys.shape[1]
    full = jax.ShapeDtypeStruct((2, tokens, half), BF)
    gathered = lambda w: (2, 2, nz, 2) + w.shape
    whole_array = lambda w: jax.ShapeDtypeStruct(gathered(w), BF)
    vmem = pl.BlockSpec(memory_space=pltpu.VMEM)
    table = jax.ShapeDtypeStruct((tokens, HEAD_DIM), F32)
    heads = 2 * half // HEAD_DIM
    memory = (2, QBLKS, (OWN_K + PART_K) * MEM_BLK, half)
    return pl.pallas_call(
        functools.partial(begin_kernel, nz),
        in_specs=[pl.BlockSpec(memory_space=pltpu.SMEM)] * 4 + [HBM] * 7,
        out_specs=[HBM] * 9 + [vmem] * 3,
        out_shape=[
            whole_array(w),
            whole_array(wa),
            whole_array(wb),
            full,
            full,
            jax.ShapeDtypeStruct((3, 2, tokens, half), BF),
            full,
            jax.ShapeDtypeStruct(memory, BF),
            jax.ShapeDtypeStruct(memory, BF),
            jax.ShapeDtypeStruct((2, half // HEAD_DIM, 1, tokens), F32),
            table,
            table,
        ],
        scratch_shapes=[
            pltpu.VMEM(gathered(w), BF),
            pltpu.VMEM((2, tokens, half), BF),
            pltpu.VMEM((tokens, 2 * half), BF),
            pltpu.VMEM((3, 2, tokens, half), BF),
            pltpu.VMEM((tokens, half), BF),
            pltpu.VMEM((2, 2 * keys, half), BF),
            pltpu.VMEM((3, 2, 2 * keys, half), BF),
            pltpu.VMEM((3, 2, keys, half), BF),
            pltpu.VMEM(memory, BF),
            pltpu.VMEM(memory, BF),
            pltpu.VMEM((2, tokens, half), BF),
            pltpu.VMEM((heads, HEAD_DIM, tokens), F32),
            pltpu.VMEM((heads, 1, tokens), F32),
            pltpu.VMEM((heads, 1, tokens), F32),
            dma((7,)),
            dma((7,)),
            dma((4,)),
            dma((4,)),
            dma((3, 4)),
            dma((3, 4)),
            dma((3, 2)),
            dma((3, 2)),
        ]
        + Spread.scratch(nz) * 3,
        compiler_params=comm_params(0),
        name="begin",
    )(own, partner, starts, seq, w, wa, wb, x, cot, cache_keys, cache_values)


class Sums:
    BUFFERS = 10

    @staticmethod
    def last(halved):
        return 4 if halved else 3

    @staticmethod
    def scratch(parts, rows, tiles, nz, halved, taken=False):
        dma = pltpu.SemaphoreType.DMA
        slab = rows // 4
        pairs = pltpu.VMEM((1, 1, 16, LANES) if taken else (2, parts, rows, LANES), BF)
        return [
            pairs,
            pairs,
            pltpu.VMEM((tiles, parts, rows, LANES), BF),
            pltpu.VMEM((tiles, 2, parts, slab // 2, LANES) if halved else (tiles, 1, parts, slab, LANES), BF),
            pltpu.VMEM((tiles, 2, parts, slab, LANES), BF),
            pltpu.VMEM((tiles, nz - 1, parts, slab // nz, LANES), BF),
            dma((tiles, 5)),
            dma((tiles, 5)),
            dma((tiles, nz - 1)),
            dma((tiles, nz - 1)),
        ]

    def __init__(self, at, halved, refs, left=0):
        (
            self.mine,
            self.other,
            self.total,
            self.diag,
            self.side,
            self.hop,
            self.sent,
            self.arrived,
            self.hop_sent,
            self.hop_arrived,
        ) = refs
        self.at, self.halved = at, halved
        self.tiles, _, self.rows, _ = self.total.shape
        self.left, self.early = left, self.tiles - left
        self.slab = self.rows // 4
        self.block = self.slab // at.nz

    def span(self, y, x, first=0, size=None):
        start = pl.multiple_of((y * 2 + x) * self.slab + first, self.block)
        return pl.ds(start, self.slab if size is None else size)

    def copy(self, j, span, target, index, device):
        return remote(
            self.total.at[j, :, span], target, self.sent.at[j, index], self.arrived.at[j, index], device
        )

    def core_copy(self, j):
        return remote(
            self.other.at[j % 2],
            self.total.at[j],
            self.sent.at[j, 0],
            self.arrived.at[j, 0],
            self.at.core,
        )

    def diag_copies(self, j):
        at, part = self.at, self.slab // 2
        y, x = 1 - at.y, 1 - at.x
        if not self.halved:
            return [self.copy(j, self.span(y, x), self.diag.at[j, 0], 1, at.corner())]
        return [
            self.copy(j, self.span(y, x, i * part, part), self.diag.at[j, i], 1 + i, device)
            for i, device in enumerate((at.next_x, at.next_y))
        ]

    def side_copies(self, j):
        at = self.at
        return [
            self.copy(j, self.span(at.y, 1 - at.x), self.side.at[j, 0], 3, at.next_x),
            self.copy(j, self.span(1 - at.y, at.x), self.side.at[j, 1], 4, at.next_y),
        ]

    def hop_copies(self, j):
        at = self.at
        copies = []
        for by in range(1, at.nz):
            device = at.level(by)
            copies.append(
                remote(
                    self.total.at[j, :, self.span(at.y, at.x, device[2] * self.block, self.block)],
                    self.hop.at[j, by - 1],
                    self.hop_sent.at[j, by - 1],
                    self.hop_arrived.at[j, by - 1],
                    device,
                )
            )
        return copies

    def add(self, j, span, *values):
        total = self.total[j, :, span, :].astype(F32)
        for value in values:
            total = total + value.astype(F32)
        self.total[j, :, span, :] = total.astype(BF)

    def start(self, j):
        self.core_copy(j).start()

    def after_core(self, j):
        self.core_copy(j).wait()

        def body(rows):
            self.add(j, rows, self.mine[j % 2, :, rows, :])

        chunks(self.rows, body)

    def begin(self, j):
        for copy in self.diag_copies(j):
            copy.start()
        if not self.halved:
            for copy in self.side_copies(j):
                copy.start()

    def after_diag(self, j):
        at, part = self.at, self.slab // 2
        for copy in self.diag_copies(j):
            copy.wait()
        self.add(j, self.span(1 - at.y, at.x, 0, part), self.diag[j, 0])
        self.add(j, self.span(at.y, 1 - at.x, part, part), self.diag[j, 1])
        for copy in self.side_copies(j):
            copy.start()

    def after_side(self, j):
        at = self.at
        for copy in self.side_copies(j):
            copy.wait()
        values = [self.side[j, 0], self.side[j, 1]]
        if not self.halved:
            for copy in self.diag_copies(j):
                copy.wait()
            values.append(self.diag[j, 0])
        self.add(j, self.span(at.y, at.x), *values)
        for copy in self.hop_copies(j):
            copy.start()

    def result(self, j):
        at = self.at
        for copy in self.hop_copies(j):
            copy.wait()
        value = self.total[j, :, self.span(at.y, at.x, at.z * self.block, self.block), :].astype(F32)
        for by in range(at.nz - 1):
            value = value + self.hop[j, by].astype(F32)
        return value

    def advance(self, step, store, leave=None, taken=False):
        def on(behind, body, first, last):
            j = step - behind
            pl.when((j >= first) & (j < last))(lambda: body(jnp.clip(j, first, last - 1)))

        def summed(j):
            self.after_core(j)
            self.begin(j)

        def left(j):
            self.after_core(j)
            leave(self.total[j])

        if not taken:
            on(1, summed, 0, self.early)
        if self.left:
            on(1, left, self.early, self.tiles)
        if self.halved:
            on(2, self.after_diag, 0, self.early)
        on(self.last(self.halved) - 1, self.after_side, 0, self.early)
        on(self.last(self.halved), lambda j: store(self.result(j)), 0, self.early)


class Norms:
    BUFFERS = 7

    @staticmethod
    def scratch(model, nz):
        dma = pltpu.SemaphoreType.DMA
        return [
            pltpu.VMEM((4, 8, model // 4), F32),
            pltpu.VMEM((8, 8, model // 4), F32),
            pltpu.VMEM((nz, 8, LANES), F32),
            dma((7,)),
            dma((7,)),
            dma((nz - 1,)),
            dma((nz - 1,)),
        ]

    def __init__(self, at, refs):
        self.at = at
        self.own, self.parts, self.level, self.sent, self.arrived, self.hop_sent, self.hop_arrived = refs

    def plane_copies(self):
        at = self.at
        me = at.y * 4 + at.x * 2 + at.me
        return [
            remote(self.own.at[device[0]], self.parts.at[me], self.sent.at[i], self.arrived.at[i], device)
            for i, device in enumerate(at.plane())
        ]

    def hop_copies(self):
        at = self.at
        me = at.y * 4 + at.x * 2 + at.me
        copies = []
        for by in range(1, at.nz):
            device = at.level(by)
            lanes = pl.ds(pl.multiple_of(device[2] // 2 * LANES, LANES), LANES)
            copies.append(
                remote(
                    self.own.at[0, :, lanes],
                    self.level.at[at.z],
                    self.hop_sent.at[by - 1],
                    self.hop_arrived.at[by - 1],
                    device,
                )
            )
        return copies

    def start(self, rows):
        at = self.at
        width = self.own.shape[2]
        for d in range(4):
            self.own[d] = rows[:, d * width : (d + 1) * width]
        self.parts[at.y * 4 + at.x * 2 + at.me] = self.own[at.y * 2 + at.x]
        for copy in self.plane_copies():
            copy.start()

    def after_plane(self):
        at = self.at
        for copy in self.plane_copies():
            copy.wait()
        total = self.parts[0]
        for i in range(1, 8):
            total = total + self.parts[i]
        self.own[0] = total
        lanes = pl.ds(pl.multiple_of(at.z // 2 * LANES, LANES), LANES)
        self.level[at.z] = self.own[0, :, lanes]
        for copy in self.hop_copies():
            copy.start()

    def result(self):
        for copy in self.hop_copies():
            copy.wait()
        total = self.level[0]
        for i in range(1, self.at.nz):
            total = total + self.level[i]
        return total


class Unsummed:
    class Tile:
        def __init__(self, ref):
            self.ref = ref

        def __setitem__(self, index, value):
            self.ref[index[1:]] = value

    def __init__(self, mine, other):
        self.mine, self.other = Unsummed.Tile(mine), Unsummed.Tile(other)

    def start(self, j):
        pass

    def advance(self, step, store, leave=None):
        pass


def features(ref, rows):
    return jnp.concatenate([ref[0, rows, :], ref[1, rows, :]], axis=1)


def pair(ref, model):
    return jnp.concatenate(
        [ref[:, 0].reshape(model, LANES), ref[:, 1].reshape(model, LANES)], axis=1
    )


def normal_of(x):
    inverse = lax.rsqrt(jnp.mean(x * x, axis=1, keepdims=True) + EPSILON)
    return x * inverse, inverse


def norm_back(normal, inverse, gain, grad):
    scaled = grad * gain
    return inverse * (scaled - normal * jnp.mean(scaled * normal, axis=1, keepdims=True))


def qkv_kernel(x_ref, gain_ref, w_ref, cos_ref, sin_ref, out_ref, n1_ref):
    part = pl.program_id(0)
    tokens, model = n1_ref.shape

    @pl.when((part == 0) & (pl.program_id(1) == 0))
    def _():
        def norm(rows):
            normal, _ = normal_of(features(x_ref, rows).astype(F32))
            n1_ref[rows, :] = (normal * gain_ref[...]).astype(BF)

        chunks(tokens, norm)

    def project(rows):
        y = nn(n1_ref[rows, :], w_ref[...].reshape(model, -1))
        cosine, sine = cos_ref[rows, :], sin_ref[rows, :]
        for h in range(y.shape[1] // HEAD_DIM):
            lanes = slice(h * HEAD_DIM, (h + 1) * HEAD_DIM)
            u = y[:, lanes]
            turned = u * cosine + pltpu.roll(u, HEAD_DIM // 2, 1) * sine
            out_ref[rows, lanes] = jnp.where(part < 2, turned, u).astype(BF)

    chunks(tokens, project, tokens)


def project_qkv(x, gain, gathered, cosine, sine):
    halves, tokens, half = x.shape
    groups, _, rows, _ = gathered.shape
    return pl.pallas_call(
        qkv_kernel,
        grid=(3, halves),
        in_specs=[
            whole(x.shape),
            whole(gain.shape),
            pl.BlockSpec((groups, None, rows, half), lambda m, h: (0, h, 0, m)),
            whole(cosine.shape),
            whole(sine.shape),
        ],
        out_specs=pl.BlockSpec((None, None, tokens, half), lambda m, h: (m, h, 0, 0)),
        out_shape=jax.ShapeDtypeStruct((3, halves, tokens, half), BF),
        scratch_shapes=[pltpu.VMEM((tokens, halves * half), BF)],
        compiler_params=params(),
        name="project_qkv",
    )(x, gain, gathered, cosine, sine)


def fill_memory(idx_ref, near_ref, far_ref, offset, mem_ref):
    for b in range(QBLKS):
        for j in range(OWN_K + PART_K):
            ref, at = (near_ref, b * OWN_K + j) if j < OWN_K else (far_ref, QBLKS * OWN_K + b * PART_K + j - OWN_K)
            start = pl.multiple_of(idx_ref[at] * MEM_BLK, MEM_BLK) + offset
            mem_ref[b, j * MEM_BLK : (j + 1) * MEM_BLK, :] = ref[pl.ds(start, MEM_BLK), :]


def masked(scores, start, first):
    keys, queries = scores.shape
    at = first + lax.broadcasted_iota(jnp.int32, (1, queries), 1)
    limit = jnp.where((at >= start) & (at < start + PIC), start + PIC - 1, at)
    key = lax.broadcasted_iota(jnp.int32, (keys, queries), 0)
    return jnp.where(key <= limit, scores, NEG)


SCALE = LOG2E / math.sqrt(HEAD_DIM)


def attend_rows(parts, q):
    scores = []
    for keys, values, mask in parts:
        s = nt(keys, q)
        scores.append((s if mask is None else masked(s, *mask), values))
    top = functools.reduce(jnp.maximum, [jnp.max(s, axis=0, keepdims=True) for s, _ in scores])
    shift = top * SCALE
    total = jnp.zeros_like(top)
    acc = jnp.zeros((HEAD_DIM, q.shape[0]), F32)
    for s, values in scores:
        e = jnp.exp2(s * SCALE - shift)
        total = total + jnp.sum(e, axis=0, keepdims=True)
        acc = acc + tn(values, e.astype(BF))
    return shift, total, acc


def attend_head(part, memory, starts, store):
    for b in range(QBLKS):
        start = starts[b] - b * QROWS

        def body(i, carry, b=b, start=start):
            first = pl.multiple_of(i * CHUNK, CHUNK)
            rows = pl.ds(pl.multiple_of(b * QROWS + first, CHUNK), CHUNK)
            parts = []
            for n in range(b + 1):
                span = slice(n * QROWS, (n + 1) * QROWS)
                parts.append((part(1, span), part(2, span), (start, first) if n == b else None))
            parts.append(memory(b) + (None,))
            store(rows, *attend_rows(parts, part(0, rows)))
            return carry

        lax.fori_loop(0, QROWS // CHUNK, body, 0)


def attend_kernel(
    idx_ref, q_ref, k_ref, v_ref, near_ref, far_ref, out_ref, lse_ref, kmem_ref, vmem_ref
):
    keys = near_ref.shape[0] // 2
    fill_memory(idx_ref, near_ref, far_ref, 0, kmem_ref)
    fill_memory(idx_ref, near_ref, far_ref, keys, vmem_ref)
    refs = (q_ref, k_ref, v_ref)

    def store(rows, shift, total, acc):
        out_ref[rows, :] = jnp.transpose(acc / total).astype(BF)
        lse_ref[:, rows] = shift + jnp.log2(total)

    attend_head(
        lambda m, rows: refs[m][rows, :],
        lambda b: (kmem_ref[b], vmem_ref[b]),
        [idx_ref[QBLKS * (OWN_K + PART_K) + b] for b in range(QBLKS)],
        store,
    )


def attend(idx, qkv, near, far):
    _, halves, tokens, half = qkv.shape
    here = half // HEAD_DIM
    cached = near.shape[1]
    memory = (OWN_K + PART_K) * MEM_BLK
    column = lambda m: pl.BlockSpec(
        (None, None, tokens, HEAD_DIM), lambda h, idx: (m, h // here, 0, h % here)
    )
    cache = pl.BlockSpec((None, cached, HEAD_DIM), lambda h, idx: (h // here, 0, h % here))
    which = QBLKS * (OWN_K + PART_K) + QBLKS
    partner = pl.BlockSpec(
        (None, None, cached, HEAD_DIM), lambda h, idx: (idx[which], h // here, 0, h % here)
    )
    chosen = pl.BlockSpec((None, QBLKS, memory, HEAD_DIM), lambda h, idx: (h // here, 0, 0, h % here))
    chosen_shape = jax.ShapeDtypeStruct((halves, QBLKS, memory, half), BF)
    return pl.pallas_call(
        attend_kernel,
        grid_spec=pltpu.PrefetchScalarGridSpec(
            num_scalar_prefetch=1,
            grid=(halves * here,),
            in_specs=[column(0), column(1), column(2), cache, partner],
            out_specs=[
                pl.BlockSpec((None, tokens, HEAD_DIM), lambda h, idx: (h // here, 0, h % here)),
                pl.BlockSpec((None, None, 1, tokens), lambda h, idx: (h // here, h % here, 0, 0)),
                chosen,
                chosen,
            ],
        ),
        out_shape=[
            jax.ShapeDtypeStruct((halves, tokens, half), BF),
            jax.ShapeDtypeStruct((halves, here, 1, tokens), F32),
            chosen_shape,
            chosen_shape,
        ],
        compiler_params=params(),
        name="attend",
    )(idx, qkv, qkv, qkv, near, far)


def split_store(me, value, mine_ref, other_ref, index):
    low, high = value[:, :LANES], value[:, LANES:]
    mine_ref[index] = jnp.where(me == 0, low, high)
    other_ref[index] = jnp.where(me == 0, high, low)


def send_halves(at, buffer, out_ref, local, sent, arrived):
    tokens = buffer.shape[1]
    rows = pl.ds(pl.multiple_of(at.me * tokens, tokens), tokens)
    return (
        pltpu.make_async_copy(buffer.at[at.me], out_ref.at[rows], local),
        remote(buffer.at[1 - at.me], out_ref.at[rows], sent, arrived, at.core),
    )


def feed_kernel(
    nz,
    steps,
    x_ref,
    att_ref,
    cot_ref,
    gain_ref,
    wo_ref,
    wg_ref,
    wu_ref,
    wd_ref,
    ghid_ref,
    gn2_ref,
    *refs,
):
    if nz:
        out_ref, grad_ref, late_ref, *refs = refs
    else:
        result_ref, mine_ref, other_ref, *refs = refs
    hid_ref, n2_ref, n2t_ref, cott_ref, acc_ref, dn_ref, a_ref, dg_ref, du_ref, *refs = refs
    tokens, model = hid_ref.shape
    half = model // 2
    step = pl.program_id(0)
    me = lax.axis_index("row")
    copies = []
    if nz:
        at = Place(nz)
        result_ref, local, sent, arrived, *refs = refs
        sums = Sums(at, True, refs, LATE)
        copies = send_halves(at, result_ref, out_ref, local.at[0], sent.at[0], arrived.at[0])
    else:
        sums = Unsummed(mine_ref, other_ref)

    def wo_half(h):
        return wo_ref[:, h].reshape(model, half)

    @pl.when(step == 0)
    def _():
        if nz:
            at.barrier([at.core, at.next_x, at.next_y] + at.levels())

        def start(rows):
            hidden = features(x_ref, rows).astype(F32)
            for h in range(2):
                hidden = hidden + nt(att_ref[h, rows, :], wo_half(h))
            hid_ref[rows, :] = hidden
            normal, _ = normal_of(hidden)
            n2_ref[rows, :] = (normal * gain_ref[...]).astype(BF)
            n2t_ref[:, rows] = jnp.transpose(n2_ref[rows, :])
            cott_ref[:, rows] = jnp.transpose(features(cot_ref, rows))
            acc_ref[rows, :] = jnp.zeros((CHUNK, model), F32)
            dn_ref[rows, :] = jnp.zeros((CHUNK, model), F32)

        chunks(tokens, start)

    def store(value):
        grad_ref[...] = value

    def leave(value):
        late_ref[...] = value

    def forward_back(rows):
        n2 = n2_ref[rows, :]
        gating = nn(n2, pair(wg_ref, model))
        upward = nn(n2, pair(wu_ref, model))
        gactive = nn(features(cot_ref, rows), pair(wd_ref, model))
        sigmoid = 1.0 / (1.0 + jnp.exp(-gating))
        silu = gating * sigmoid
        a_ref[rows, :] = (silu * upward).astype(BF)
        dg_ref[rows, :] = (gactive * upward * (sigmoid + silu * (1.0 - sigmoid))).astype(BF)
        du_ref[rows, :] = (gactive * silu).astype(BF)
        acc_ref[rows, :] += nt(a_ref[rows, :], pair(wd_ref, model))
        dn_ref[rows, :] += nt(dg_ref[rows, :], pair(wg_ref, model)) + nt(
            du_ref[rows, :], pair(wu_ref, model)
        )

    @pl.when(step < steps)
    def _():
        chunks(tokens, forward_back, tokens)
        slot = step % 2

        def weights(rows):
            n2t = n2t_ref[rows, :]
            for p, value in enumerate(
                (nn(n2t, dg_ref[...]), nn(n2t, du_ref[...]), nn(cott_ref[rows, :], a_ref[...]))
            ):
                split_store(me, value.astype(BF), sums.mine, sums.other, (slot, p, rows))

        chunks(model, weights, model)
        sums.start(step)

    sums.advance(step, store, leave)

    @pl.when(step == (steps if nz else steps - 1))
    def _():
        gn2_ref[...] = jnp.zeros_like(gn2_ref)

        def finish(rows):
            hidden = hid_ref[rows, :]
            result = (hidden + acc_ref[rows, :]).astype(BF)
            result_ref[0, rows, :] = result[:, :half]
            result_ref[1, rows, :] = result[:, half:]
            normal, inverse = normal_of(hidden)
            dn = dn_ref[rows, :]
            gn2_ref[...] += jnp.sum(dn * normal, axis=0, keepdims=True)
            ghid_ref[rows, :] = features(cot_ref, rows).astype(F32) + norm_back(
                normal, inverse, gain_ref[...], dn
            )

        chunks(tokens, finish)
        for copy in copies:
            copy.start()

    if nz:

        @pl.when(step == pl.num_programs(0) - 1)
        def _():
            for copy in copies:
                copy.wait()


def feed(x, attended, cotangent, gain, narrow, wide, units, nz):
    halves, tokens, half = x.shape
    model = halves * half
    groups, _, rows, _ = wide.shape
    steps = units // LANES
    tile = lambda at: pl.BlockSpec(
        (groups, halves, rows, LANES),
        lambda j: (0, 0, 0, at // LANES + jnp.minimum(j, steps - 1)),
    )
    big = lambda dtype: pltpu.VMEM((tokens, model), dtype)
    small = pltpu.VMEM((tokens, 2 * LANES), BF)
    early = steps - LATE
    last = Sums.last(True)
    dma = pltpu.SemaphoreType.DMA((1,))
    if nz:
        out_specs = [
            HBM,
            pl.BlockSpec((3, rows, LANES), lambda j: (0, 0, jnp.clip(j - last, 0, early - 1))),
            pl.BlockSpec((3, model, LANES), lambda j: (0, 0, jnp.clip(j - 1 - early, 0, LATE - 1))),
        ]
        out_shape = [
            jax.ShapeDtypeStruct((halves * tokens, half), BF),
            jax.ShapeDtypeStruct((3, rows, early * LANES), F32),
            jax.ShapeDtypeStruct((3, model, LATE * LANES), BF),
        ]
        more = [pltpu.VMEM(x.shape, BF), dma, dma, dma] + Sums.scratch(3, model, steps, nz, True)
    else:
        grads = pl.BlockSpec((3, model, LANES), lambda j: (0, 0, j))
        out_specs = [once(x.shape), grads, grads]
        grads = jax.ShapeDtypeStruct((3, model, units), BF)
        out_shape = [jax.ShapeDtypeStruct(x.shape, BF), grads, grads]
        more = []
    return pl.pallas_call(
        functools.partial(feed_kernel, nz, steps),
        grid=(max(steps + 1, early + last) if nz else steps,),
        in_specs=[
            once(x.shape),
            once(x.shape),
            once(x.shape),
            once(gain.shape),
            pl.BlockSpec(
                (groups, halves, rows, half),
                lambda j: (0, 0, 0, 0),
                pipeline_mode=pl.Buffered(1),
            ),
            tile(0),
            tile(units),
            tile(half),
        ],
        out_specs=[once((tokens, model)), once(gain.shape)] + out_specs,
        out_shape=[
            jax.ShapeDtypeStruct((tokens, model), F32),
            jax.ShapeDtypeStruct(gain.shape, F32),
        ]
        + out_shape,
        scratch_shapes=[big(F32), big(BF), big(BF), big(BF), big(F32), big(F32), small, small, small]
        + more,
        compiler_params=comm_params(1) if nz else params(),
        name="feed",
    )(x, attended, cotangent, gain, narrow, wide, wide, narrow)


def back_kernel(
    nz,
    steps,
    starts_ref,
    qkv_ref,
    kmem_ref,
    vmem_ref,
    att_ref,
    lse_ref,
    wo_ref,
    wq_ref,
    wk_ref,
    wv_ref,
    x_ref,
    gain_ref,
    ghid_ref,
    gn2_ref,
    cos_ref,
    sin_ref,
    *refs,
):
    if nz:
        left_ref, out_ref, grad_ref, late_ref, norms_ref, *refs = refs
    else:
        result_ref, mine_ref, other_ref, gn1_ref, *refs = refs
    gmix_ref, gmixt_ref, n1t_ref, dn_ref, gatt_ref, g_ref, dk_ref, dv_ref, *refs = refs
    tokens, model = ghid_ref.shape
    half = model // 2
    step = pl.program_id(0)
    me = lax.axis_index("row")
    copies = []
    if nz:
        at = Place(nz)
        result_ref, local, sent, arrived, *refs = refs
        sums = Sums(at, False, refs[: Sums.BUFFERS])
        late = Sums(at, True, refs[Sums.BUFFERS : 2 * Sums.BUFFERS])
        norms = Norms(at, refs[2 * Sums.BUFFERS :])
        copies = send_halves(at, result_ref, out_ref, local.at[0], sent.at[0], arrived.at[0])
    else:
        sums = Unsummed(mine_ref, other_ref)
    scale = LOG2E / math.sqrt(HEAD_DIM)
    plain = 1.0 / math.sqrt(HEAD_DIM)

    @pl.when(step == 0)
    def _():
        if nz:
            at.barrier(at.plane() + at.levels())

        def start(rows):
            normal, _ = normal_of(features(x_ref, rows).astype(F32))
            n1t_ref[:, rows] = jnp.transpose((normal * gain_ref[...]).astype(BF))
            gmix_ref[rows, :] = ghid_ref[rows, :].astype(BF)
            gmixt_ref[:, rows] = jnp.transpose(gmix_ref[rows, :])
            dn_ref[rows, :] = jnp.zeros((CHUNK, model), F32)

        chunks(tokens, start)

    def store(value):
        grad_ref[...] = value

    def store_late(value):
        late_ref[...] = value

    if nz:

        @pl.when(step < LATE)
        def _():
            late.total[step] = left_ref[...]
            late.begin(step)

    def unturn(g, rows):
        return g * cos_ref[rows, :] - pltpu.roll(g, HEAD_DIM // 2, 1) * sin_ref[rows, :]

    def one_head(hh, carry):
        dk_ref[...] = jnp.zeros_like(dk_ref)
        dv_ref[...] = jnp.zeros_like(dv_ref)
        for b in range(QBLKS):
            start = starts_ref[me, b] - b * QROWS

            def body(i, carry, b=b, start=start):
                first = pl.multiple_of(i * CHUNK, CHUNK)
                rows = pl.ds(pl.multiple_of(b * QROWS + first, CHUNK), CHUNK)
                q = qkv_ref[0, hh, rows, :]
                do = gatt_ref[hh, rows, :]
                lse = lse_ref[hh, 0, :, rows]
                dots = jnp.transpose(do.astype(F32) * att_ref[hh, rows, :].astype(F32))
                dot = jnp.sum(dots, axis=0, keepdims=True)
                dq = jnp.zeros((HEAD_DIM, CHUNK), F32)
                for n in range(b + 2):
                    span = slice(n * QROWS, (n + 1) * QROWS)
                    if n <= b:
                        k, v = qkv_ref[1, hh, span, :], qkv_ref[2, hh, span, :]
                    else:
                        k, v = kmem_ref[hh, b], vmem_ref[hh, b]
                    s = nt(k, q)
                    if n == b:
                        s = masked(s, start, first)
                    share = jnp.exp2(s * scale - lse)
                    ds = (share * (nt(v, do) - dot)).astype(BF)
                    if n <= b:
                        dv_ref[span, :] += nn(share.astype(BF), do)
                        dk_ref[span, :] += nn(ds, q)
                    dq = dq + tn(k, ds)
                g_ref[0, hh, rows, :] = unturn(jnp.transpose(dq) * plain, rows).astype(BF)
                return carry

            lax.fori_loop(0, QROWS // CHUNK, body, 0)

        def finish(rows):
            g_ref[1, hh, rows, :] = unturn(dk_ref[rows, :] * plain, rows).astype(BF)
            g_ref[2, hh, rows, :] = dv_ref[rows, :].astype(BF)

        chunks(tokens, finish)
        return carry

    @pl.when(step < steps)
    def _():
        def grad_attended(rows):
            value = nn(gmix_ref[rows, :], pair(wo_ref, model)).astype(BF)
            gatt_ref[0, rows, :] = value[:, :LANES]
            gatt_ref[1, rows, :] = value[:, LANES:]

        chunks(tokens, grad_attended, tokens)

    sums.advance(step, store)
    if nz:
        late.advance(step + 1, store_late, taken=True)

    @pl.when(step < steps)
    def _():
        lax.fori_loop(0, 2, one_head, 0)
        slot = step % 2

        def weights(rows):
            n1t = n1t_ref[rows, :]
            for p in range(3):
                value = nn(n1t, jnp.concatenate([g_ref[p, 0], g_ref[p, 1]], axis=1))
                split_store(me, value.astype(BF), sums.mine, sums.other, (slot, p, rows))
            value = nn(gmixt_ref[rows, :], jnp.concatenate([att_ref[0], att_ref[1]], axis=1))
            split_store(me, value.astype(BF), sums.mine, sums.other, (slot, 3, rows))

        chunks(model, weights, model)
        sums.start(step)

        def inward(rows):
            total = dn_ref[rows, :]
            for p, ref in enumerate((wq_ref, wk_ref, wv_ref)):
                g = jnp.concatenate([g_ref[p, 0, rows, :], g_ref[p, 1, rows, :]], axis=1)
                total = total + nt(g, pair(ref, model))
            dn_ref[rows, :] = total

        chunks(tokens, inward, tokens)

    @pl.when(step == (steps if nz else steps - 1))
    def _():
        def finish(rows, carry):
            normal, inverse = normal_of(features(x_ref, rows).astype(F32))
            dn = dn_ref[rows, :]
            value = (ghid_ref[rows, :] + norm_back(normal, inverse, gain_ref[...], dn)).astype(BF)
            result_ref[0, rows, :] = value[:, :half]
            result_ref[1, rows, :] = value[:, half:]
            return carry + jnp.sum(dn * normal, axis=0, keepdims=True)

        gn1 = lax.fori_loop(
            0,
            tokens // CHUNK,
            lambda i, c: finish(pl.ds(pl.multiple_of(i * CHUNK, CHUNK), CHUNK), c),
            jnp.zeros((1, model), F32),
        )
        for copy in copies:
            copy.start()
        if not nz:
            gn1_ref[...] = gn1
            return
        row = lax.broadcasted_iota(jnp.int32, (8, model), 0)
        norms.start(jnp.where(row == 0, gn1, jnp.where(row == 1, gn2_ref[...], 0.0)))

    if nz:

        @pl.when(step == steps + 1)
        def _():
            norms.after_plane()

        @pl.when(step == steps + 2)
        def _():
            norms_ref[...] = norms.result()

        @pl.when(step == pl.num_programs(0) - 1)
        def _():
            for copy in copies:
                copy.wait()


def back(starts, qkv, kmem, vmem, attended, lse, first, narrow, x, gain, ghid, gn2, cosine, sine, nz, *left):
    halves, tokens, half = x.shape
    model = halves * half
    groups, _, rows, _ = first.shape
    steps = half // HEAD_DIM
    memory = kmem.shape[2]
    now = lambda j: jnp.minimum(j, steps - 1)
    tile = lambda at: pl.BlockSpec(
        (groups, halves, rows, LANES), lambda j: (0, 0, 0, at // LANES + now(j))
    )
    chosen = pl.BlockSpec((halves, QBLKS, memory, HEAD_DIM), lambda j: (0, 0, 0, now(j)))
    big = lambda dtype: pltpu.VMEM((tokens, model), dtype)
    last = Sums.last(False)
    dma = pltpu.SemaphoreType.DMA((1,))
    if nz:
        out_specs = [
            HBM,
            pl.BlockSpec((4, rows, LANES), lambda j: (0, 0, jnp.clip(j - last, 0, steps - 1))),
            pl.BlockSpec((3, rows, LANES), lambda j: (0, 0, jnp.clip(j - last, 0, LATE - 1))),
            once((8, LANES)),
        ]
        out_shape = [
            jax.ShapeDtypeStruct((halves * tokens, half), BF),
            jax.ShapeDtypeStruct((4, rows, half), F32),
            jax.ShapeDtypeStruct((3, rows, LATE * LANES), F32),
            jax.ShapeDtypeStruct((8, LANES), F32),
        ]
        more = (
            [pltpu.VMEM(x.shape, BF), dma, dma, dma]
            + Sums.scratch(4, model, steps, nz, False)
            + Sums.scratch(3, model, LATE, nz, True, True)
            + Norms.scratch(model, nz)
        )
        left_spec = [pl.BlockSpec((3, model, LANES), lambda j: (0, 0, jnp.minimum(j, LATE - 1)))]
    else:
        grads = pl.BlockSpec((4, model, LANES), lambda j: (0, 0, j))
        out_specs = [once(x.shape), grads, grads, once(gain.shape)]
        grads = jax.ShapeDtypeStruct((4, model, half), BF)
        out_shape = [jax.ShapeDtypeStruct(x.shape, BF), grads, grads]
        out_shape.append(jax.ShapeDtypeStruct(gain.shape, F32))
        more = []
        left_spec = []
    return pl.pallas_call(
        functools.partial(back_kernel, nz, steps),
        grid=(steps + last if nz else steps,),
        in_specs=[
            pl.BlockSpec(memory_space=pltpu.SMEM),
            pl.BlockSpec((3, halves, tokens, HEAD_DIM), lambda j: (0, 0, 0, now(j))),
            chosen,
            chosen,
            pl.BlockSpec((halves, tokens, HEAD_DIM), lambda j: (0, 0, now(j))),
            pl.BlockSpec((halves, 1, 1, tokens), lambda j: (0, now(j), 0, 0)),
            tile(0),
            tile(0),
            tile(half),
            tile(2 * half),
            once(x.shape),
            once(gain.shape),
            once(ghid.shape),
            once(gain.shape),
            once(cosine.shape),
            once(sine.shape),
        ]
        + left_spec,
        out_specs=out_specs,
        out_shape=out_shape,
        scratch_shapes=[big(BF), big(BF), big(BF), big(F32)]
        + [
            pltpu.VMEM((halves, tokens, HEAD_DIM), BF),
            pltpu.VMEM((3, halves, tokens, HEAD_DIM), BF),
            pltpu.VMEM((tokens, HEAD_DIM), F32),
            pltpu.VMEM((tokens, HEAD_DIM), F32),
        ]
        + more,
        compiler_params=comm_params(2) if nz else params(),
        name="back",
    )(
        starts,
        qkv,
        kmem,
        vmem,
        attended,
        lse,
        narrow,
        first,
        first,
        first,
        x,
        gain,
        ghid,
        gn2,
        cosine,
        sine,
        *left,
    )


def swap(value):
    return lax.ppermute(value, "row", [(0, 1), (1, 0)])


def in_order(mine, got, me):
    return jnp.where(me == 0, jnp.stack([mine, got]), jnp.stack([got, mine]))


def own_sequence(value, me):
    take = lambda i: lax.dynamic_index_in_dim(value, i, 0, keepdims=False)
    return in_order(take(me), swap(take(1 - me)), me)


def own_features(value, me):
    return own_sequence(value, me).reshape(-1, value.shape[2])


def summed(mine, other):
    total = mine.astype(F32) + swap(other).astype(F32)
    return lax.psum_scatter(total, ("dp", "col"), scatter_dimension=1, tiled=True)


def on_device(
    inputs,
    w_query,
    w_key,
    w_value,
    w_out,
    w_gate,
    w_up,
    w_down,
    norm_one,
    norm_two,
    cache_keys,
    cache_values,
    own_index,
    partner_index,
    picture_start,
    partner_seq,
    cotangent,
):
    me = lax.axis_index("row")
    nz = lax.axis_size("col")
    chips = lax.axis_size("dp") * nz
    half = inputs.shape[1]
    model = 2 * half
    units = w_gate.shape[1]
    rows = w_query.shape[0]

    gains = jnp.pad(jnp.stack([norm_one, norm_two], axis=1), ((0, 0), (0, LANES - 2)))
    first = jnp.concatenate([w_query, w_key, w_value, gains], axis=1)
    narrow = jnp.concatenate([w_out.T, w_down.T], axis=1)
    wide = jnp.concatenate([w_gate, w_up], axis=1)
    tokens = inputs.reshape(SEQ_DEV, SEQ_LEN, half)
    upstream = cotangent.reshape(SEQ_DEV, SEQ_LEN, half)
    lines = lax.axis_size("dp") == 4 and nz * rows == 2 * LANES and rows * 2 == LANES
    if lines:
        first, narrow, wide, x, cot, qkv, attended, kmem, vmem, lse, cosine, sine = begin(
            own_index,
            partner_index,
            picture_start,
            partner_seq,
            first,
            narrow,
            wide,
            tokens,
            upstream,
            cache_keys,
            cache_values,
            nz,
        )
    else:
        spread = lambda w: lax.all_gather(w, ("dp", "col", "row"), axis=0, tiled=True)
        first, narrow, wide = spread(first), spread(narrow), spread(wide)
        x, cot = own_sequence(tokens, me), own_sequence(upstream, me)
        near = own_sequence(jnp.concatenate([cache_keys, cache_values], axis=1), me)
        far = lax.all_gather(near, "dp", axis=0)
        cosine, sine = rotary_tables()
        pick = lambda table: lax.dynamic_index_in_dim(table, me, 0, keepdims=False).reshape(-1)
        source = lax.dynamic_index_in_dim(partner_seq, me, 0) // SEQ_DEV // nz
        idx = jnp.concatenate([pick(own_index), pick(partner_index), pick(picture_start), source])
    first, narrow, wide = [w.reshape(chips, 2, rows, -1) for w in (first, narrow, wide)]
    gains = first[:, 0, :, 3 * half : 3 * half + 2].reshape(model, 2).astype(F32)
    gain_one, gain_two = gains[:, 0].reshape(1, model), gains[:, 1].reshape(1, model)
    if not lines:
        qkv = project_qkv(x, gain_one, first, cosine, sine)
        attended, lse, kmem, vmem = attend(idx, qkv, near, far)
    hops = nz if lines else 0
    ghid, gn2, *fed = feed(
        x, attended, cot, gain_two, narrow, wide, units, hops
    )
    left = fed[2:] if lines else []
    backed = back(
        picture_start,
        qkv,
        kmem,
        vmem,
        attended,
        lse,
        first,
        narrow,
        x,
        gain_one,
        ghid,
        gn2,
        cosine,
        sine,
        hops,
        *left,
    )
    if lines:
        out, feed_grads, _ = fed
        input_grad, model_grads, late, norms = backed
        feed_grads = jnp.concatenate([feed_grads, late], axis=2)
        norms = lax.dynamic_slice_in_dim(norms[:2], lax.axis_index("col") % 2 * rows, rows, 1).T
    else:
        out, input_grad = own_features(fed[0], me), own_features(backed[0], me)
        feed_grads, model_grads = summed(*fed[1:]), summed(*backed[1:3])
        norms = jnp.concatenate([backed[3], gn2], axis=0).T
        norms = lax.psum_scatter(norms, ("dp", "col"), scatter_dimension=0, tiled=True)
        norms = lax.psum(norms, "row")
    return (
        out,
        input_grad,
        model_grads[0],
        model_grads[1],
        model_grads[2],
        model_grads[3].T,
        feed_grads[0],
        feed_grads[1],
        feed_grads[2].T,
        norms[:, 0],
        norms[:, 1],
    )


def solution(mesh):
    tokens = P(("dp", "col"), "row")
    down = P("row", ("dp", "col"))
    gain = P(("dp", "col"))
    cache = P(("dp", "col"), None, "row")
    index = P(("dp", "col"), None, None)
    weights = (tokens, tokens, tokens, down, tokens, tokens, down)
    return jax.shard_map(
        on_device,
        mesh=mesh,
        in_specs=(tokens,)
        + weights
        + (gain, gain, cache, cache, index, index, P(("dp", "col"), None), gain, tokens),
        out_specs=(tokens, tokens) + weights + (gain, gain),
        check_vma=False,
    )
```

```python
import functools
import math

import jax
import jax.numpy as jnp
from jax import lax
from jax.experimental import pallas as pl
from jax.experimental.pallas import tpu as pltpu
from jax.sharding import PartitionSpec as P

HEAD_DIM = 128
SEQ_LEN = 1024
QROWS = 512
PIC = 256
MEM_BLK = 128
OWN_K = 2
PART_K = 2
SEQ_DEV = 2
QBLKS = 2
EPSILON = 1e-05
NEG = -1e30
CHUNK = 256
LANES = 128

BF = jnp.bfloat16
F32 = jnp.float32
LATE = 2
LOG2E = math.log2(math.e)
MESH = pl.DeviceIdType.MESH


def nn(a, b):
    return jnp.dot(a, b, preferred_element_type=F32)


def nt(a, b):
    return lax.dot_general(a, b, (((1,), (1,)), ((), ())), preferred_element_type=F32)


def tn(a, b):
    return lax.dot_general(a, b, (((0,), (0,)), ((), ())), preferred_element_type=F32)


def rotary_tables():
    half = HEAD_DIM // 2
    frequency = 10000.0 ** (-2.0 * jnp.arange(half, dtype=F32) / HEAD_DIM)
    angles = jnp.arange(SEQ_LEN, dtype=jnp.int32).astype(F32)[:, None] * frequency[None, :]
    cosine, sine = jnp.cos(angles), jnp.sin(angles)
    return jnp.concatenate([cosine, cosine], axis=1), jnp.concatenate([-sine, sine], axis=1)


def whole(shape):
    return pl.BlockSpec(shape, lambda *_: (0,) * len(shape))


def once(shape):
    return pl.BlockSpec(shape, lambda *_: (0,) * len(shape), pipeline_mode=pl.Buffered(1))


def params(limit=60):
    return pltpu.CompilerParams(
        vmem_limit_bytes=limit * 1024 * 1024
    )


def chunks(total, body, size=CHUNK):
    def step(i, carry):
        body(pl.ds(pl.multiple_of(i * size, size), size))
        return carry

    if total == size:
        body(pl.ds(0, size))
    else:
        lax.fori_loop(0, total // size, step, 0)


class Place:
    def __init__(self, nz):
        dp, self.me, self.z = lax.axis_index("dp"), lax.axis_index("row"), lax.axis_index("col")
        self.x, self.y, self.nz = dp % 2, dp // 2, nz
        self.core = (dp, 1 - self.me, self.z)
        self.next_x = (self.y * 2 + 1 - self.x, self.me, self.z)
        self.next_y = ((1 - self.y) * 2 + self.x, self.me, self.z)
        self.above = (dp, self.me, lax.rem(self.z + 1, nz))
        self.below = (dp, self.me, lax.rem(self.z + nz - 1, nz))
        self.has_above = self.z < nz - 1
        self.has_below = self.z > 0

    def corner(self):
        return ((1 - self.y) * 2 + 1 - self.x, self.me, self.z)

    def level(self, by):
        return (self.y * 2 + self.x, self.me, lax.rem(self.z + by, self.nz))

    def levels(self):
        return [self.level(by) for by in range(1, self.nz)]

    def plane(self):
        devices = []
        for by in range(1, 8):
            place = lax.rem(self.y * 4 + self.x * 2 + self.me + by, 8)
            devices.append((place // 2, place % 2, self.z))
        return devices

    def barrier(self, devices):
        semaphore = pltpu.get_barrier_semaphore()
        for device in devices:
            pl.semaphore_signal(semaphore, inc=1, device_id=device, device_id_type=MESH)
        pl.semaphore_wait(semaphore, len(devices))


def remote(source, target, sent, arrived, device):
    return pltpu.make_async_remote_copy(
        src_ref=source,
        dst_ref=target,
        send_sem=sent,
        recv_sem=arrived,
        device_id=device,
        device_id_type=MESH,
    )


def comm_params(number, limit=60):
    return pltpu.CompilerParams(
        vmem_limit_bytes=limit * 1024 * 1024, collective_id=number, has_side_effects=True
    )


HBM = pl.BlockSpec(memory_space=pl.ANY)


class Sent:
    def __init__(self):
        self.copies = []

    def go(self, copy, when=None):
        if when is None:
            copy.start()
        else:
            pl.when(when)(copy.start)
        self.copies.append((when, copy))

    def wait(self):
        for when, copy in self.copies:
            copy.wait_send() if when is None else pl.when(when)(copy.wait_send)


class Spread:
    BUFFERS = 6

    @staticmethod
    def scratch(nz):
        dma = pltpu.SemaphoreType.DMA
        return [dma((4, nz)), dma((4, nz)), dma((2, 5, nz)), dma((5, nz)), dma((5, nz)), dma((5, nz))]

    def __init__(self, at, sent, source, target, refs):
        self.at, self.sent, self.source, self.target = at, sent, source, target
        (
            self.flat_sent,
            self.flat_arrived,
            self.line_sent,
            self.line_arrived,
            self.core_sent,
            self.core_arrived,
        ) = refs

    def block(self, place, zz, core=None):
        at = self.at
        y = at.y if place < 2 else 1 - at.y
        x = at.x if place in (0, 2) else 1 - at.x
        ref = self.target.at[y, x, zz, at.me if core is None else core]
        if place >= 3:
            part = self.source.shape[0] // 2
            ref = ref.at[pl.ds((place - 3) * part, part)]
        return ref

    def half(self, place, zz, piece):
        part = self.source.shape[0] // 2
        return self.block(place, zz).at[pl.ds(piece * part, part)]

    def own(self):
        return self.target.at[self.at.y, self.at.x, self.at.z, self.at.me]

    def flat(self, source, target, index, zz, device):
        return remote(source, target, self.flat_sent.at[index, zz], self.flat_arrived.at[index, zz], device)

    def sides(self, source, zz, when=None):
        target = self.block(0, zz)
        self.sent.go(self.flat(source, target, 0, zz, self.at.next_x), when)
        self.sent.go(self.flat(source, target, 1, zz, self.at.next_y), when)

    def from_side(self, index, zz, when=None):
        at = self.at
        place = 1 + index
        ref = self.block(place, zz)
        copy = self.flat(ref, ref, index, zz, (at.next_x, at.next_y)[index])
        copy.wait_recv() if when is None else pl.when(when)(copy.wait_recv)
        ref = self.half(place, zz, index)
        self.sent.go(self.flat(ref, ref, 2 + index, zz, (at.next_y, at.next_x)[index]), when)
        self.hand_over(place, zz, when)

    def from_across(self, index, zz):
        ref = self.block(3 + index, zz)
        self.flat(ref, ref, 2 + index, zz, (self.at.next_y, self.at.next_x)[index]).wait_recv()
        self.hand_over(3 + index, zz)

    def line(self, source, place, zz, up, when):
        at = self.at
        ref = self.block(place, zz)
        copy = remote(
            ref if source is None else source,
            ref,
            self.line_sent.at[int(up), place, zz],
            self.line_arrived.at[place, zz],
            at.above if up else at.below,
        )
        self.sent.go(copy, (at.has_above if up else at.has_below) & when)

    def both_ways(self, place, source=None):
        for up in (True, False):
            self.line(source, place, self.at.z, up, True)

    def from_line(self, step, up, place, onward):
        at = self.at
        zz = at.z - step if up else at.z + step
        valid = zz >= 0 if up else zz < at.nz
        zz = jnp.clip(zz, 0, at.nz - 1)
        ref = self.block(place, zz)
        copy = remote(
            ref,
            ref,
            self.line_sent.at[int(up), place, zz],
            self.line_arrived.at[place, zz],
            at.below if up else at.above,
        )
        pl.when(valid)(copy.wait_recv)
        self.line(None, place, zz, up, valid)
        if onward:
            self.sides(ref, zz, valid)
        self.hand_over(place, zz, valid)

    def hand_over(self, place, zz, when=None, source=None):
        ref = self.block(place, zz)
        copy = remote(
            ref if source is None else source,
            ref,
            self.core_sent.at[place, zz],
            self.core_arrived.at[place, zz],
            self.at.core,
        )
        self.sent.go(copy, when)

    def finish(self):
        for zz in range(self.at.nz):
            for place in range(5):
                ref = self.block(place, zz, 1 - self.at.me)
                remote(
                    ref,
                    ref,
                    self.core_sent.at[place, zz],
                    self.core_arrived.at[place, zz],
                    self.at.core,
                ).wait_recv()


    def begin_line(self):
        self.both_ways(0, self.source)

    def begin_sides(self):
        self.sides(self.source, self.at.z)
        self.hand_over(0, self.at.z, source=self.source)

    def sides_at(self, step):
        at = self.at
        if step == 0:
            for index in range(2):
                self.from_side(index, at.z)
            return
        for zz, valid in ((at.z - step, at.z >= step), (at.z + step, at.z + step < at.nz)):
            for index in range(2):
                self.from_side(index, jnp.clip(zz, 0, at.nz - 1), valid)

    def corners(self):
        for zz in range(self.at.nz):
            for index in range(2):
                self.from_across(index, zz)


    def plane(self, place):
        z = self.at.z
        if place < 3:
            self.from_side(place - 1, z)
        else:
            self.from_across(place - 3, z)
        self.both_ways(place)


def begin_kernel(
    nz,
    own_ref,
    partner_ref,
    starts_ref,
    seq_ref,
    w_ref,
    wa_ref,
    wb_ref,
    x_ref,
    cot_ref,
    ck_ref,
    cv_ref,
    first_ref,
    a_ref,
    b_ref,
    xs_ref,
    cots_ref,
    qkv_ref,
    att_out,
    kmem_out,
    vmem_out,
    lse_ref,
    cos_ref,
    sin_ref,
    all_ref,
    xv_ref,
    n1_ref,
    y_ref,
    cotbuf,
    near_ref,
    far_ref,
    stage_ref,
    kmem_ref,
    vmem_ref,
    att_ref,
    acc_ref,
    shift_ref,
    total_ref,
    loaded,
    stored,
    csent,
    carrived,
    far_sent,
    far_arrived,
    far_csent,
    far_carrived,
    *refs,
):
    at = Place(nz)
    me, x, y, z = at.me, at.x, at.y, at.z
    keys = ck_ref.shape[1]
    width = w_ref.shape[1]
    tokens, model = n1_ref.shape
    half = model // 2
    sent = Sent()
    n = Spread.BUFFERS
    first = Spread(at, sent, w_ref, all_ref, refs[:n])
    late = Spread(at, sent, wa_ref, a_ref, refs[n : 2 * n])
    wide = Spread(at, sent, wb_ref, b_ref, refs[2 * n :])
    span = [pl.ds(0, keys), pl.ds(keys, keys)]
    caches = (ck_ref, cv_ref)

    def local(source, target, semaphore):
        return pltpu.make_async_copy(source, target, semaphore)

    loads = [
        local(source, target, loaded.at[i])
        for i, (source, target) in enumerate(
            (
                (w_ref, first.own()),
                (x_ref.at[me], xv_ref.at[me]),
                (cot_ref.at[me], cotbuf),
                (ck_ref.at[me], near_ref.at[me, span[0]]),
                (cv_ref.at[me], near_ref.at[me, span[1]]),
                (wa_ref, late.own()),
                (wb_ref, wide.own()),
            )
        )
    ]
    stores = [
        local(source, target, stored.at[i])
        for i, (source, target) in enumerate(
            (
                (cotbuf, cots_ref.at[me]),
                (xv_ref, xs_ref),
                (all_ref, first_ref),
                (y_ref, qkv_ref),
                (kmem_ref, kmem_out),
                (vmem_ref, vmem_out),
                (att_ref, att_out),
            )
        )
    ]
    for copy in loads:
        copy.start()
    at.barrier([at.core, at.next_x, at.next_y, at.above, at.below])
    exchange = [
        remote(source, target, csent.at[i], carrived.at[i], at.core)
        for i, (source, target) in enumerate(
            (
                (x_ref.at[1 - me], xv_ref.at[me]),
                (ck_ref.at[1 - me], near_ref.at[me, span[0]]),
                (cv_ref.at[1 - me], near_ref.at[me, span[1]]),
                (cot_ref.at[1 - me], cots_ref.at[me]),
            )
        )
    ]

    def landing(source, turn, kv):
        return far_ref.at[source, me, span[kv]] if turn == 0 else stage_ref.at[source, kv]

    def cache_copy(line, turn, kv):
        index = (line, turn * 2 + kv)
        return remote(
            caches[kv].at[me if turn == 0 else 1 - me],
            landing(line, turn, kv),
            far_sent.at[index],
            far_arrived.at[index],
            (at.next_x, at.next_y)[line],
        )

    def corner_copy(turn, kv):
        source, device = (0, at.next_y) if turn == 0 else (1, at.next_x)
        index = (2, turn * 2 + kv)
        return remote(
            landing(source, turn, kv), landing(2, turn, kv), far_sent.at[index], far_arrived.at[index], device
        )

    def hand_over(source, kv):
        return remote(
            stage_ref.at[source, kv],
            far_ref.at[source, me, span[kv]],
            far_csent.at[source, kv],
            far_carrived.at[source, kv],
            at.core,
        )

    def from_lines(spread, step, places, onward):
        for place in places:
            for up in (True, False):
                spread.from_line(step, up, place, onward)


    first.begin_line()
    first.begin_sides()
    wide.begin_line()
    wide.begin_sides()
    sent.go(exchange[0])

    place_in = lax.broadcasted_iota(jnp.int32, (tokens, HEAD_DIM), 0).astype(F32)
    lane = lax.broadcasted_iota(jnp.int32, (1, HEAD_DIM), 1)
    turns = lax.rem(lane, HEAD_DIM // 2).astype(F32) * (-2.0 * math.log(10000.0) / HEAD_DIM)
    angles = place_in * jnp.exp(turns)
    cos_ref[...] = jnp.cos(angles)
    sin_ref[...] = jnp.where(lane < HEAD_DIM // 2, -1.0, 1.0) * jnp.sin(angles)

    from_lines(first, 1, (0,), True)
    wide.plane(1)
    wide.plane(2)
    first.sides_at(0)
    from_lines(first, 2, (0,), True)
    wide.plane(3)
    wide.plane(4)
    first.sides_at(1)
    for kv in range(2):
        sent.go(cache_copy(0, 0, kv))
        sent.go(cache_copy(1, 1, kv))
    from_lines(first, 3, (0,), True)
    first.sides_at(2)
    for kv in range(2):
        sent.go(cache_copy(0, 1, kv))
        sent.go(cache_copy(1, 0, kv))
    for copy in exchange[1:]:
        sent.go(copy)
    late.begin_line()
    late.begin_sides()
    first.sides_at(3)
    from_lines(wide, 1, range(3), False)
    loads[2].wait()
    stores[0].start()
    loads[1].wait()
    exchange[0].wait_recv()
    stores[1].start()
    first.corners()
    loads[0].wait()
    first.finish()
    stores[2].start()
    from_lines(wide, 1, range(3, 5), False)

    gains = all_ref[:, :, :, 0, :, pl.ds(width - LANES, LANES)].reshape(model, LANES).astype(F32)
    gain = jnp.transpose(gains)[0:1, :]

    def norm(rows):
        normal, _ = normal_of(features(xv_ref, rows).astype(F32))
        n1_ref[rows, :] = (normal * gain).astype(BF)

    chunks(tokens, norm)

    def project(i, carry):
        m, h = i // 2, i % 2
        lanes = pl.ds(pl.multiple_of(m * half, half), half)
        value = nn(n1_ref[...], all_ref[:, :, :, h, :, lanes].reshape(model, half))
        for head in range(half // HEAD_DIM):
            lanes = slice(head * HEAD_DIM, (head + 1) * HEAD_DIM)
            u = value[:, lanes]
            turned = u * cos_ref[...] + pltpu.roll(u, HEAD_DIM // 2, 1) * sin_ref[...]
            y_ref[m, h, :, lanes] = jnp.where(m < 2, turned, u).astype(BF)
        return carry

    lax.fori_loop(0, 6, project, 0)
    stores[3].start()


    for kv in range(2):
        cache_copy(0, 0, kv).wait_recv()
        sent.go(corner_copy(0, kv))
        cache_copy(1, 1, kv).wait_recv()
        sent.go(corner_copy(1, kv))
        sent.go(hand_over(1, kv))
    for copy in loads[3:5]:
        copy.wait()
    for copy in exchange[1:3]:
        copy.wait_recv()

    def choose(index_ref, first_row):
        for b in range(QBLKS):
            for j in range(OWN_K):
                index = index_ref[me, b, j]
                rows = pl.ds(first_row + j * MEM_BLK, MEM_BLK)
                for h in range(2):
                    for offset, ref in ((0, kmem_ref), (keys, vmem_ref)):
                        block = near_ref[h, pl.ds(offset, MEM_BLK), :]
                        for c in range(1, keys // MEM_BLK):
                            other = near_ref[h, pl.ds(offset + c * MEM_BLK, MEM_BLK), :]
                            block = jnp.where(index == c, other, block)
                        ref[h, b, rows, :] = block

    choose(own_ref, 0)
    heads = half // HEAD_DIM
    near_rows = slice(0, OWN_K * MEM_BLK)
    far_rows = slice(OWN_K * MEM_BLK, (OWN_K + PART_K) * MEM_BLK)

    def place(i):
        h, column = i // heads, i % heads
        return h, column, pl.ds(pl.multiple_of(column * HEAD_DIM, HEAD_DIM), HEAD_DIM)

    def without_partner(i, carry):
        h, column, lanes = place(i)

        def store(rows, shift, total, acc):
            acc_ref[i, :, rows] = acc
            shift_ref[i, :, rows] = shift
            total_ref[i, :, rows] = total

        attend_head(
            lambda m, rows: y_ref[m, h, rows, lanes],
            lambda b: (kmem_ref[h, b, near_rows, lanes], vmem_ref[h, b, near_rows, lanes]),
            [starts_ref[me, b] for b in range(QBLKS)],
            store,
        )
        return carry

    def with_partner(i, carry):
        h, column, lanes = place(i)
        for b in range(QBLKS):
            rows = pl.ds(b * QROWS, QROWS)
            shift, total, acc = attend_rows(
                [(kmem_ref[h, b, far_rows, lanes], vmem_ref[h, b, far_rows, lanes], None)],
                y_ref[0, h, rows, lanes],
            )
            before = shift_ref[i, :, rows]
            top = jnp.maximum(shift, before)
            now, then = jnp.exp2(shift - top), jnp.exp2(before - top)
            total = total * now + total_ref[i, :, rows] * then
            acc = acc * now + acc_ref[i, :, rows] * then
            att_ref[h, rows, lanes] = jnp.transpose(acc / total).astype(BF)
            lse_ref[h, column, :, rows] = top + jnp.log2(total)
        return carry

    lax.fori_loop(0, heads, without_partner, 0)
    from_lines(late, 1, (0,), True)
    from_lines(wide, 2, range(3), False)
    for kv in range(2):
        cache_copy(0, 1, kv).wait_recv()
        sent.go(hand_over(0, kv))
        cache_copy(1, 0, kv).wait_recv()
    lax.fori_loop(heads, 2 * heads, without_partner, 0)
    from_lines(wide, 2, range(3, 5), False)
    from_lines(late, 2, (0,), True)
    from_lines(late, 3, (0,), True)
    late.sides_at(0)
    for kv in range(2):
        corner_copy(1, kv).wait_recv()
        sent.go(hand_over(2, kv))
        corner_copy(0, kv).wait_recv()
    for source in range(3):
        for kv in range(2):
            remote(
                stage_ref.at[source, kv],
                far_ref.at[source, 1 - me, span[kv]],
                far_csent.at[source, kv],
                far_carrived.at[source, kv],
                at.core,
            ).wait_recv()
    source = seq_ref[me]
    across = (1 - y) * 2 + 1 - x
    near_y = (1 - y) * 2 + x
    at_most = SEQ_DEV * nz

    def comes_from(place):
        return (source >= place * at_most) & (source < (place + 1) * at_most)

    def take(i, carry):
        rows = pl.ds(pl.multiple_of(i * MEM_BLK, MEM_BLK), MEM_BLK)
        for h in range(2):
            block = jnp.where(comes_from(near_y), far_ref[1, h, rows, :], far_ref[0, h, rows, :])
            near_ref[h, rows, :] = jnp.where(comes_from(across), far_ref[2, h, rows, :], block)
        return carry

    lax.fori_loop(0, 2 * keys // MEM_BLK, take, 0)
    choose(partner_ref, OWN_K * MEM_BLK)
    stores[4].start()
    stores[5].start()
    lax.fori_loop(0, 2 * heads, with_partner, 0)
    stores[6].start()
    late.sides_at(1)
    from_lines(wide, 3, range(5), False)
    late.sides_at(2)
    late.sides_at(3)

    late.corners()
    late.finish()
    wide.finish()
    exchange[3].wait_recv()
    for copy in loads[5:]:
        copy.wait()
    for copy in stores:
        copy.wait()
    sent.wait()


def begin(own, partner, starts, seq, w, wa, wb, x, cot, cache_keys, cache_values, nz):
    dma = pltpu.SemaphoreType.DMA
    _, tokens, half = x.shape
    keys = cache_keys.shape[1]
    full = jax.ShapeDtypeStruct((2, tokens, half), BF)
    gathered = lambda w: (2, 2, nz, 2) + w.shape
    whole_array = lambda w: jax.ShapeDtypeStruct(gathered(w), BF)
    vmem = pl.BlockSpec(memory_space=pltpu.VMEM)
    table = jax.ShapeDtypeStruct((tokens, HEAD_DIM), F32)
    heads = 2 * half // HEAD_DIM
    memory = (2, QBLKS, (OWN_K + PART_K) * MEM_BLK, half)
    return pl.pallas_call(
        functools.partial(begin_kernel, nz),
        in_specs=[pl.BlockSpec(memory_space=pltpu.SMEM)] * 4 + [HBM] * 7,
        out_specs=[HBM] * 9 + [vmem] * 3,
        out_shape=[
            whole_array(w),
            whole_array(wa),
            whole_array(wb),
            full,
            full,
            jax.ShapeDtypeStruct((3, 2, tokens, half), BF),
            full,
            jax.ShapeDtypeStruct(memory, BF),
            jax.ShapeDtypeStruct(memory, BF),
            jax.ShapeDtypeStruct((2, half // HEAD_DIM, 1, tokens), F32),
            table,
            table,
        ],
        scratch_shapes=[
            pltpu.VMEM(gathered(w), BF),
            pltpu.VMEM((2, tokens, half), BF),
            pltpu.VMEM((tokens, 2 * half), BF),
            pltpu.VMEM((3, 2, tokens, half), BF),
            pltpu.VMEM((tokens, half), BF),
            pltpu.VMEM((2, 2 * keys, half), BF),
            pltpu.VMEM((3, 2, 2 * keys, half), BF),
            pltpu.VMEM((3, 2, keys, half), BF),
            pltpu.VMEM(memory, BF),
            pltpu.VMEM(memory, BF),
            pltpu.VMEM((2, tokens, half), BF),
            pltpu.VMEM((heads, HEAD_DIM, tokens), F32),
            pltpu.VMEM((heads, 1, tokens), F32),
            pltpu.VMEM((heads, 1, tokens), F32),
            dma((7,)),
            dma((7,)),
            dma((4,)),
            dma((4,)),
            dma((3, 4)),
            dma((3, 4)),
            dma((3, 2)),
            dma((3, 2)),
        ]
        + Spread.scratch(nz) * 3,
        compiler_params=comm_params(0),
        name="begin",
    )(own, partner, starts, seq, w, wa, wb, x, cot, cache_keys, cache_values)


class Sums:
    BUFFERS = 10

    @staticmethod
    def last(halved):
        return 4 if halved else 3

    @staticmethod
    def scratch(parts, rows, tiles, nz, halved, taken=False):
        dma = pltpu.SemaphoreType.DMA
        slab = rows // 4
        pairs = pltpu.VMEM((1, 1, 16, LANES) if taken else (2, parts, rows, LANES), BF)
        return [
            pairs,
            pairs,
            pltpu.VMEM((tiles, parts, rows, LANES), BF),
            pltpu.VMEM((tiles, 2, parts, slab // 2, LANES) if halved else (tiles, 1, parts, slab, LANES), BF),
            pltpu.VMEM((tiles, 2, parts, slab, LANES), BF),
            pltpu.VMEM((tiles, nz - 1, parts, slab // nz, LANES), BF),
            dma((tiles, 5)),
            dma((tiles, 5)),
            dma((tiles, nz - 1)),
            dma((tiles, nz - 1)),
        ]

    def __init__(self, at, halved, refs, left=0):
        (
            self.mine,
            self.other,
            self.total,
            self.diag,
            self.side,
            self.hop,
            self.sent,
            self.arrived,
            self.hop_sent,
            self.hop_arrived,
        ) = refs
        self.at, self.halved = at, halved
        self.tiles, _, self.rows, _ = self.total.shape
        self.left, self.early = left, self.tiles - left
        self.slab = self.rows // 4
        self.block = self.slab // at.nz

    def span(self, y, x, first=0, size=None):
        start = pl.multiple_of((y * 2 + x) * self.slab + first, self.block)
        return pl.ds(start, self.slab if size is None else size)

    def copy(self, j, span, target, index, device):
        return remote(
            self.total.at[j, :, span], target, self.sent.at[j, index], self.arrived.at[j, index], device
        )

    def core_copy(self, j):
        return remote(
            self.other.at[j % 2],
            self.total.at[j],
            self.sent.at[j, 0],
            self.arrived.at[j, 0],
            self.at.core,
        )

    def diag_copies(self, j):
        at, part = self.at, self.slab // 2
        y, x = 1 - at.y, 1 - at.x
        if not self.halved:
            return [self.copy(j, self.span(y, x), self.diag.at[j, 0], 1, at.corner())]
        return [
            self.copy(j, self.span(y, x, i * part, part), self.diag.at[j, i], 1 + i, device)
            for i, device in enumerate((at.next_x, at.next_y))
        ]

    def side_copies(self, j):
        at = self.at
        return [
            self.copy(j, self.span(at.y, 1 - at.x), self.side.at[j, 0], 3, at.next_x),
            self.copy(j, self.span(1 - at.y, at.x), self.side.at[j, 1], 4, at.next_y),
        ]

    def hop_copies(self, j):
        at = self.at
        copies = []
        for by in range(1, at.nz):
            device = at.level(by)
            copies.append(
                remote(
                    self.total.at[j, :, self.span(at.y, at.x, device[2] * self.block, self.block)],
                    self.hop.at[j, by - 1],
                    self.hop_sent.at[j, by - 1],
                    self.hop_arrived.at[j, by - 1],
                    device,
                )
            )
        return copies

    def add(self, j, span, *values):
        total = self.total[j, :, span, :].astype(F32)
        for value in values:
            total = total + value.astype(F32)
        self.total[j, :, span, :] = total.astype(BF)

    def start(self, j):
        self.core_copy(j).start()

    def after_core(self, j):
        self.core_copy(j).wait()

        def body(rows):
            self.add(j, rows, self.mine[j % 2, :, rows, :])

        chunks(self.rows, body)

    def begin(self, j):
        for copy in self.diag_copies(j):
            copy.start()
        if not self.halved:
            for copy in self.side_copies(j):
                copy.start()

    def after_diag(self, j):
        at, part = self.at, self.slab // 2
        for copy in self.diag_copies(j):
            copy.wait()
        self.add(j, self.span(1 - at.y, at.x, 0, part), self.diag[j, 0])
        self.add(j, self.span(at.y, 1 - at.x, part, part), self.diag[j, 1])
        for copy in self.side_copies(j):
            copy.start()

    def after_side(self, j):
        at = self.at
        for copy in self.side_copies(j):
            copy.wait()
        values = [self.side[j, 0], self.side[j, 1]]
        if not self.halved:
            for copy in self.diag_copies(j):
                copy.wait()
            values.append(self.diag[j, 0])
        self.add(j, self.span(at.y, at.x), *values)
        for copy in self.hop_copies(j):
            copy.start()

    def result(self, j):
        at = self.at
        for copy in self.hop_copies(j):
            copy.wait()
        value = self.total[j, :, self.span(at.y, at.x, at.z * self.block, self.block), :].astype(F32)
        for by in range(at.nz - 1):
            value = value + self.hop[j, by].astype(F32)
        return value

    def advance(self, step, store, leave=None, taken=False):
        def on(behind, body, first, last):
            j = step - behind
            pl.when((j >= first) & (j < last))(lambda: body(jnp.clip(j, first, last - 1)))

        def summed(j):
            self.after_core(j)
            self.begin(j)

        def left(j):
            self.after_core(j)
            leave(self.total[j])

        if not taken:
            on(1, summed, 0, self.early)
        if self.left:
            on(1, left, self.early, self.tiles)
        if self.halved:
            on(2, self.after_diag, 0, self.early)
        on(self.last(self.halved) - 1, self.after_side, 0, self.early)
        on(self.last(self.halved), lambda j: store(self.result(j)), 0, self.early)


class Norms:
    BUFFERS = 7

    @staticmethod
    def scratch(model, nz):
        dma = pltpu.SemaphoreType.DMA
        return [
            pltpu.VMEM((4, 8, model // 4), F32),
            pltpu.VMEM((8, 8, model // 4), F32),
            pltpu.VMEM((nz, 8, LANES), F32),
            dma((7,)),
            dma((7,)),
            dma((nz - 1,)),
            dma((nz - 1,)),
        ]

    def __init__(self, at, refs):
        self.at = at
        self.own, self.parts, self.level, self.sent, self.arrived, self.hop_sent, self.hop_arrived = refs

    def plane_copies(self):
        at = self.at
        me = at.y * 4 + at.x * 2 + at.me
        return [
            remote(self.own.at[device[0]], self.parts.at[me], self.sent.at[i], self.arrived.at[i], device)
            for i, device in enumerate(at.plane())
        ]

    def hop_copies(self):
        at = self.at
        me = at.y * 4 + at.x * 2 + at.me
        copies = []
        for by in range(1, at.nz):
            device = at.level(by)
            lanes = pl.ds(pl.multiple_of(device[2] // 2 * LANES, LANES), LANES)
            copies.append(
                remote(
                    self.own.at[0, :, lanes],
                    self.level.at[at.z],
                    self.hop_sent.at[by - 1],
                    self.hop_arrived.at[by - 1],
                    device,
                )
            )
        return copies

    def start(self, rows):
        at = self.at
        width = self.own.shape[2]
        for d in range(4):
            self.own[d] = rows[:, d * width : (d + 1) * width]
        self.parts[at.y * 4 + at.x * 2 + at.me] = self.own[at.y * 2 + at.x]
        for copy in self.plane_copies():
            copy.start()

    def after_plane(self):
        at = self.at
        for copy in self.plane_copies():
            copy.wait()
        total = self.parts[0]
        for i in range(1, 8):
            total = total + self.parts[i]
        self.own[0] = total
        lanes = pl.ds(pl.multiple_of(at.z // 2 * LANES, LANES), LANES)
        self.level[at.z] = self.own[0, :, lanes]
        for copy in self.hop_copies():
            copy.start()

    def result(self):
        for copy in self.hop_copies():
            copy.wait()
        total = self.level[0]
        for i in range(1, self.at.nz):
            total = total + self.level[i]
        return total


class Unsummed:
    class Tile:
        def __init__(self, ref):
            self.ref = ref

        def __setitem__(self, index, value):
            self.ref[index[1:]] = value

    def __init__(self, mine, other):
        self.mine, self.other = Unsummed.Tile(mine), Unsummed.Tile(other)

    def start(self, j):
        pass

    def advance(self, step, store, leave=None):
        pass


def features(ref, rows):
    return jnp.concatenate([ref[0, rows, :], ref[1, rows, :]], axis=1)


def pair(ref, model):
    return jnp.concatenate(
        [ref[:, 0].reshape(model, LANES), ref[:, 1].reshape(model, LANES)], axis=1
    )


def normal_of(x):
    inverse = lax.rsqrt(jnp.mean(x * x, axis=1, keepdims=True) + EPSILON)
    return x * inverse, inverse


def norm_back(normal, inverse, gain, grad):
    scaled = grad * gain
    return inverse * (scaled - normal * jnp.mean(scaled * normal, axis=1, keepdims=True))


def qkv_kernel(x_ref, gain_ref, w_ref, cos_ref, sin_ref, out_ref, n1_ref):
    part = pl.program_id(0)
    tokens, model = n1_ref.shape

    @pl.when((part == 0) & (pl.program_id(1) == 0))
    def _():
        def norm(rows):
            normal, _ = normal_of(features(x_ref, rows).astype(F32))
            n1_ref[rows, :] = (normal * gain_ref[...]).astype(BF)

        chunks(tokens, norm)

    def project(rows):
        y = nn(n1_ref[rows, :], w_ref[...].reshape(model, -1))
        cosine, sine = cos_ref[rows, :], sin_ref[rows, :]
        for h in range(y.shape[1] // HEAD_DIM):
            lanes = slice(h * HEAD_DIM, (h + 1) * HEAD_DIM)
            u = y[:, lanes]
            turned = u * cosine + pltpu.roll(u, HEAD_DIM // 2, 1) * sine
            out_ref[rows, lanes] = jnp.where(part < 2, turned, u).astype(BF)

    chunks(tokens, project, tokens)


def project_qkv(x, gain, gathered, cosine, sine):
    halves, tokens, half = x.shape
    groups, _, rows, _ = gathered.shape
    return pl.pallas_call(
        qkv_kernel,
        grid=(3, halves),
        in_specs=[
            whole(x.shape),
            whole(gain.shape),
            pl.BlockSpec((groups, None, rows, half), lambda m, h: (0, h, 0, m)),
            whole(cosine.shape),
            whole(sine.shape),
        ],
        out_specs=pl.BlockSpec((None, None, tokens, half), lambda m, h: (m, h, 0, 0)),
        out_shape=jax.ShapeDtypeStruct((3, halves, tokens, half), BF),
        scratch_shapes=[pltpu.VMEM((tokens, halves * half), BF)],
        compiler_params=params(),
        name="project_qkv",
    )(x, gain, gathered, cosine, sine)


def fill_memory(idx_ref, near_ref, far_ref, offset, mem_ref):
    for b in range(QBLKS):
        for j in range(OWN_K + PART_K):
            ref, at = (near_ref, b * OWN_K + j) if j < OWN_K else (far_ref, QBLKS * OWN_K + b * PART_K + j - OWN_K)
            start = pl.multiple_of(idx_ref[at] * MEM_BLK, MEM_BLK) + offset
            mem_ref[b, j * MEM_BLK : (j + 1) * MEM_BLK, :] = ref[pl.ds(start, MEM_BLK), :]


def masked(scores, start):
    keys, queries = scores.shape
    at = lax.broadcasted_iota(jnp.int32, (1, queries), 1)
    limit = jnp.where((at >= start) & (at < start + PIC), start + PIC - 1, at)
    key = lax.broadcasted_iota(jnp.int32, (keys, queries), 0)
    return jnp.where(key <= limit, scores, NEG)


SCALE = LOG2E / math.sqrt(HEAD_DIM)


def attend_rows(parts, q):
    scores = []
    for keys, values, mask in parts:
        s = nt(keys, q)
        scores.append((s if mask is None else masked(s, *mask), values))
    top = functools.reduce(jnp.maximum, [jnp.max(s, axis=0, keepdims=True) for s, _ in scores])
    shift = top * SCALE
    total = jnp.zeros_like(top)
    acc = jnp.zeros((HEAD_DIM, q.shape[0]), F32)
    for s, values in scores:
        e = jnp.exp2(s * SCALE - shift)
        total = total + jnp.sum(e, axis=0, keepdims=True)
        acc = acc + tn(values, e.astype(BF))
    return shift, total, acc


def attend_head(part, memory, starts, store):
    for b in range(QBLKS):
        rows = slice(b * QROWS, (b + 1) * QROWS)
        parts = []
        for n in range(b + 1):
            span = slice(n * QROWS, (n + 1) * QROWS)
            mask = (starts[b] - b * QROWS,) if n == b else None
            parts.append((part(1, span), part(2, span), mask))
        parts.append(memory(b) + (None,))
        store(rows, *attend_rows(parts, part(0, rows)))


def attend_kernel(
    idx_ref, q_ref, k_ref, v_ref, near_ref, far_ref, out_ref, lse_ref, kmem_ref, vmem_ref
):
    keys = near_ref.shape[0] // 2
    fill_memory(idx_ref, near_ref, far_ref, 0, kmem_ref)
    fill_memory(idx_ref, near_ref, far_ref, keys, vmem_ref)
    refs = (q_ref, k_ref, v_ref)

    def store(rows, shift, total, acc):
        out_ref[rows, :] = jnp.transpose(acc / total).astype(BF)
        lse_ref[:, rows] = shift + jnp.log2(total)

    attend_head(
        lambda m, rows: refs[m][rows, :],
        lambda b: (kmem_ref[b], vmem_ref[b]),
        [idx_ref[QBLKS * (OWN_K + PART_K) + b] for b in range(QBLKS)],
        store,
    )


def attend(idx, qkv, near, far):
    _, halves, tokens, half = qkv.shape
    here = half // HEAD_DIM
    cached = near.shape[1]
    memory = (OWN_K + PART_K) * MEM_BLK
    column = lambda m: pl.BlockSpec(
        (None, None, tokens, HEAD_DIM), lambda h, idx: (m, h // here, 0, h % here)
    )
    cache = pl.BlockSpec((None, cached, HEAD_DIM), lambda h, idx: (h // here, 0, h % here))
    which = QBLKS * (OWN_K + PART_K) + QBLKS
    partner = pl.BlockSpec(
        (None, None, cached, HEAD_DIM), lambda h, idx: (idx[which], h // here, 0, h % here)
    )
    chosen = pl.BlockSpec((None, QBLKS, memory, HEAD_DIM), lambda h, idx: (h // here, 0, 0, h % here))
    chosen_shape = jax.ShapeDtypeStruct((halves, QBLKS, memory, half), BF)
    return pl.pallas_call(
        attend_kernel,
        grid_spec=pltpu.PrefetchScalarGridSpec(
            num_scalar_prefetch=1,
            grid=(halves * here,),
            in_specs=[column(0), column(1), column(2), cache, partner],
            out_specs=[
                pl.BlockSpec((None, tokens, HEAD_DIM), lambda h, idx: (h // here, 0, h % here)),
                pl.BlockSpec((None, None, 1, tokens), lambda h, idx: (h // here, h % here, 0, 0)),
                chosen,
                chosen,
            ],
        ),
        out_shape=[
            jax.ShapeDtypeStruct((halves, tokens, half), BF),
            jax.ShapeDtypeStruct((halves, here, 1, tokens), F32),
            chosen_shape,
            chosen_shape,
        ],
        compiler_params=params(),
        name="attend",
    )(idx, qkv, qkv, qkv, near, far)


def split_store(me, value, mine_ref, other_ref, index):
    low, high = value[:, :LANES], value[:, LANES:]
    mine_ref[index] = jnp.where(me == 0, low, high)
    other_ref[index] = jnp.where(me == 0, high, low)


def send_halves(at, buffer, out_ref, local, sent, arrived):
    tokens = buffer.shape[1]
    rows = pl.ds(pl.multiple_of(at.me * tokens, tokens), tokens)
    return (
        pltpu.make_async_copy(buffer.at[at.me], out_ref.at[rows], local),
        remote(buffer.at[1 - at.me], out_ref.at[rows], sent, arrived, at.core),
    )


def feed_kernel(
    nz,
    steps,
    x_ref,
    att_ref,
    cot_ref,
    gain_ref,
    wo_ref,
    wg_ref,
    wu_ref,
    wd_ref,
    ghid_ref,
    gn2_ref,
    *refs,
):
    if nz:
        out_ref, grad_ref, late_ref, *refs = refs
    else:
        result_ref, mine_ref, other_ref, *refs = refs
    hid_ref, n2_ref, n2t_ref, cott_ref, acc_ref, dn_ref, a_ref, dg_ref, du_ref, *refs = refs
    tokens, model = hid_ref.shape
    half = model // 2
    step = pl.program_id(0)
    me = lax.axis_index("row")
    copies = []
    if nz:
        at = Place(nz)
        result_ref, local, sent, arrived, *refs = refs
        sums = Sums(at, True, refs, LATE)
        copies = send_halves(at, result_ref, out_ref, local.at[0], sent.at[0], arrived.at[0])
    else:
        sums = Unsummed(mine_ref, other_ref)

    def wo_half(h):
        return wo_ref[:, h].reshape(model, half)

    @pl.when(step == 0)
    def _():
        if nz:
            at.barrier([at.core, at.next_x, at.next_y] + at.levels())

        def start(rows):
            hidden = features(x_ref, rows).astype(F32)
            for h in range(2):
                hidden = hidden + nt(att_ref[h, rows, :], wo_half(h))
            hid_ref[rows, :] = hidden
            normal, _ = normal_of(hidden)
            n2_ref[rows, :] = (normal * gain_ref[...]).astype(BF)
            n2t_ref[:, rows] = jnp.transpose(n2_ref[rows, :])
            cott_ref[:, rows] = jnp.transpose(features(cot_ref, rows))
            acc_ref[rows, :] = jnp.zeros((CHUNK, model), F32)
            dn_ref[rows, :] = jnp.zeros((CHUNK, model), F32)

        chunks(tokens, start)

    def store(value):
        grad_ref[...] = value

    def leave(value):
        late_ref[...] = value

    def forward_back(rows):
        n2 = n2_ref[rows, :]
        gating = nn(n2, pair(wg_ref, model))
        upward = nn(n2, pair(wu_ref, model))
        gactive = nn(features(cot_ref, rows), pair(wd_ref, model))
        sigmoid = 1.0 / (1.0 + jnp.exp(-gating))
        silu = gating * sigmoid
        a_ref[rows, :] = (silu * upward).astype(BF)
        dg_ref[rows, :] = (gactive * upward * (sigmoid + silu * (1.0 - sigmoid))).astype(BF)
        du_ref[rows, :] = (gactive * silu).astype(BF)
        acc_ref[rows, :] += nt(a_ref[rows, :], pair(wd_ref, model))
        dn_ref[rows, :] += nt(dg_ref[rows, :], pair(wg_ref, model)) + nt(
            du_ref[rows, :], pair(wu_ref, model)
        )

    @pl.when(step < steps)
    def _():
        chunks(tokens, forward_back, tokens)
        slot = step % 2

        def weights(rows):
            n2t = n2t_ref[rows, :]
            for p, value in enumerate(
                (nn(n2t, dg_ref[...]), nn(n2t, du_ref[...]), nn(cott_ref[rows, :], a_ref[...]))
            ):
                split_store(me, value.astype(BF), sums.mine, sums.other, (slot, p, rows))

        chunks(model, weights, model)
        sums.start(step)

    sums.advance(step, store, leave)

    @pl.when(step == (steps if nz else steps - 1))
    def _():
        gn2_ref[...] = jnp.zeros_like(gn2_ref)

        def finish(rows):
            hidden = hid_ref[rows, :]
            result = (hidden + acc_ref[rows, :]).astype(BF)
            result_ref[0, rows, :] = result[:, :half]
            result_ref[1, rows, :] = result[:, half:]
            normal, inverse = normal_of(hidden)
            dn = dn_ref[rows, :]
            gn2_ref[...] += jnp.sum(dn * normal, axis=0, keepdims=True)
            ghid_ref[rows, :] = features(cot_ref, rows).astype(F32) + norm_back(
                normal, inverse, gain_ref[...], dn
            )

        chunks(tokens, finish)
        for copy in copies:
            copy.start()

    if nz:

        @pl.when(step == pl.num_programs(0) - 1)
        def _():
            for copy in copies:
                copy.wait()


def feed(x, attended, cotangent, gain, narrow, wide, units, nz):
    halves, tokens, half = x.shape
    model = halves * half
    groups, _, rows, _ = wide.shape
    steps = units // LANES
    tile = lambda at: pl.BlockSpec(
        (groups, halves, rows, LANES),
        lambda j: (0, 0, 0, at // LANES + jnp.minimum(j, steps - 1)),
    )
    big = lambda dtype: pltpu.VMEM((tokens, model), dtype)
    small = pltpu.VMEM((tokens, 2 * LANES), BF)
    early = steps - LATE
    last = Sums.last(True)
    dma = pltpu.SemaphoreType.DMA((1,))
    if nz:
        out_specs = [
            HBM,
            pl.BlockSpec((3, rows, LANES), lambda j: (0, 0, jnp.clip(j - last, 0, early - 1))),
            pl.BlockSpec((3, model, LANES), lambda j: (0, 0, jnp.clip(j - 1 - early, 0, LATE - 1))),
        ]
        out_shape = [
            jax.ShapeDtypeStruct((halves * tokens, half), BF),
            jax.ShapeDtypeStruct((3, rows, early * LANES), F32),
            jax.ShapeDtypeStruct((3, model, LATE * LANES), BF),
        ]
        more = [pltpu.VMEM(x.shape, BF), dma, dma, dma] + Sums.scratch(3, model, steps, nz, True)
    else:
        grads = pl.BlockSpec((3, model, LANES), lambda j: (0, 0, j))
        out_specs = [once(x.shape), grads, grads]
        grads = jax.ShapeDtypeStruct((3, model, units), BF)
        out_shape = [jax.ShapeDtypeStruct(x.shape, BF), grads, grads]
        more = []
    return pl.pallas_call(
        functools.partial(feed_kernel, nz, steps),
        grid=(max(steps + 1, early + last) if nz else steps,),
        in_specs=[
            once(x.shape),
            once(x.shape),
            once(x.shape),
            once(gain.shape),
            pl.BlockSpec(
                (groups, halves, rows, half),
                lambda j: (0, 0, 0, 0),
                pipeline_mode=pl.Buffered(1),
            ),
            tile(0),
            tile(units),
            tile(half),
        ],
        out_specs=[once((tokens, model)), once(gain.shape)] + out_specs,
        out_shape=[
            jax.ShapeDtypeStruct((tokens, model), F32),
            jax.ShapeDtypeStruct(gain.shape, F32),
        ]
        + out_shape,
        scratch_shapes=[big(F32), big(BF), big(BF), big(BF), big(F32), big(F32), small, small, small]
        + more,
        compiler_params=comm_params(1) if nz else params(),
        name="feed",
    )(x, attended, cotangent, gain, narrow, wide, wide, narrow)


def back_kernel(
    nz,
    steps,
    starts_ref,
    qkv_ref,
    kmem_ref,
    vmem_ref,
    att_ref,
    lse_ref,
    wo_ref,
    wq_ref,
    wk_ref,
    wv_ref,
    x_ref,
    gain_ref,
    ghid_ref,
    gn2_ref,
    cos_ref,
    sin_ref,
    *refs,
):
    if nz:
        left_ref, out_ref, grad_ref, late_ref, norms_ref, *refs = refs
    else:
        result_ref, mine_ref, other_ref, gn1_ref, *refs = refs
    gmix_ref, gmixt_ref, n1t_ref, dn_ref, gatt_ref, g_ref, dk_ref, dv_ref, *refs = refs
    tokens, model = ghid_ref.shape
    half = model // 2
    step = pl.program_id(0)
    me = lax.axis_index("row")
    copies = []
    if nz:
        at = Place(nz)
        result_ref, local, sent, arrived, *refs = refs
        sums = Sums(at, True, refs[: Sums.BUFFERS])
        late = Sums(at, True, refs[Sums.BUFFERS : 2 * Sums.BUFFERS])
        norms = Norms(at, refs[2 * Sums.BUFFERS :])
        copies = send_halves(at, result_ref, out_ref, local.at[0], sent.at[0], arrived.at[0])
    else:
        sums = Unsummed(mine_ref, other_ref)
    scale = LOG2E / math.sqrt(HEAD_DIM)
    plain = 1.0 / math.sqrt(HEAD_DIM)

    @pl.when(step == 0)
    def _():
        if nz:
            at.barrier(at.plane() + at.levels())

        def start(rows):
            normal, _ = normal_of(features(x_ref, rows).astype(F32))
            n1t_ref[:, rows] = jnp.transpose((normal * gain_ref[...]).astype(BF))
            gmix_ref[rows, :] = ghid_ref[rows, :].astype(BF)
            gmixt_ref[:, rows] = jnp.transpose(gmix_ref[rows, :])
            dn_ref[rows, :] = jnp.zeros((CHUNK, model), F32)

        chunks(tokens, start)

    def store(value):
        grad_ref[...] = value

    def store_late(value):
        late_ref[...] = value

    if nz:

        @pl.when(step < LATE)
        def _():
            late.total[step] = left_ref[...]
            late.begin(step)

    def unturn(g, rows):
        return g * cos_ref[rows, :] - pltpu.roll(g, HEAD_DIM // 2, 1) * sin_ref[rows, :]

    def one_head(hh, carry):
        dk_ref[...] = jnp.zeros_like(dk_ref)
        dv_ref[...] = jnp.zeros_like(dv_ref)
        for b in range(QBLKS):
            start = starts_ref[me, b] - b * QROWS

            rows = slice(b * QROWS, (b + 1) * QROWS)
            q = qkv_ref[0, hh, rows, :]
            do = gatt_ref[hh, rows, :]
            lse = lse_ref[hh, 0, :, rows]
            dots = jnp.transpose(do.astype(F32) * att_ref[hh, rows, :].astype(F32))
            dot = jnp.sum(dots, axis=0, keepdims=True)
            dq = jnp.zeros((HEAD_DIM, QROWS), F32)
            for n in range(b + 2):
                span = slice(n * QROWS, (n + 1) * QROWS)
                if n <= b:
                    k, v = qkv_ref[1, hh, span, :], qkv_ref[2, hh, span, :]
                else:
                    k, v = kmem_ref[hh, b], vmem_ref[hh, b]
                s = nt(k, q)
                if n == b:
                    s = masked(s, start)
                share = jnp.exp2(s * scale - lse)
                ds = (share * (nt(v, do) - dot)).astype(BF)
                if n <= b:
                    dv_ref[span, :] += nn(share.astype(BF), do)
                    dk_ref[span, :] += nn(ds, q)
                dq = dq + tn(k, ds)
            g_ref[0, hh, rows, :] = unturn(jnp.transpose(dq) * plain, rows).astype(BF)

        def finish(rows):
            g_ref[1, hh, rows, :] = unturn(dk_ref[rows, :] * plain, rows).astype(BF)
            g_ref[2, hh, rows, :] = dv_ref[rows, :].astype(BF)

        chunks(tokens, finish)
        return carry

    @pl.when(step < steps)
    def _():
        def grad_attended(rows):
            value = nn(gmix_ref[rows, :], pair(wo_ref, model)).astype(BF)
            gatt_ref[0, rows, :] = value[:, :LANES]
            gatt_ref[1, rows, :] = value[:, LANES:]

        chunks(tokens, grad_attended, tokens)

    sums.advance(step, store)
    if nz:
        late.advance(step + 1, store_late, taken=True)

    @pl.when(step < steps)
    def _():
        lax.fori_loop(0, 2, one_head, 0)
        slot = step % 2

        def weights(rows):
            n1t = n1t_ref[rows, :]
            for p in range(3):
                value = nn(n1t, jnp.concatenate([g_ref[p, 0], g_ref[p, 1]], axis=1))
                split_store(me, value.astype(BF), sums.mine, sums.other, (slot, p, rows))
            value = nn(gmixt_ref[rows, :], jnp.concatenate([att_ref[0], att_ref[1]], axis=1))
            split_store(me, value.astype(BF), sums.mine, sums.other, (slot, 3, rows))

        chunks(model, weights, model)
        sums.start(step)

        def inward(rows):
            total = dn_ref[rows, :]
            for p, ref in enumerate((wq_ref, wk_ref, wv_ref)):
                g = jnp.concatenate([g_ref[p, 0, rows, :], g_ref[p, 1, rows, :]], axis=1)
                total = total + nt(g, pair(ref, model))
            dn_ref[rows, :] = total

        chunks(tokens, inward, tokens)

    @pl.when(step == (steps if nz else steps - 1))
    def _():
        def finish(rows, carry):
            normal, inverse = normal_of(features(x_ref, rows).astype(F32))
            dn = dn_ref[rows, :]
            value = (ghid_ref[rows, :] + norm_back(normal, inverse, gain_ref[...], dn)).astype(BF)
            result_ref[0, rows, :] = value[:, :half]
            result_ref[1, rows, :] = value[:, half:]
            return carry + jnp.sum(dn * normal, axis=0, keepdims=True)

        gn1 = lax.fori_loop(
            0,
            tokens // CHUNK,
            lambda i, c: finish(pl.ds(pl.multiple_of(i * CHUNK, CHUNK), CHUNK), c),
            jnp.zeros((1, model), F32),
        )
        for copy in copies:
            copy.start()
        if not nz:
            gn1_ref[...] = gn1
            return
        row = lax.broadcasted_iota(jnp.int32, (8, model), 0)
        norms.start(jnp.where(row == 0, gn1, jnp.where(row == 1, gn2_ref[...], 0.0)))

    if nz:

        @pl.when(step == steps + 1)
        def _():
            norms.after_plane()

        @pl.when(step == steps + 2)
        def _():
            norms_ref[...] = norms.result()

        @pl.when(step == pl.num_programs(0) - 1)
        def _():
            for copy in copies:
                copy.wait()


def back(starts, qkv, kmem, vmem, attended, lse, first, narrow, x, gain, ghid, gn2, cosine, sine, nz, *left):
    halves, tokens, half = x.shape
    model = halves * half
    groups, _, rows, _ = first.shape
    steps = half // HEAD_DIM
    memory = kmem.shape[2]
    now = lambda j: jnp.minimum(j, steps - 1)
    tile = lambda at: pl.BlockSpec(
        (groups, halves, rows, LANES), lambda j: (0, 0, 0, at // LANES + now(j))
    )
    chosen = pl.BlockSpec((halves, QBLKS, memory, HEAD_DIM), lambda j: (0, 0, 0, now(j)))
    big = lambda dtype: pltpu.VMEM((tokens, model), dtype)
    last = Sums.last(True)
    dma = pltpu.SemaphoreType.DMA((1,))
    if nz:
        out_specs = [
            HBM,
            pl.BlockSpec((4, rows, LANES), lambda j: (0, 0, jnp.clip(j - last, 0, steps - 1))),
            pl.BlockSpec((3, rows, LANES), lambda j: (0, 0, jnp.clip(j - 3, 0, LATE - 1))),
            once((8, LANES)),
        ]
        out_shape = [
            jax.ShapeDtypeStruct((halves * tokens, half), BF),
            jax.ShapeDtypeStruct((4, rows, half), F32),
            jax.ShapeDtypeStruct((3, rows, LATE * LANES), F32),
            jax.ShapeDtypeStruct((8, LANES), F32),
        ]
        more = (
            [pltpu.VMEM(x.shape, BF), dma, dma, dma]
            + Sums.scratch(4, model, steps, nz, True)
            + Sums.scratch(3, model, LATE, nz, True, True)
            + Norms.scratch(model, nz)
        )
        left_spec = [pl.BlockSpec((3, model, LANES), lambda j: (0, 0, jnp.minimum(j, LATE - 1)))]
    else:
        grads = pl.BlockSpec((4, model, LANES), lambda j: (0, 0, j))
        out_specs = [once(x.shape), grads, grads, once(gain.shape)]
        grads = jax.ShapeDtypeStruct((4, model, half), BF)
        out_shape = [jax.ShapeDtypeStruct(x.shape, BF), grads, grads]
        out_shape.append(jax.ShapeDtypeStruct(gain.shape, F32))
        more = []
        left_spec = []
    return pl.pallas_call(
        functools.partial(back_kernel, nz, steps),
        grid=(steps + last if nz else steps,),
        in_specs=[
            pl.BlockSpec(memory_space=pltpu.SMEM),
            pl.BlockSpec((3, halves, tokens, HEAD_DIM), lambda j: (0, 0, 0, now(j))),
            chosen,
            chosen,
            pl.BlockSpec((halves, tokens, HEAD_DIM), lambda j: (0, 0, now(j))),
            pl.BlockSpec((halves, 1, 1, tokens), lambda j: (0, now(j), 0, 0)),
            tile(0),
            tile(0),
            tile(half),
            tile(2 * half),
            once(x.shape),
            once(gain.shape),
            once(ghid.shape),
            once(gain.shape),
            once(cosine.shape),
            once(sine.shape),
        ]
        + left_spec,
        out_specs=out_specs,
        out_shape=out_shape,
        scratch_shapes=[big(BF), big(BF), big(BF), big(F32)]
        + [
            pltpu.VMEM((halves, tokens, HEAD_DIM), BF),
            pltpu.VMEM((3, halves, tokens, HEAD_DIM), BF),
            pltpu.VMEM((tokens, HEAD_DIM), F32),
            pltpu.VMEM((tokens, HEAD_DIM), F32),
        ]
        + more,
        compiler_params=comm_params(2) if nz else params(),
        name="back",
    )(
        starts,
        qkv,
        kmem,
        vmem,
        attended,
        lse,
        narrow,
        first,
        first,
        first,
        x,
        gain,
        ghid,
        gn2,
        cosine,
        sine,
        *left,
    )


def swap(value):
    return lax.ppermute(value, "row", [(0, 1), (1, 0)])


def in_order(mine, got, me):
    return jnp.where(me == 0, jnp.stack([mine, got]), jnp.stack([got, mine]))


def own_sequence(value, me):
    take = lambda i: lax.dynamic_index_in_dim(value, i, 0, keepdims=False)
    return in_order(take(me), swap(take(1 - me)), me)


def own_features(value, me):
    return own_sequence(value, me).reshape(-1, value.shape[2])


def summed(mine, other):
    total = mine.astype(F32) + swap(other).astype(F32)
    return lax.psum_scatter(total, ("dp", "col"), scatter_dimension=1, tiled=True)


def on_device(
    inputs,
    w_query,
    w_key,
    w_value,
    w_out,
    w_gate,
    w_up,
    w_down,
    norm_one,
    norm_two,
    cache_keys,
    cache_values,
    own_index,
    partner_index,
    picture_start,
    partner_seq,
    cotangent,
):
    me = lax.axis_index("row")
    nz = lax.axis_size("col")
    chips = lax.axis_size("dp") * nz
    half = inputs.shape[1]
    model = 2 * half
    units = w_gate.shape[1]
    rows = w_query.shape[0]

    gains = jnp.pad(jnp.stack([norm_one, norm_two], axis=1), ((0, 0), (0, LANES - 2)))
    first = jnp.concatenate([w_query, w_key, w_value, gains], axis=1)
    narrow = jnp.concatenate([w_out.T, w_down.T], axis=1)
    wide = jnp.concatenate([w_gate, w_up], axis=1)
    tokens = inputs.reshape(SEQ_DEV, SEQ_LEN, half)
    upstream = cotangent.reshape(SEQ_DEV, SEQ_LEN, half)
    lines = lax.axis_size("dp") == 4 and nz * rows == 2 * LANES and rows * 2 == LANES
    if lines:
        first, narrow, wide, x, cot, qkv, attended, kmem, vmem, lse, cosine, sine = begin(
            own_index,
            partner_index,
            picture_start,
            partner_seq,
            first,
            narrow,
            wide,
            tokens,
            upstream,
            cache_keys,
            cache_values,
            nz,
        )
    else:
        spread = lambda w: lax.all_gather(w, ("dp", "col", "row"), axis=0, tiled=True)
        first, narrow, wide = spread(first), spread(narrow), spread(wide)
        x, cot = own_sequence(tokens, me), own_sequence(upstream, me)
        near = own_sequence(jnp.concatenate([cache_keys, cache_values], axis=1), me)
        far = lax.all_gather(near, "dp", axis=0)
        cosine, sine = rotary_tables()
        pick = lambda table: lax.dynamic_index_in_dim(table, me, 0, keepdims=False).reshape(-1)
        source = lax.dynamic_index_in_dim(partner_seq, me, 0) // SEQ_DEV // nz
        idx = jnp.concatenate([pick(own_index), pick(partner_index), pick(picture_start), source])
    first, narrow, wide = [w.reshape(chips, 2, rows, -1) for w in (first, narrow, wide)]
    gains = first[:, 0, :, 3 * half : 3 * half + 2].reshape(model, 2).astype(F32)
    gain_one, gain_two = gains[:, 0].reshape(1, model), gains[:, 1].reshape(1, model)
    if not lines:
        qkv = project_qkv(x, gain_one, first, cosine, sine)
        attended, lse, kmem, vmem = attend(idx, qkv, near, far)
    hops = nz if lines else 0
    ghid, gn2, *fed = feed(
        x, attended, cot, gain_two, narrow, wide, units, hops
    )
    left = fed[2:] if lines else []
    backed = back(
        picture_start,
        qkv,
        kmem,
        vmem,
        attended,
        lse,
        first,
        narrow,
        x,
        gain_one,
        ghid,
        gn2,
        cosine,
        sine,
        hops,
        *left,
    )
    if lines:
        out, feed_grads, _ = fed
        input_grad, model_grads, late, norms = backed
        feed_grads = jnp.concatenate([feed_grads, late], axis=2)
        norms = lax.dynamic_slice_in_dim(norms[:2], lax.axis_index("col") % 2 * rows, rows, 1).T
    else:
        out, input_grad = own_features(fed[0], me), own_features(backed[0], me)
        feed_grads, model_grads = summed(*fed[1:]), summed(*backed[1:3])
        norms = jnp.concatenate([backed[3], gn2], axis=0).T
        norms = lax.psum_scatter(norms, ("dp", "col"), scatter_dimension=0, tiled=True)
        norms = lax.psum(norms, "row")
    return (
        out,
        input_grad,
        model_grads[0],
        model_grads[1],
        model_grads[2],
        model_grads[3].T,
        feed_grads[0],
        feed_grads[1],
        feed_grads[2].T,
        norms[:, 0],
        norms[:, 1],
    )


def solution(mesh):
    tokens = P(("dp", "col"), "row")
    down = P("row", ("dp", "col"))
    gain = P(("dp", "col"))
    cache = P(("dp", "col"), None, "row")
    index = P(("dp", "col"), None, None)
    weights = (tokens, tokens, tokens, down, tokens, tokens, down)
    return jax.shard_map(
        on_device,
        mesh=mesh,
        in_specs=(tokens,)
        + weights
        + (gain, gain, cache, cache, index, index, P(("dp", "col"), None), gain, tokens),
        out_specs=(tokens, tokens) + weights + (gain, gain),
        check_vma=False,
    )
```

```python
import functools
import math

import jax
import jax.numpy as jnp
from jax import lax
from jax.experimental import pallas as pl
from jax.experimental.pallas import tpu as pltpu
from jax.sharding import PartitionSpec as P

HEAD_DIM = 128
SEQ_LEN = 1024
QROWS = 512
PIC = 256
MEM_BLK = 128
OWN_K = 2
PART_K = 2
SEQ_DEV = 2
QBLKS = 2
EPSILON = 1e-05
NEG = -1e30
CHUNK = 256
LANES = 128

BF = jnp.bfloat16
F32 = jnp.float32
LATE = 2
LOG2E = math.log2(math.e)
MESH = pl.DeviceIdType.MESH


def nn(a, b):
    return jnp.dot(a, b, preferred_element_type=F32)


def nt(a, b):
    return lax.dot_general(a, b, (((1,), (1,)), ((), ())), preferred_element_type=F32)


def tn(a, b):
    return lax.dot_general(a, b, (((0,), (0,)), ((), ())), preferred_element_type=F32)


def rotary_tables():
    half = HEAD_DIM // 2
    frequency = 10000.0 ** (-2.0 * jnp.arange(half, dtype=F32) / HEAD_DIM)
    angles = jnp.arange(SEQ_LEN, dtype=jnp.int32).astype(F32)[:, None] * frequency[None, :]
    cosine, sine = jnp.cos(angles), jnp.sin(angles)
    return jnp.concatenate([cosine, cosine], axis=1), jnp.concatenate([-sine, sine], axis=1)


def whole(shape):
    return pl.BlockSpec(shape, lambda *_: (0,) * len(shape))


def once(shape):
    return pl.BlockSpec(shape, lambda *_: (0,) * len(shape), pipeline_mode=pl.Buffered(1))


def params(limit=60):
    return pltpu.CompilerParams(
        vmem_limit_bytes=limit * 1024 * 1024
    )


def chunks(total, body, size=CHUNK):
    def step(i, carry):
        body(pl.ds(pl.multiple_of(i * size, size), size))
        return carry

    if total == size:
        body(pl.ds(0, size))
    else:
        lax.fori_loop(0, total // size, step, 0)


class Place:
    def __init__(self, nz):
        dp, self.me, self.z = lax.axis_index("dp"), lax.axis_index("row"), lax.axis_index("col")
        self.x, self.y, self.nz = dp % 2, dp // 2, nz
        self.core = (dp, 1 - self.me, self.z)
        self.next_x = (self.y * 2 + 1 - self.x, self.me, self.z)
        self.next_y = ((1 - self.y) * 2 + self.x, self.me, self.z)
        self.above = (dp, self.me, lax.rem(self.z + 1, nz))
        self.below = (dp, self.me, lax.rem(self.z + nz - 1, nz))
        self.has_above = self.z < nz - 1
        self.has_below = self.z > 0

    def corner(self):
        return ((1 - self.y) * 2 + 1 - self.x, self.me, self.z)

    def level(self, by):
        return (self.y * 2 + self.x, self.me, lax.rem(self.z + by, self.nz))

    def levels(self):
        return [self.level(by) for by in range(1, self.nz)]

    def plane(self):
        devices = []
        for by in range(1, 8):
            place = lax.rem(self.y * 4 + self.x * 2 + self.me + by, 8)
            devices.append((place // 2, place % 2, self.z))
        return devices

    def barrier(self, devices):
        semaphore = pltpu.get_barrier_semaphore()
        for device in devices:
            pl.semaphore_signal(semaphore, inc=1, device_id=device, device_id_type=MESH)
        pl.semaphore_wait(semaphore, len(devices))


def remote(source, target, sent, arrived, device):
    return pltpu.make_async_remote_copy(
        src_ref=source,
        dst_ref=target,
        send_sem=sent,
        recv_sem=arrived,
        device_id=device,
        device_id_type=MESH,
    )


def comm_params(number, limit=60):
    return pltpu.CompilerParams(
        vmem_limit_bytes=limit * 1024 * 1024, collective_id=number, has_side_effects=True
    )


HBM = pl.BlockSpec(memory_space=pl.ANY)


class Sent:
    def __init__(self):
        self.copies = []

    def go(self, copy, when=None):
        if when is None:
            copy.start()
        else:
            pl.when(when)(copy.start)
        self.copies.append((when, copy))

    def wait(self):
        for when, copy in self.copies:
            copy.wait_send() if when is None else pl.when(when)(copy.wait_send)


class Spread:
    BUFFERS = 6

    @staticmethod
    def scratch(nz):
        dma = pltpu.SemaphoreType.DMA
        return [dma((4, nz)), dma((4, nz)), dma((2, 5, nz)), dma((5, nz)), dma((nz,)), dma((nz,))]

    def __init__(self, at, sent, source, target, refs):
        self.at, self.sent, self.target = at, sent, target
        self.source = self.own() if source is None else source
        self.part = target.shape[-2] // 2
        (
            self.flat_sent,
            self.flat_arrived,
            self.line_sent,
            self.line_arrived,
            self.core_sent,
            self.core_arrived,
        ) = refs

    def block(self, place, zz, core=None):
        at = self.at
        y = at.y if place < 2 else 1 - at.y
        x = at.x if place in (0, 2) else 1 - at.x
        ref = self.target.at[y, x, zz, at.me if core is None else core]
        if place >= 3:
            ref = ref.at[pl.ds((place - 3) * self.part, self.part)]
        return ref

    def half(self, place, zz, piece):
        return self.block(place, zz).at[pl.ds(piece * self.part, self.part)]

    def own(self):
        return self.target.at[self.at.y, self.at.x, self.at.z, self.at.me]

    def flat(self, source, target, index, zz, device):
        return remote(source, target, self.flat_sent.at[index, zz], self.flat_arrived.at[index, zz], device)

    def sides(self, source, zz, when=None):
        target = self.block(0, zz)
        self.sent.go(self.flat(source, target, 0, zz, self.at.next_x), when)
        self.sent.go(self.flat(source, target, 1, zz, self.at.next_y), when)

    def from_side(self, index, zz, when=None):
        at = self.at
        place = 1 + index
        ref = self.block(place, zz)
        copy = self.flat(ref, ref, index, zz, (at.next_x, at.next_y)[index])
        copy.wait_recv() if when is None else pl.when(when)(copy.wait_recv)
        ref = self.half(place, zz, index)
        self.sent.go(self.flat(ref, ref, 2 + index, zz, (at.next_y, at.next_x)[index]), when)

    def from_across(self, index, zz, when=None):
        ref = self.block(3 + index, zz)
        copy = self.flat(ref, ref, 2 + index, zz, (self.at.next_y, self.at.next_x)[index])
        copy.wait_recv() if when is None else pl.when(when)(copy.wait_recv)

    def line(self, source, place, zz, up, when):
        at = self.at
        ref = self.block(place, zz)
        copy = remote(
            ref if source is None else source,
            ref,
            self.line_sent.at[int(up), place, zz],
            self.line_arrived.at[place, zz],
            at.above if up else at.below,
        )
        self.sent.go(copy, (at.has_above if up else at.has_below) & when)

    def both_ways(self, place, source=None):
        for up in (True, False):
            self.line(source, place, self.at.z, up, True)

    def from_line(self, step, up, place, onward):
        at = self.at
        zz = at.z - step if up else at.z + step
        valid = zz >= 0 if up else zz < at.nz
        zz = jnp.clip(zz, 0, at.nz - 1)
        ref = self.block(place, zz)
        copy = remote(
            ref,
            ref,
            self.line_sent.at[int(up), place, zz],
            self.line_arrived.at[place, zz],
            at.below if up else at.above,
        )
        pl.when(valid)(copy.wait_recv)
        self.line(None, place, zz, up, valid)
        if onward:
            self.sides(ref, zz, valid)

    def levels(self, step):
        at = self.at
        if step == 0:
            return [(at.z, None)]
        places = ((at.z - step, at.z >= step), (at.z + step, at.z + step < at.nz))
        return [(jnp.clip(zz, 0, at.nz - 1), valid) for zz, valid in places]

    def hand_copy(self, zz, core):
        ref = self.target.at[:, :, zz, core]
        return remote(ref, ref, self.core_sent.at[zz], self.core_arrived.at[zz], self.at.core)

    def hand_over(self, step):
        for zz, valid in self.levels(step):
            self.sent.go(self.hand_copy(zz, self.at.me), valid)

    def finish(self):
        for zz in range(self.at.nz):
            self.hand_copy(zz, 1 - self.at.me).wait_recv()


    def begin_line(self):
        self.both_ways(0, self.source)

    def begin_sides(self):
        self.sides(self.source, self.at.z)

    def level_sides(self, step):
        for zz, valid in self.levels(step):
            self.sides(self.block(0, zz), zz, valid)

    def sides_at(self, step):
        for zz, valid in self.levels(step):
            for index in range(2):
                self.from_side(index, zz, valid)

    def corners(self, step):
        for zz, valid in self.levels(step):
            for index in range(2):
                self.from_across(index, zz, valid)


    def plane(self, place):
        z = self.at.z
        if place < 3:
            self.from_side(place - 1, z)
        else:
            self.from_across(place - 3, z)
        self.both_ways(place)


def begin_kernel(
    nz,
    own_ref,
    partner_ref,
    starts_ref,
    seq_ref,
    wq_ref,
    wk_ref,
    wv_ref,
    gain_ref,
    wa_ref,
    wg_ref,
    wu_ref,
    x_ref,
    cot_ref,
    ck_ref,
    cv_ref,
    first_ref,
    a_ref,
    b_ref,
    xs_ref,
    cots_ref,
    qkv_ref,
    att_out,
    kmem_out,
    vmem_out,
    lse_ref,
    cos_ref,
    sin_ref,
    all_ref,
    xv_ref,
    n1_ref,
    y_ref,
    cotbuf,
    near_ref,
    far_ref,
    stage_ref,
    kmem_ref,
    vmem_ref,
    att_ref,
    acc_ref,
    shift_ref,
    total_ref,
    wide_ref,
    loaded,
    stored,
    csent,
    carrived,
    far_sent,
    far_arrived,
    far_csent,
    far_carrived,
    *refs,
):
    at = Place(nz)
    me, x, y, z = at.me, at.x, at.y, at.z
    keys = ck_ref.shape[1]
    width = all_ref.shape[-1]
    units = wg_ref.shape[1]
    tokens, model = n1_ref.shape
    half = model // 2
    sent = Sent()
    n = Spread.BUFFERS
    first = Spread(at, sent, None, all_ref, refs[:n])
    late = Spread(at, sent, wa_ref, a_ref, refs[n : 2 * n])
    wide = Spread(at, sent, wide_ref, b_ref, refs[2 * n :])
    span = [pl.ds(0, keys), pl.ds(keys, keys)]
    caches = (ck_ref, cv_ref)

    def local(source, target, semaphore):
        return pltpu.make_async_copy(source, target, semaphore)

    loads = [
        local(source, target, loaded.at[i])
        for i, (source, target) in enumerate(
            (
                (wq_ref, first.own().at[:, pl.ds(0, half)]),
                (x_ref.at[me], xv_ref.at[me]),
                (cot_ref.at[me], cotbuf),
                (ck_ref.at[me], near_ref.at[me, span[0]]),
                (cv_ref.at[me], near_ref.at[me, span[1]]),
                (wa_ref, late.own()),
                (wk_ref, first.own().at[:, pl.ds(half, half)]),
                (wv_ref, first.own().at[:, pl.ds(2 * half, half)]),
                (gain_ref, first.own().at[:, pl.ds(3 * half, LANES)]),
                (wg_ref, wide_ref.at[:, pl.ds(0, units)]),
                (wu_ref, wide_ref.at[:, pl.ds(units, units)]),
            )
        )
    ]
    stores = [
        local(source, target, stored.at[i])
        for i, (source, target) in enumerate(
            (
                (cotbuf, cots_ref.at[me]),
                (xv_ref, xs_ref),
                (all_ref, first_ref),
                (y_ref, qkv_ref),
                (kmem_ref, kmem_out),
                (vmem_ref, vmem_out),
                (att_ref, att_out),
            )
        )
    ]
    placed = local(wide_ref, wide.own(), stored.at[7])
    for copy in loads:
        copy.start()
    at.barrier([at.core, at.next_x, at.next_y, at.above, at.below])
    exchange = [
        remote(source, target, csent.at[i], carrived.at[i], at.core)
        for i, (source, target) in enumerate(
            (
                (x_ref.at[1 - me], xv_ref.at[me]),
                (ck_ref.at[1 - me], near_ref.at[me, span[0]]),
                (cv_ref.at[1 - me], near_ref.at[me, span[1]]),
                (cot_ref.at[1 - me], cots_ref.at[me]),
            )
        )
    ]

    def landing(source, turn, kv):
        return far_ref.at[source, me, span[kv]] if turn == 0 else stage_ref.at[source, kv]

    def cache_copy(line, turn, kv):
        index = (line, turn * 2 + kv)
        return remote(
            caches[kv].at[me if turn == 0 else 1 - me],
            landing(line, turn, kv),
            far_sent.at[index],
            far_arrived.at[index],
            (at.next_x, at.next_y)[line],
        )

    def corner_copy(turn, kv):
        source, device = (0, at.next_y) if turn == 0 else (1, at.next_x)
        index = (2, turn * 2 + kv)
        return remote(
            landing(source, turn, kv), landing(2, turn, kv), far_sent.at[index], far_arrived.at[index], device
        )

    def hand_over(source, kv):
        return remote(
            stage_ref.at[source, kv],
            far_ref.at[source, me, span[kv]],
            far_csent.at[source, kv],
            far_carrived.at[source, kv],
            at.core,
        )

    def from_lines(spread, step, places, onward):
        for place in places:
            for up in (True, False):
                spread.from_line(step, up, place, onward)


    for i in (0, 6, 7, 8):
        loads[i].wait()
    first.begin_line()
    first.begin_sides()
    late.begin_line()
    for i in (9, 10):
        loads[i].wait()
    placed.start()
    wide.begin_line()
    wide.begin_sides()
    sent.go(exchange[0])

    place_in = lax.broadcasted_iota(jnp.int32, (tokens, HEAD_DIM), 0).astype(F32)
    lane = lax.broadcasted_iota(jnp.int32, (1, HEAD_DIM), 1)
    turns = lax.rem(lane, HEAD_DIM // 2).astype(F32) * (-2.0 * math.log(10000.0) / HEAD_DIM)
    angles = place_in * jnp.exp(turns)
    cos_ref[...] = jnp.cos(angles)
    sin_ref[...] = jnp.where(lane < HEAD_DIM // 2, -1.0, 1.0) * jnp.sin(angles)

    from_lines(first, 1, (0,), True)
    wide.plane(1)
    wide.plane(2)
    first.sides_at(0)
    from_lines(first, 2, (0,), True)
    from_lines(late, 1, (0,), False)
    wide.plane(3)
    wide.plane(4)
    placed.wait()
    wide.hand_over(0)
    first.sides_at(1)
    for kv in range(2):
        sent.go(cache_copy(0, 0, kv))
        sent.go(cache_copy(1, 1, kv))
    from_lines(first, 3, (0,), True)
    from_lines(late, 2, (0,), False)
    first.sides_at(2)
    for kv in range(2):
        sent.go(cache_copy(0, 1, kv))
        sent.go(cache_copy(1, 0, kv))
    for copy in exchange[1:]:
        sent.go(copy)
    first.sides_at(3)
    from_lines(late, 3, (0,), False)
    from_lines(wide, 1, range(3), False)
    loads[2].wait()
    stores[0].start()
    loads[1].wait()
    exchange[0].wait_recv()
    stores[1].start()
    for step in range(nz):
        first.corners(step)
        first.hand_over(step)
    first.finish()
    stores[2].start()
    from_lines(wide, 1, range(3, 5), False)
    wide.hand_over(1)

    gains = all_ref[:, :, :, 0, :, pl.ds(width - LANES, LANES)].reshape(model, LANES).astype(F32)
    gain = jnp.transpose(gains)[0:1, :]

    def norm(rows):
        normal, _ = normal_of(features(xv_ref, rows).astype(F32))
        n1_ref[rows, :] = (normal * gain).astype(BF)

    chunks(tokens, norm)

    def project(i, carry):
        m, h = i // 2, i % 2
        lanes = pl.ds(pl.multiple_of(m * half, half), half)
        value = nn(n1_ref[...], all_ref[:, :, :, h, :, lanes].reshape(model, half))
        for head in range(half // HEAD_DIM):
            lanes = slice(head * HEAD_DIM, (head + 1) * HEAD_DIM)
            u = value[:, lanes]
            turned = u * cos_ref[...] + pltpu.roll(u, HEAD_DIM // 2, 1) * sin_ref[...]
            y_ref[m, h, :, lanes] = jnp.where(m < 2, turned, u).astype(BF)
        return carry

    lax.fori_loop(0, 6, project, 0)
    stores[3].start()


    for kv in range(2):
        cache_copy(0, 0, kv).wait_recv()
        sent.go(corner_copy(0, kv))
        cache_copy(1, 1, kv).wait_recv()
        sent.go(corner_copy(1, kv))
        sent.go(hand_over(1, kv))
    late.begin_sides()
    for step in range(1, nz):
        late.level_sides(step)
    for copy in loads[3:5]:
        copy.wait()
    for copy in exchange[1:3]:
        copy.wait_recv()

    def choose(index_ref, first_row):
        for b in range(QBLKS):
            for j in range(OWN_K):
                index = index_ref[me, b, j]
                rows = pl.ds(first_row + j * MEM_BLK, MEM_BLK)
                for h in range(2):
                    for offset, ref in ((0, kmem_ref), (keys, vmem_ref)):
                        block = near_ref[h, pl.ds(offset, MEM_BLK), :]
                        for c in range(1, keys // MEM_BLK):
                            other = near_ref[h, pl.ds(offset + c * MEM_BLK, MEM_BLK), :]
                            block = jnp.where(index == c, other, block)
                        ref[h, b, rows, :] = block

    choose(own_ref, 0)
    heads = half // HEAD_DIM
    near_rows = slice(0, OWN_K * MEM_BLK)
    far_rows = slice(OWN_K * MEM_BLK, (OWN_K + PART_K) * MEM_BLK)

    def place(i):
        h, column = i // heads, i % heads
        return h, column, pl.ds(pl.multiple_of(column * HEAD_DIM, HEAD_DIM), HEAD_DIM)

    def without_partner(i, carry):
        h, column, lanes = place(i)

        def store(rows, shift, total, acc):
            acc_ref[i, :, rows] = acc
            shift_ref[i, :, rows] = shift
            total_ref[i, :, rows] = total

        attend_head(
            lambda m, rows: y_ref[m, h, rows, lanes],
            lambda b: (kmem_ref[h, b, near_rows, lanes], vmem_ref[h, b, near_rows, lanes]),
            [starts_ref[me, b] for b in range(QBLKS)],
            store,
        )
        return carry

    def with_partner(i, carry):
        h, column, lanes = place(i)
        for b in range(QBLKS):
            rows = pl.ds(b * QROWS, QROWS)
            shift, total, acc = attend_rows(
                [(kmem_ref[h, b, far_rows, lanes], vmem_ref[h, b, far_rows, lanes], None)],
                y_ref[0, h, rows, lanes],
            )
            before = shift_ref[i, :, rows]
            top = jnp.maximum(shift, before)
            now, then = jnp.exp2(shift - top), jnp.exp2(before - top)
            total = total * now + total_ref[i, :, rows] * then
            acc = acc * now + acc_ref[i, :, rows] * then
            att_ref[h, rows, lanes] = jnp.transpose(acc / total).astype(BF)
            lse_ref[h, column, :, rows] = top + jnp.log2(total)
        return carry

    lax.fori_loop(0, heads, without_partner, 0)
    from_lines(wide, 2, range(3), False)
    for kv in range(2):
        cache_copy(0, 1, kv).wait_recv()
        sent.go(hand_over(0, kv))
        cache_copy(1, 0, kv).wait_recv()
    lax.fori_loop(heads, 2 * heads, without_partner, 0)
    from_lines(wide, 2, range(3, 5), False)
    wide.hand_over(2)
    late.sides_at(0)
    for kv in range(2):
        corner_copy(1, kv).wait_recv()
        sent.go(hand_over(2, kv))
        corner_copy(0, kv).wait_recv()
    for source in range(3):
        for kv in range(2):
            remote(
                stage_ref.at[source, kv],
                far_ref.at[source, 1 - me, span[kv]],
                far_csent.at[source, kv],
                far_carrived.at[source, kv],
                at.core,
            ).wait_recv()
    source = seq_ref[me]
    across = (1 - y) * 2 + 1 - x
    near_y = (1 - y) * 2 + x
    at_most = SEQ_DEV * nz

    def comes_from(place):
        return (source >= place * at_most) & (source < (place + 1) * at_most)

    def take(i, carry):
        rows = pl.ds(pl.multiple_of(i * MEM_BLK, MEM_BLK), MEM_BLK)
        for h in range(2):
            block = jnp.where(comes_from(near_y), far_ref[1, h, rows, :], far_ref[0, h, rows, :])
            near_ref[h, rows, :] = jnp.where(comes_from(across), far_ref[2, h, rows, :], block)
        return carry

    lax.fori_loop(0, 2 * keys // MEM_BLK, take, 0)
    choose(partner_ref, OWN_K * MEM_BLK)
    stores[4].start()
    stores[5].start()
    lax.fori_loop(0, 2 * heads, with_partner, 0)
    stores[6].start()
    late.sides_at(1)
    loads[5].wait()
    late.corners(0)
    late.hand_over(0)
    from_lines(wide, 3, range(5), False)
    wide.hand_over(3)
    late.sides_at(2)
    late.corners(1)
    late.hand_over(1)
    late.sides_at(3)
    for step in range(2, nz):
        late.corners(step)
        late.hand_over(step)
    late.finish()
    wide.finish()
    exchange[3].wait_recv()
    for copy in stores:
        copy.wait()
    sent.wait()


def begin(own, partner, starts, seq, wq, wk, wv, gains, wa, wg, wu, x, cot, cache_keys, cache_values, nz):
    dma = pltpu.SemaphoreType.DMA
    _, tokens, half = x.shape
    keys = cache_keys.shape[1]
    full = jax.ShapeDtypeStruct((2, tokens, half), BF)
    rows, units = wg.shape
    gathered = lambda width: (2, 2, nz, 2, rows, width)
    whole_array = lambda width: jax.ShapeDtypeStruct(gathered(width), BF)
    first = 3 * half + LANES
    vmem = pl.BlockSpec(memory_space=pltpu.VMEM)
    table = jax.ShapeDtypeStruct((tokens, HEAD_DIM), F32)
    heads = 2 * half // HEAD_DIM
    memory = (2, QBLKS, (OWN_K + PART_K) * MEM_BLK, half)
    return pl.pallas_call(
        functools.partial(begin_kernel, nz),
        in_specs=[pl.BlockSpec(memory_space=pltpu.SMEM)] * 4 + [HBM] * 11,
        out_specs=[HBM] * 9 + [vmem] * 3,
        out_shape=[
            whole_array(first),
            whole_array(wa.shape[1]),
            whole_array(2 * units),
            full,
            full,
            jax.ShapeDtypeStruct((3, 2, tokens, half), BF),
            full,
            jax.ShapeDtypeStruct(memory, BF),
            jax.ShapeDtypeStruct(memory, BF),
            jax.ShapeDtypeStruct((2, half // HEAD_DIM, 1, tokens), F32),
            table,
            table,
        ],
        scratch_shapes=[
            pltpu.VMEM(gathered(first), BF),
            pltpu.VMEM((2, tokens, half), BF),
            pltpu.VMEM((tokens, 2 * half), BF),
            pltpu.VMEM((3, 2, tokens, half), BF),
            pltpu.VMEM((tokens, half), BF),
            pltpu.VMEM((2, 2 * keys, half), BF),
            pltpu.VMEM((3, 2, 2 * keys, half), BF),
            pltpu.VMEM((3, 2, keys, half), BF),
            pltpu.VMEM(memory, BF),
            pltpu.VMEM(memory, BF),
            pltpu.VMEM((2, tokens, half), BF),
            pltpu.VMEM((heads, HEAD_DIM, tokens), F32),
            pltpu.VMEM((heads, 1, tokens), F32),
            pltpu.VMEM((heads, 1, tokens), F32),
            pltpu.VMEM((rows, 2 * units), BF),
            dma((11,)),
            dma((8,)),
            dma((4,)),
            dma((4,)),
            dma((3, 4)),
            dma((3, 4)),
            dma((3, 2)),
            dma((3, 2)),
        ]
        + Spread.scratch(nz) * 3,
        compiler_params=comm_params(0),
        name="begin",
    )(own, partner, starts, seq, wq, wk, wv, gains, wa, wg, wu, x, cot, cache_keys, cache_values)


class Sums:
    BUFFERS = 10

    @staticmethod
    def last(halved):
        return 4 if halved else 3

    @staticmethod
    def scratch(parts, rows, tiles, nz, halved, taken=False):
        dma = pltpu.SemaphoreType.DMA
        slab = rows // 4
        pairs = pltpu.VMEM((1, 1, 16, LANES) if taken else (2, parts, rows, LANES), BF)
        return [
            pairs,
            pairs,
            pltpu.VMEM((tiles, parts, rows, LANES), BF),
            pltpu.VMEM((tiles, 2, parts, slab // 2, LANES) if halved else (tiles, 1, parts, slab, LANES), BF),
            pltpu.VMEM((tiles, 2, parts, slab, LANES), BF),
            pltpu.VMEM((tiles, nz - 1, parts, slab // nz, LANES), BF),
            dma((tiles, 5)),
            dma((tiles, 5)),
            dma((tiles, nz - 1)),
            dma((tiles, nz - 1)),
        ]

    def __init__(self, at, halved, refs, left=0):
        (
            self.mine,
            self.other,
            self.total,
            self.diag,
            self.side,
            self.hop,
            self.sent,
            self.arrived,
            self.hop_sent,
            self.hop_arrived,
        ) = refs
        self.at, self.halved = at, halved
        self.tiles, _, self.rows, _ = self.total.shape
        self.left, self.early = left, self.tiles - left
        self.slab = self.rows // 4
        self.block = self.slab // at.nz

    def span(self, y, x, first=0, size=None):
        start = pl.multiple_of((y * 2 + x) * self.slab + first, self.block)
        return pl.ds(start, self.slab if size is None else size)

    def copy(self, j, span, target, index, device):
        return remote(
            self.total.at[j, :, span], target, self.sent.at[j, index], self.arrived.at[j, index], device
        )

    def core_copy(self, j):
        return remote(
            self.other.at[j % 2],
            self.total.at[j],
            self.sent.at[j, 0],
            self.arrived.at[j, 0],
            self.at.core,
        )

    def diag_copies(self, j):
        at, part = self.at, self.slab // 2
        y, x = 1 - at.y, 1 - at.x
        if not self.halved:
            return [self.copy(j, self.span(y, x), self.diag.at[j, 0], 1, at.corner())]
        return [
            self.copy(j, self.span(y, x, i * part, part), self.diag.at[j, i], 1 + i, device)
            for i, device in enumerate((at.next_x, at.next_y))
        ]

    def side_copies(self, j):
        at = self.at
        return [
            self.copy(j, self.span(at.y, 1 - at.x), self.side.at[j, 0], 3, at.next_x),
            self.copy(j, self.span(1 - at.y, at.x), self.side.at[j, 1], 4, at.next_y),
        ]

    def hop_copies(self, j):
        at = self.at
        copies = []
        for by in range(1, at.nz):
            device = at.level(by)
            copies.append(
                remote(
                    self.total.at[j, :, self.span(at.y, at.x, device[2] * self.block, self.block)],
                    self.hop.at[j, by - 1],
                    self.hop_sent.at[j, by - 1],
                    self.hop_arrived.at[j, by - 1],
                    device,
                )
            )
        return copies

    def add(self, j, span, *values):
        total = self.total[j, :, span, :].astype(F32)
        for value in values:
            total = total + value.astype(F32)
        self.total[j, :, span, :] = total.astype(BF)

    def start(self, j):
        self.core_copy(j).start()

    def after_core(self, j):
        self.core_copy(j).wait()

        def body(rows):
            self.add(j, rows, self.mine[j % 2, :, rows, :])

        chunks(self.rows, body)

    def begin(self, j):
        for copy in self.diag_copies(j):
            copy.start()
        if not self.halved:
            for copy in self.side_copies(j):
                copy.start()

    def after_diag(self, j):
        at, part = self.at, self.slab // 2
        for copy in self.diag_copies(j):
            copy.wait()
        self.add(j, self.span(1 - at.y, at.x, 0, part), self.diag[j, 0])
        self.add(j, self.span(at.y, 1 - at.x, part, part), self.diag[j, 1])
        for copy in self.side_copies(j):
            copy.start()

    def after_side(self, j):
        at = self.at
        for copy in self.side_copies(j):
            copy.wait()
        values = [self.side[j, 0], self.side[j, 1]]
        if not self.halved:
            for copy in self.diag_copies(j):
                copy.wait()
            values.append(self.diag[j, 0])
        self.add(j, self.span(at.y, at.x), *values)
        for copy in self.hop_copies(j):
            copy.start()

    def result(self, j):
        at = self.at
        for copy in self.hop_copies(j):
            copy.wait()
        value = self.total[j, :, self.span(at.y, at.x, at.z * self.block, self.block), :].astype(F32)
        for by in range(at.nz - 1):
            value = value + self.hop[j, by].astype(F32)
        return value

    def advance(self, step, store, leave=None, taken=False):
        def on(behind, body, first, last):
            j = step - behind
            pl.when((j >= first) & (j < last))(lambda: body(jnp.clip(j, first, last - 1)))

        def summed(j):
            self.after_core(j)
            self.begin(j)

        def left(j):
            self.after_core(j)
            leave(self.total[j])

        if not taken:
            on(1, summed, 0, self.early)
        if self.left:
            on(1, left, self.early, self.tiles)
        if self.halved:
            on(2, self.after_diag, 0, self.early)
        on(self.last(self.halved) - 1, self.after_side, 0, self.early)
        on(self.last(self.halved), lambda j: store(self.result(j)), 0, self.early)


class Norms:
    BUFFERS = 7

    @staticmethod
    def scratch(model, nz):
        dma = pltpu.SemaphoreType.DMA
        return [
            pltpu.VMEM((4, 8, model // 4), F32),
            pltpu.VMEM((8, 8, model // 4), F32),
            pltpu.VMEM((nz, 8, LANES), F32),
            dma((7,)),
            dma((7,)),
            dma((nz - 1,)),
            dma((nz - 1,)),
        ]

    def __init__(self, at, refs):
        self.at = at
        self.own, self.parts, self.level, self.sent, self.arrived, self.hop_sent, self.hop_arrived = refs

    def plane_copies(self):
        at = self.at
        me = at.y * 4 + at.x * 2 + at.me
        return [
            remote(self.own.at[device[0]], self.parts.at[me], self.sent.at[i], self.arrived.at[i], device)
            for i, device in enumerate(at.plane())
        ]

    def hop_copies(self):
        at = self.at
        me = at.y * 4 + at.x * 2 + at.me
        copies = []
        for by in range(1, at.nz):
            device = at.level(by)
            lanes = pl.ds(pl.multiple_of(device[2] // 2 * LANES, LANES), LANES)
            copies.append(
                remote(
                    self.own.at[0, :, lanes],
                    self.level.at[at.z],
                    self.hop_sent.at[by - 1],
                    self.hop_arrived.at[by - 1],
                    device,
                )
            )
        return copies

    def start(self, rows):
        at = self.at
        width = self.own.shape[2]
        for d in range(4):
            self.own[d] = rows[:, d * width : (d + 1) * width]
        self.parts[at.y * 4 + at.x * 2 + at.me] = self.own[at.y * 2 + at.x]
        for copy in self.plane_copies():
            copy.start()

    def after_plane(self):
        at = self.at
        for copy in self.plane_copies():
            copy.wait()
        total = self.parts[0]
        for i in range(1, 8):
            total = total + self.parts[i]
        self.own[0] = total
        lanes = pl.ds(pl.multiple_of(at.z // 2 * LANES, LANES), LANES)
        self.level[at.z] = self.own[0, :, lanes]
        for copy in self.hop_copies():
            copy.start()

    def result(self):
        for copy in self.hop_copies():
            copy.wait()
        total = self.level[0]
        for i in range(1, self.at.nz):
            total = total + self.level[i]
        return total


class Unsummed:
    class Tile:
        def __init__(self, ref):
            self.ref = ref

        def __setitem__(self, index, value):
            self.ref[index[1:]] = value

    def __init__(self, mine, other):
        self.mine, self.other = Unsummed.Tile(mine), Unsummed.Tile(other)

    def start(self, j):
        pass

    def advance(self, step, store, leave=None):
        pass


def features(ref, rows):
    return jnp.concatenate([ref[0, rows, :], ref[1, rows, :]], axis=1)


def pair(ref, model):
    return jnp.concatenate(
        [ref[:, 0].reshape(model, LANES), ref[:, 1].reshape(model, LANES)], axis=1
    )


def normal_of(x):
    inverse = lax.rsqrt(jnp.mean(x * x, axis=1, keepdims=True) + EPSILON)
    return x * inverse, inverse


def norm_back(normal, inverse, gain, grad):
    scaled = grad * gain
    return inverse * (scaled - normal * jnp.mean(scaled * normal, axis=1, keepdims=True))


def qkv_kernel(x_ref, gain_ref, w_ref, cos_ref, sin_ref, out_ref, n1_ref):
    part = pl.program_id(0)
    tokens, model = n1_ref.shape

    @pl.when((part == 0) & (pl.program_id(1) == 0))
    def _():
        def norm(rows):
            normal, _ = normal_of(features(x_ref, rows).astype(F32))
            n1_ref[rows, :] = (normal * gain_ref[...]).astype(BF)

        chunks(tokens, norm)

    def project(rows):
        y = nn(n1_ref[rows, :], w_ref[...].reshape(model, -1))
        cosine, sine = cos_ref[rows, :], sin_ref[rows, :]
        for h in range(y.shape[1] // HEAD_DIM):
            lanes = slice(h * HEAD_DIM, (h + 1) * HEAD_DIM)
            u = y[:, lanes]
            turned = u * cosine + pltpu.roll(u, HEAD_DIM // 2, 1) * sine
            out_ref[rows, lanes] = jnp.where(part < 2, turned, u).astype(BF)

    chunks(tokens, project, tokens)


def project_qkv(x, gain, gathered, cosine, sine):
    halves, tokens, half = x.shape
    groups, _, rows, _ = gathered.shape
    return pl.pallas_call(
        qkv_kernel,
        grid=(3, halves),
        in_specs=[
            whole(x.shape),
            whole(gain.shape),
            pl.BlockSpec((groups, None, rows, half), lambda m, h: (0, h, 0, m)),
            whole(cosine.shape),
            whole(sine.shape),
        ],
        out_specs=pl.BlockSpec((None, None, tokens, half), lambda m, h: (m, h, 0, 0)),
        out_shape=jax.ShapeDtypeStruct((3, halves, tokens, half), BF),
        scratch_shapes=[pltpu.VMEM((tokens, halves * half), BF)],
        compiler_params=params(),
        name="project_qkv",
    )(x, gain, gathered, cosine, sine)


def fill_memory(idx_ref, near_ref, far_ref, offset, mem_ref):
    for b in range(QBLKS):
        for j in range(OWN_K + PART_K):
            ref, at = (near_ref, b * OWN_K + j) if j < OWN_K else (far_ref, QBLKS * OWN_K + b * PART_K + j - OWN_K)
            start = pl.multiple_of(idx_ref[at] * MEM_BLK, MEM_BLK) + offset
            mem_ref[b, j * MEM_BLK : (j + 1) * MEM_BLK, :] = ref[pl.ds(start, MEM_BLK), :]


def masked(scores, start):
    keys, queries = scores.shape
    at = lax.broadcasted_iota(jnp.int32, (1, queries), 1)
    limit = jnp.where((at >= start) & (at < start + PIC), start + PIC - 1, at)
    key = lax.broadcasted_iota(jnp.int32, (keys, queries), 0)
    return jnp.where(key <= limit, scores, NEG)


SCALE = LOG2E / math.sqrt(HEAD_DIM)


def attend_rows(parts, q):
    scores = []
    for keys, values, mask in parts:
        s = nt(keys, q)
        scores.append((s if mask is None else masked(s, *mask), values))
    top = functools.reduce(jnp.maximum, [jnp.max(s, axis=0, keepdims=True) for s, _ in scores])
    shift = top * SCALE
    total = jnp.zeros_like(top)
    acc = jnp.zeros((HEAD_DIM, q.shape[0]), F32)
    for s, values in scores:
        e = jnp.exp2(s * SCALE - shift)
        total = total + jnp.sum(e, axis=0, keepdims=True)
        acc = acc + tn(values, e.astype(BF))
    return shift, total, acc


def attend_head(part, memory, starts, store):
    for b in range(QBLKS):
        rows = slice(b * QROWS, (b + 1) * QROWS)
        parts = []
        for n in range(b + 1):
            span = slice(n * QROWS, (n + 1) * QROWS)
            mask = (starts[b] - b * QROWS,) if n == b else None
            parts.append((part(1, span), part(2, span), mask))
        parts.append(memory(b) + (None,))
        store(rows, *attend_rows(parts, part(0, rows)))


def attend_kernel(
    idx_ref, q_ref, k_ref, v_ref, near_ref, far_ref, out_ref, lse_ref, kmem_ref, vmem_ref
):
    keys = near_ref.shape[0] // 2
    fill_memory(idx_ref, near_ref, far_ref, 0, kmem_ref)
    fill_memory(idx_ref, near_ref, far_ref, keys, vmem_ref)
    refs = (q_ref, k_ref, v_ref)

    def store(rows, shift, total, acc):
        out_ref[rows, :] = jnp.transpose(acc / total).astype(BF)
        lse_ref[:, rows] = shift + jnp.log2(total)

    attend_head(
        lambda m, rows: refs[m][rows, :],
        lambda b: (kmem_ref[b], vmem_ref[b]),
        [idx_ref[QBLKS * (OWN_K + PART_K) + b] for b in range(QBLKS)],
        store,
    )


def attend(idx, qkv, near, far):
    _, halves, tokens, half = qkv.shape
    here = half // HEAD_DIM
    cached = near.shape[1]
    memory = (OWN_K + PART_K) * MEM_BLK
    column = lambda m: pl.BlockSpec(
        (None, None, tokens, HEAD_DIM), lambda h, idx: (m, h // here, 0, h % here)
    )
    cache = pl.BlockSpec((None, cached, HEAD_DIM), lambda h, idx: (h // here, 0, h % here))
    which = QBLKS * (OWN_K + PART_K) + QBLKS
    partner = pl.BlockSpec(
        (None, None, cached, HEAD_DIM), lambda h, idx: (idx[which], h // here, 0, h % here)
    )
    chosen = pl.BlockSpec((None, QBLKS, memory, HEAD_DIM), lambda h, idx: (h // here, 0, 0, h % here))
    chosen_shape = jax.ShapeDtypeStruct((halves, QBLKS, memory, half), BF)
    return pl.pallas_call(
        attend_kernel,
        grid_spec=pltpu.PrefetchScalarGridSpec(
            num_scalar_prefetch=1,
            grid=(halves * here,),
            in_specs=[column(0), column(1), column(2), cache, partner],
            out_specs=[
                pl.BlockSpec((None, tokens, HEAD_DIM), lambda h, idx: (h // here, 0, h % here)),
                pl.BlockSpec((None, None, 1, tokens), lambda h, idx: (h // here, h % here, 0, 0)),
                chosen,
                chosen,
            ],
        ),
        out_shape=[
            jax.ShapeDtypeStruct((halves, tokens, half), BF),
            jax.ShapeDtypeStruct((halves, here, 1, tokens), F32),
            chosen_shape,
            chosen_shape,
        ],
        compiler_params=params(),
        name="attend",
    )(idx, qkv, qkv, qkv, near, far)


def split_store(me, value, mine_ref, other_ref, index):
    low, high = value[:, :LANES], value[:, LANES:]
    mine_ref[index] = jnp.where(me == 0, low, high)
    other_ref[index] = jnp.where(me == 0, high, low)


def send_halves(at, buffer, out_ref, local, sent, arrived):
    tokens = buffer.shape[1]
    rows = pl.ds(pl.multiple_of(at.me * tokens, tokens), tokens)
    return (
        pltpu.make_async_copy(buffer.at[at.me], out_ref.at[rows], local),
        remote(buffer.at[1 - at.me], out_ref.at[rows], sent, arrived, at.core),
    )


def feed_kernel(
    nz,
    steps,
    x_ref,
    att_ref,
    cot_ref,
    gain_ref,
    wo_ref,
    wg_ref,
    wu_ref,
    wd_ref,
    ghid_ref,
    gn2_ref,
    *refs,
):
    if nz:
        out_ref, grad_ref, down_ref, late_ref, *refs = refs
    else:
        result_ref, mine_ref, other_ref, *refs = refs
    hid_ref, n2_ref, n2t_ref, cott_ref, acc_ref, dn_ref, a_ref, dg_ref, du_ref, *refs = refs
    tokens, model = hid_ref.shape
    half = model // 2
    step = pl.program_id(0)
    me = lax.axis_index("row")
    copies = []
    if nz:
        at = Place(nz)
        result_ref, local, sent, arrived, *refs = refs
        sums = Sums(at, True, refs, LATE)
        copies = send_halves(at, result_ref, out_ref, local.at[0], sent.at[0], arrived.at[0])
    else:
        sums = Unsummed(mine_ref, other_ref)

    def wo_half(h):
        return wo_ref[:, h].reshape(model, half)

    @pl.when(step == 0)
    def _():
        if nz:
            at.barrier([at.core, at.next_x, at.next_y] + at.levels())

        def start(rows):
            hidden = features(x_ref, rows).astype(F32)
            for h in range(2):
                hidden = hidden + nt(att_ref[h, rows, :], wo_half(h))
            hid_ref[rows, :] = hidden
            normal, _ = normal_of(hidden)
            n2_ref[rows, :] = (normal * gain_ref[...]).astype(BF)
            n2t_ref[:, rows] = jnp.transpose(n2_ref[rows, :])
            cott_ref[:, rows] = jnp.transpose(features(cot_ref, rows))
            acc_ref[rows, :] = jnp.zeros((CHUNK, model), F32)
            dn_ref[rows, :] = jnp.zeros((CHUNK, model), F32)

        chunks(tokens, start)

    def store(value):
        grad_ref[...] = value[:2]
        down_ref[...] = jnp.transpose(value[2])

    def leave(value):
        late_ref[...] = value

    def forward_back(rows):
        n2 = n2_ref[rows, :]
        gating = nn(n2, pair(wg_ref, model))
        upward = nn(n2, pair(wu_ref, model))
        gactive = nn(features(cot_ref, rows), pair(wd_ref, model))
        sigmoid = 1.0 / (1.0 + jnp.exp(-gating))
        silu = gating * sigmoid
        a_ref[rows, :] = (silu * upward).astype(BF)
        dg_ref[rows, :] = (gactive * upward * (sigmoid + silu * (1.0 - sigmoid))).astype(BF)
        du_ref[rows, :] = (gactive * silu).astype(BF)
        acc_ref[rows, :] += nt(a_ref[rows, :], pair(wd_ref, model))
        dn_ref[rows, :] += nt(dg_ref[rows, :], pair(wg_ref, model)) + nt(
            du_ref[rows, :], pair(wu_ref, model)
        )

    @pl.when(step < steps)
    def _():
        chunks(tokens, forward_back, tokens)
        slot = step % 2

        def weights(rows):
            n2t = n2t_ref[rows, :]
            for p, value in enumerate(
                (nn(n2t, dg_ref[...]), nn(n2t, du_ref[...]), nn(cott_ref[rows, :], a_ref[...]))
            ):
                split_store(me, value.astype(BF), sums.mine, sums.other, (slot, p, rows))

        chunks(model, weights, model)
        sums.start(step)

    sums.advance(step, store, leave)

    @pl.when(step == (steps if nz else steps - 1))
    def _():
        gn2_ref[...] = jnp.zeros_like(gn2_ref)

        def finish(rows):
            hidden = hid_ref[rows, :]
            result = (hidden + acc_ref[rows, :]).astype(BF)
            result_ref[0, rows, :] = result[:, :half]
            result_ref[1, rows, :] = result[:, half:]
            normal, inverse = normal_of(hidden)
            dn = dn_ref[rows, :]
            gn2_ref[...] += jnp.sum(dn * normal, axis=0, keepdims=True)
            ghid_ref[rows, :] = features(cot_ref, rows).astype(F32) + norm_back(
                normal, inverse, gain_ref[...], dn
            )

        chunks(tokens, finish)
        for copy in copies:
            copy.start()

    if nz:

        @pl.when(step == pl.num_programs(0) - 1)
        def _():
            for copy in copies:
                copy.wait()


def feed(x, attended, cotangent, gain, narrow, wide, units, nz):
    halves, tokens, half = x.shape
    model = halves * half
    groups, _, rows, _ = wide.shape
    steps = units // LANES
    tile = lambda at: pl.BlockSpec(
        (groups, halves, rows, LANES),
        lambda j: (0, 0, 0, at // LANES + jnp.minimum(j, steps - 1)),
    )
    big = lambda dtype: pltpu.VMEM((tokens, model), dtype)
    small = pltpu.VMEM((tokens, 2 * LANES), BF)
    early = steps - LATE
    last = Sums.last(True)
    dma = pltpu.SemaphoreType.DMA((1,))
    if nz:
        out_specs = [
            HBM,
            pl.BlockSpec((2, rows, LANES), lambda j: (0, 0, jnp.clip(j - last, 0, early - 1))),
            pl.BlockSpec((LANES, rows), lambda j: (jnp.clip(j - last, 0, early - 1), 0)),
            pl.BlockSpec((3, model, LANES), lambda j: (0, 0, jnp.clip(j - 1 - early, 0, LATE - 1))),
        ]
        out_shape = [
            jax.ShapeDtypeStruct((halves * tokens, half), BF),
            jax.ShapeDtypeStruct((2, rows, early * LANES), F32),
            jax.ShapeDtypeStruct((early * LANES, rows), F32),
            jax.ShapeDtypeStruct((3, model, LATE * LANES), BF),
        ]
        more = [pltpu.VMEM(x.shape, BF), dma, dma, dma] + Sums.scratch(3, model, steps, nz, True)
    else:
        grads = pl.BlockSpec((3, model, LANES), lambda j: (0, 0, j))
        out_specs = [once(x.shape), grads, grads]
        grads = jax.ShapeDtypeStruct((3, model, units), BF)
        out_shape = [jax.ShapeDtypeStruct(x.shape, BF), grads, grads]
        more = []
    return pl.pallas_call(
        functools.partial(feed_kernel, nz, steps),
        grid=(max(steps + 1, early + last) if nz else steps,),
        in_specs=[
            once(x.shape),
            once(x.shape),
            once(x.shape),
            once(gain.shape),
            pl.BlockSpec(
                (groups, halves, rows, half),
                lambda j: (0, 0, 0, 0),
                pipeline_mode=pl.Buffered(1),
            ),
            tile(0),
            tile(units),
            tile(half),
        ],
        out_specs=[once((tokens, model)), once(gain.shape)] + out_specs,
        out_shape=[
            jax.ShapeDtypeStruct((tokens, model), F32),
            jax.ShapeDtypeStruct(gain.shape, F32),
        ]
        + out_shape,
        scratch_shapes=[big(F32), big(BF), big(BF), big(BF), big(F32), big(F32), small, small, small]
        + more,
        compiler_params=comm_params(1) if nz else params(),
        name="feed",
    )(x, attended, cotangent, gain, narrow, wide, wide, narrow)


def back_kernel(
    nz,
    steps,
    starts_ref,
    qkv_ref,
    kmem_ref,
    vmem_ref,
    att_ref,
    lse_ref,
    wo_ref,
    wq_ref,
    wk_ref,
    wv_ref,
    x_ref,
    gain_ref,
    ghid_ref,
    gn2_ref,
    cos_ref,
    sin_ref,
    *refs,
):
    if nz:
        left_ref, out_ref, grad_ref, gout_ref, late_ref, down_ref, norms_ref, *refs = refs
    else:
        result_ref, mine_ref, other_ref, gn1_ref, *refs = refs
    gmix_ref, gmixt_ref, n1t_ref, dn_ref, gatt_ref, g_ref, dk_ref, dv_ref, *refs = refs
    tokens, model = ghid_ref.shape
    half = model // 2
    step = pl.program_id(0)
    me = lax.axis_index("row")
    copies = []
    if nz:
        at = Place(nz)
        result_ref, local, sent, arrived, *refs = refs
        sums = Sums(at, True, refs[: Sums.BUFFERS])
        late = Sums(at, True, refs[Sums.BUFFERS : 2 * Sums.BUFFERS])
        norms = Norms(at, refs[2 * Sums.BUFFERS :])
        copies = send_halves(at, result_ref, out_ref, local.at[0], sent.at[0], arrived.at[0])
    else:
        sums = Unsummed(mine_ref, other_ref)
    scale = LOG2E / math.sqrt(HEAD_DIM)
    plain = 1.0 / math.sqrt(HEAD_DIM)

    @pl.when(step == 0)
    def _():
        if nz:
            at.barrier(at.plane() + at.levels())

        def start(rows):
            normal, _ = normal_of(features(x_ref, rows).astype(F32))
            n1t_ref[:, rows] = jnp.transpose((normal * gain_ref[...]).astype(BF))
            gmix_ref[rows, :] = ghid_ref[rows, :].astype(BF)
            gmixt_ref[:, rows] = jnp.transpose(gmix_ref[rows, :])
            dn_ref[rows, :] = jnp.zeros((CHUNK, model), F32)

        chunks(tokens, start)

    def store(value):
        grad_ref[...] = value[:3]
        gout_ref[...] = jnp.transpose(value[3])

    def store_late(value):
        late_ref[...] = value[:2]
        down_ref[...] = jnp.transpose(value[2])

    if nz:

        @pl.when(step < LATE)
        def _():
            late.total[step] = left_ref[...]
            late.begin(step)

    def unturn(g, rows):
        return g * cos_ref[rows, :] - pltpu.roll(g, HEAD_DIM // 2, 1) * sin_ref[rows, :]

    def one_head(hh, carry):
        dk_ref[...] = jnp.zeros_like(dk_ref)
        dv_ref[...] = jnp.zeros_like(dv_ref)
        for b in range(QBLKS):
            start = starts_ref[me, b] - b * QROWS

            rows = slice(b * QROWS, (b + 1) * QROWS)
            q = qkv_ref[0, hh, rows, :]
            do = gatt_ref[hh, rows, :]
            lse = lse_ref[hh, 0, :, rows]
            dots = jnp.transpose(do.astype(F32) * att_ref[hh, rows, :].astype(F32))
            dot = jnp.sum(dots, axis=0, keepdims=True)
            dq = jnp.zeros((HEAD_DIM, QROWS), F32)
            for n in range(b + 2):
                span = slice(n * QROWS, (n + 1) * QROWS)
                if n <= b:
                    k, v = qkv_ref[1, hh, span, :], qkv_ref[2, hh, span, :]
                else:
                    k, v = kmem_ref[hh, b], vmem_ref[hh, b]
                s = nt(k, q)
                if n == b:
                    s = masked(s, start)
                share = jnp.exp2(s * scale - lse)
                ds = (share * (nt(v, do) - dot)).astype(BF)
                if n <= b:
                    dv_ref[span, :] += nn(share.astype(BF), do)
                    dk_ref[span, :] += nn(ds, q)
                dq = dq + tn(k, ds)
            g_ref[0, hh, rows, :] = unturn(jnp.transpose(dq) * plain, rows).astype(BF)

        def finish(rows):
            g_ref[1, hh, rows, :] = unturn(dk_ref[rows, :] * plain, rows).astype(BF)
            g_ref[2, hh, rows, :] = dv_ref[rows, :].astype(BF)

        chunks(tokens, finish)
        return carry

    @pl.when(step < steps)
    def _():
        def grad_attended(rows):
            value = nn(gmix_ref[rows, :], pair(wo_ref, model)).astype(BF)
            gatt_ref[0, rows, :] = value[:, :LANES]
            gatt_ref[1, rows, :] = value[:, LANES:]

        chunks(tokens, grad_attended, tokens)

    sums.advance(step, store)
    if nz:
        late.advance(step + 1, store_late, taken=True)

    @pl.when(step < steps)
    def _():
        lax.fori_loop(0, 2, one_head, 0)
        slot = step % 2

        def weights(rows):
            n1t = n1t_ref[rows, :]
            for p in range(3):
                value = nn(n1t, jnp.concatenate([g_ref[p, 0], g_ref[p, 1]], axis=1))
                split_store(me, value.astype(BF), sums.mine, sums.other, (slot, p, rows))
            value = nn(gmixt_ref[rows, :], jnp.concatenate([att_ref[0], att_ref[1]], axis=1))
            split_store(me, value.astype(BF), sums.mine, sums.other, (slot, 3, rows))

        chunks(model, weights, model)
        sums.start(step)

        def inward(rows):
            total = dn_ref[rows, :]
            for p, ref in enumerate((wq_ref, wk_ref, wv_ref)):
                g = jnp.concatenate([g_ref[p, 0, rows, :], g_ref[p, 1, rows, :]], axis=1)
                total = total + nt(g, pair(ref, model))
            dn_ref[rows, :] = total

        chunks(tokens, inward, tokens)

    @pl.when(step == (steps if nz else steps - 1))
    def _():
        def finish(rows, carry):
            normal, inverse = normal_of(features(x_ref, rows).astype(F32))
            dn = dn_ref[rows, :]
            value = (ghid_ref[rows, :] + norm_back(normal, inverse, gain_ref[...], dn)).astype(BF)
            result_ref[0, rows, :] = value[:, :half]
            result_ref[1, rows, :] = value[:, half:]
            return carry + jnp.sum(dn * normal, axis=0, keepdims=True)

        gn1 = lax.fori_loop(
            0,
            tokens // CHUNK,
            lambda i, c: finish(pl.ds(pl.multiple_of(i * CHUNK, CHUNK), CHUNK), c),
            jnp.zeros((1, model), F32),
        )
        for copy in copies:
            copy.start()
        if not nz:
            gn1_ref[...] = gn1
            return
        row = lax.broadcasted_iota(jnp.int32, (8, model), 0)
        norms.start(jnp.where(row == 0, gn1, jnp.where(row == 1, gn2_ref[...], 0.0)))

    if nz:

        @pl.when(step == steps + 1)
        def _():
            norms.after_plane()

        @pl.when(step == steps + 2)
        def _():
            norms_ref[...] = norms.result()

        @pl.when(step == pl.num_programs(0) - 1)
        def _():
            for copy in copies:
                copy.wait()


def back(starts, qkv, kmem, vmem, attended, lse, first, narrow, x, gain, ghid, gn2, cosine, sine, nz, *left):
    halves, tokens, half = x.shape
    model = halves * half
    groups, _, rows, _ = first.shape
    steps = half // HEAD_DIM
    memory = kmem.shape[2]
    now = lambda j: jnp.minimum(j, steps - 1)
    tile = lambda at: pl.BlockSpec(
        (groups, halves, rows, LANES), lambda j: (0, 0, 0, at // LANES + now(j))
    )
    chosen = pl.BlockSpec((halves, QBLKS, memory, HEAD_DIM), lambda j: (0, 0, 0, now(j)))
    big = lambda dtype: pltpu.VMEM((tokens, model), dtype)
    last = Sums.last(True)
    dma = pltpu.SemaphoreType.DMA((1,))
    if nz:
        out_specs = [
            HBM,
            pl.BlockSpec((3, rows, LANES), lambda j: (0, 0, jnp.clip(j - last, 0, steps - 1))),
            pl.BlockSpec((LANES, rows), lambda j: (jnp.clip(j - last, 0, steps - 1), 0)),
            pl.BlockSpec((2, rows, LANES), lambda j: (0, 0, jnp.clip(j - 3, 0, LATE - 1))),
            pl.BlockSpec((LANES, rows), lambda j: (jnp.clip(j - 3, 0, LATE - 1), 0)),
            once((8, LANES)),
        ]
        out_shape = [
            jax.ShapeDtypeStruct((halves * tokens, half), BF),
            jax.ShapeDtypeStruct((3, rows, half), F32),
            jax.ShapeDtypeStruct((half, rows), F32),
            jax.ShapeDtypeStruct((2, rows, LATE * LANES), F32),
            jax.ShapeDtypeStruct((LATE * LANES, rows), F32),
            jax.ShapeDtypeStruct((8, LANES), F32),
        ]
        more = (
            [pltpu.VMEM(x.shape, BF), dma, dma, dma]
            + Sums.scratch(4, model, steps, nz, True)
            + Sums.scratch(3, model, LATE, nz, True, True)
            + Norms.scratch(model, nz)
        )
        left_spec = [pl.BlockSpec((3, model, LANES), lambda j: (0, 0, jnp.minimum(j, LATE - 1)))]
    else:
        grads = pl.BlockSpec((4, model, LANES), lambda j: (0, 0, j))
        out_specs = [once(x.shape), grads, grads, once(gain.shape)]
        grads = jax.ShapeDtypeStruct((4, model, half), BF)
        out_shape = [jax.ShapeDtypeStruct(x.shape, BF), grads, grads]
        out_shape.append(jax.ShapeDtypeStruct(gain.shape, F32))
        more = []
        left_spec = []
    return pl.pallas_call(
        functools.partial(back_kernel, nz, steps),
        grid=(steps + last if nz else steps,),
        in_specs=[
            pl.BlockSpec(memory_space=pltpu.SMEM),
            pl.BlockSpec((3, halves, tokens, HEAD_DIM), lambda j: (0, 0, 0, now(j))),
            chosen,
            chosen,
            pl.BlockSpec((halves, tokens, HEAD_DIM), lambda j: (0, 0, now(j))),
            pl.BlockSpec((halves, 1, 1, tokens), lambda j: (0, now(j), 0, 0)),
            tile(0),
            tile(0),
            tile(half),
            tile(2 * half),
            once(x.shape),
            once(gain.shape),
            once(ghid.shape),
            once(gain.shape),
            once(cosine.shape),
            once(sine.shape),
        ]
        + left_spec,
        out_specs=out_specs,
        out_shape=out_shape,
        scratch_shapes=[big(BF), big(BF), big(BF), big(F32)]
        + [
            pltpu.VMEM((halves, tokens, HEAD_DIM), BF),
            pltpu.VMEM((3, halves, tokens, HEAD_DIM), BF),
            pltpu.VMEM((tokens, HEAD_DIM), F32),
            pltpu.VMEM((tokens, HEAD_DIM), F32),
        ]
        + more,
        compiler_params=comm_params(2) if nz else params(),
        name="back",
    )(
        starts,
        qkv,
        kmem,
        vmem,
        attended,
        lse,
        narrow,
        first,
        first,
        first,
        x,
        gain,
        ghid,
        gn2,
        cosine,
        sine,
        *left,
    )


def swap(value):
    return lax.ppermute(value, "row", [(0, 1), (1, 0)])


def in_order(mine, got, me):
    return jnp.where(me == 0, jnp.stack([mine, got]), jnp.stack([got, mine]))


def own_sequence(value, me):
    take = lambda i: lax.dynamic_index_in_dim(value, i, 0, keepdims=False)
    return in_order(take(me), swap(take(1 - me)), me)


def own_features(value, me):
    return own_sequence(value, me).reshape(-1, value.shape[2])


def summed(mine, other):
    total = mine.astype(F32) + swap(other).astype(F32)
    return lax.psum_scatter(total, ("dp", "col"), scatter_dimension=1, tiled=True)


def on_device(
    inputs,
    w_query,
    w_key,
    w_value,
    w_out,
    w_gate,
    w_up,
    w_down,
    norm_one,
    norm_two,
    cache_keys,
    cache_values,
    own_index,
    partner_index,
    picture_start,
    partner_seq,
    cotangent,
):
    me = lax.axis_index("row")
    nz = lax.axis_size("col")
    chips = lax.axis_size("dp") * nz
    half = inputs.shape[1]
    model = 2 * half
    units = w_gate.shape[1]
    rows = w_query.shape[0]

    gains = jnp.pad(jnp.stack([norm_one, norm_two], axis=1), ((0, 0), (0, LANES - 2)))
    narrow = jnp.concatenate([w_out.T, w_down.T], axis=1)
    tokens = inputs.reshape(SEQ_DEV, SEQ_LEN, half)
    upstream = cotangent.reshape(SEQ_DEV, SEQ_LEN, half)
    lines = lax.axis_size("dp") == 4 and nz * rows == 2 * LANES and rows * 2 == LANES
    if lines:
        first, narrow, wide, x, cot, qkv, attended, kmem, vmem, lse, cosine, sine = begin(
            own_index,
            partner_index,
            picture_start,
            partner_seq,
            w_query,
            w_key,
            w_value,
            gains,
            narrow,
            w_gate,
            w_up,
            tokens,
            upstream,
            cache_keys,
            cache_values,
            nz,
        )
    else:
        spread = lambda w: lax.all_gather(w, ("dp", "col", "row"), axis=0, tiled=True)
        first = spread(jnp.concatenate([w_query, w_key, w_value, gains], axis=1))
        narrow, wide = spread(narrow), spread(jnp.concatenate([w_gate, w_up], axis=1))
        x, cot = own_sequence(tokens, me), own_sequence(upstream, me)
        near = own_sequence(jnp.concatenate([cache_keys, cache_values], axis=1), me)
        far = lax.all_gather(near, "dp", axis=0)
        cosine, sine = rotary_tables()
        pick = lambda table: lax.dynamic_index_in_dim(table, me, 0, keepdims=False).reshape(-1)
        source = lax.dynamic_index_in_dim(partner_seq, me, 0) // SEQ_DEV // nz
        idx = jnp.concatenate([pick(own_index), pick(partner_index), pick(picture_start), source])
    first, narrow, wide = [w.reshape(chips, 2, rows, -1) for w in (first, narrow, wide)]
    gains = first[:, 0, :, 3 * half : 3 * half + 2].reshape(model, 2).astype(F32)
    gain_one, gain_two = gains[:, 0].reshape(1, model), gains[:, 1].reshape(1, model)
    if not lines:
        qkv = project_qkv(x, gain_one, first, cosine, sine)
        attended, lse, kmem, vmem = attend(idx, qkv, near, far)
    hops = nz if lines else 0
    ghid, gn2, *fed = feed(
        x, attended, cot, gain_two, narrow, wide, units, hops
    )
    left = fed[3:] if lines else []
    backed = back(
        picture_start,
        qkv,
        kmem,
        vmem,
        attended,
        lse,
        first,
        narrow,
        x,
        gain_one,
        ghid,
        gn2,
        cosine,
        sine,
        hops,
        *left,
    )
    if lines:
        out, feed_grads, down, _ = fed
        input_grad, model_grads, grad_out, late, late_down, norms = backed
        grad_gate, grad_up = [jnp.concatenate([feed_grads[i], late[i]], axis=1) for i in range(2)]
        grad_down = jnp.concatenate([down, late_down], axis=0)
        norms = lax.dynamic_slice_in_dim(norms[:2], lax.axis_index("col") % 2 * rows, rows, 1).T
    else:
        out, input_grad = own_features(fed[0], me), own_features(backed[0], me)
        feed_grads, model_grads = summed(*fed[1:]), summed(*backed[1:3])
        norms = jnp.concatenate([backed[3], gn2], axis=0).T
        norms = lax.psum_scatter(norms, ("dp", "col"), scatter_dimension=0, tiled=True)
        norms = lax.psum(norms, "row")
        grad_out, grad_down = model_grads[3].T, feed_grads[2].T
        grad_gate, grad_up = feed_grads[0], feed_grads[1]
    return (
        out,
        input_grad,
        model_grads[0],
        model_grads[1],
        model_grads[2],
        grad_out,
        grad_gate,
        grad_up,
        grad_down,
        norms[:, 0],
        norms[:, 1],
    )


def solution(mesh):
    tokens = P(("dp", "col"), "row")
    down = P("row", ("dp", "col"))
    gain = P(("dp", "col"))
    cache = P(("dp", "col"), None, "row")
    index = P(("dp", "col"), None, None)
    weights = (tokens, tokens, tokens, down, tokens, tokens, down)
    return jax.shard_map(
        on_device,
        mesh=mesh,
        in_specs=(tokens,)
        + weights
        + (gain, gain, cache, cache, index, index, P(("dp", "col"), None), gain, tokens),
        out_specs=(tokens, tokens) + weights + (gain, gain),
        check_vma=False,
    )
```

```python
import functools
import math

import jax
import jax.numpy as jnp
from jax import lax
from jax.experimental import pallas as pl
from jax.experimental.pallas import tpu as pltpu
from jax.sharding import PartitionSpec as P

HEAD_DIM = 128
SEQ_LEN = 1024
QROWS = 512
PIC = 256
MEM_BLK = 128
OWN_K = 2
PART_K = 2
SEQ_DEV = 2
QBLKS = 2
EPSILON = 1e-05
NEG = -1e30
CHUNK = 256
LANES = 128

BF = jnp.bfloat16
F32 = jnp.float32
LATE = 2
LOG2E = math.log2(math.e)
MESH = pl.DeviceIdType.MESH


def nn(a, b):
    return jnp.dot(a, b, preferred_element_type=F32)


def nt(a, b):
    return lax.dot_general(a, b, (((1,), (1,)), ((), ())), preferred_element_type=F32)


def tn(a, b):
    return lax.dot_general(a, b, (((0,), (0,)), ((), ())), preferred_element_type=F32)


def rotary_tables():
    half = HEAD_DIM // 2
    frequency = 10000.0 ** (-2.0 * jnp.arange(half, dtype=F32) / HEAD_DIM)
    angles = jnp.arange(SEQ_LEN, dtype=jnp.int32).astype(F32)[:, None] * frequency[None, :]
    cosine, sine = jnp.cos(angles), jnp.sin(angles)
    return jnp.concatenate([cosine, cosine], axis=1), jnp.concatenate([-sine, sine], axis=1)


def whole(shape):
    return pl.BlockSpec(shape, lambda *_: (0,) * len(shape))


def once(shape):
    return pl.BlockSpec(shape, lambda *_: (0,) * len(shape), pipeline_mode=pl.Buffered(1))


def params(limit=60):
    return pltpu.CompilerParams(
        vmem_limit_bytes=limit * 1024 * 1024
    )


def chunks(total, body, size=CHUNK):
    def step(i, carry):
        body(pl.ds(pl.multiple_of(i * size, size), size))
        return carry

    if total == size:
        body(pl.ds(0, size))
    else:
        lax.fori_loop(0, total // size, step, 0)


class Place:
    def __init__(self, nz):
        dp, self.me, self.z = lax.axis_index("dp"), lax.axis_index("row"), lax.axis_index("col")
        self.x, self.y, self.nz = dp % 2, dp // 2, nz
        self.core = (dp, 1 - self.me, self.z)
        self.next_x = (self.y * 2 + 1 - self.x, self.me, self.z)
        self.next_y = ((1 - self.y) * 2 + self.x, self.me, self.z)
        self.above = (dp, self.me, lax.rem(self.z + 1, nz))
        self.below = (dp, self.me, lax.rem(self.z + nz - 1, nz))
        self.has_above = self.z < nz - 1
        self.has_below = self.z > 0

    def corner(self):
        return ((1 - self.y) * 2 + 1 - self.x, self.me, self.z)

    def level(self, by):
        return (self.y * 2 + self.x, self.me, lax.rem(self.z + by, self.nz))

    def levels(self):
        return [self.level(by) for by in range(1, self.nz)]

    def plane(self):
        devices = []
        for by in range(1, 8):
            place = lax.rem(self.y * 4 + self.x * 2 + self.me + by, 8)
            devices.append((place // 2, place % 2, self.z))
        return devices

    def barrier(self, devices):
        semaphore = pltpu.get_barrier_semaphore()
        for device in devices:
            pl.semaphore_signal(semaphore, inc=1, device_id=device, device_id_type=MESH)
        pl.semaphore_wait(semaphore, len(devices))


def remote(source, target, sent, arrived, device):
    return pltpu.make_async_remote_copy(
        src_ref=source,
        dst_ref=target,
        send_sem=sent,
        recv_sem=arrived,
        device_id=device,
        device_id_type=MESH,
    )


def comm_params(number, limit=60):
    return pltpu.CompilerParams(
        vmem_limit_bytes=limit * 1024 * 1024, collective_id=number, has_side_effects=True
    )


HBM = pl.BlockSpec(memory_space=pl.ANY)


class Sent:
    def __init__(self):
        self.copies = []

    def go(self, copy, when=None):
        if when is None:
            copy.start()
        else:
            pl.when(when)(copy.start)
        self.copies.append((when, copy))

    def wait(self):
        for when, copy in self.copies:
            copy.wait_send() if when is None else pl.when(when)(copy.wait_send)


class Spread:
    BUFFERS = 6

    @staticmethod
    def scratch(nz):
        dma = pltpu.SemaphoreType.DMA
        return [dma((4, nz)), dma((4, nz)), dma((2, 5, nz)), dma((5, nz)), dma((nz,)), dma((nz,))]

    def __init__(self, at, sent, source, target, refs):
        self.at, self.sent, self.target = at, sent, target
        self.source = self.own() if source is None else source
        self.part = target.shape[-2] // 2
        (
            self.flat_sent,
            self.flat_arrived,
            self.line_sent,
            self.line_arrived,
            self.core_sent,
            self.core_arrived,
        ) = refs

    def block(self, place, zz, core=None):
        at = self.at
        y = at.y if place < 2 else 1 - at.y
        x = at.x if place in (0, 2) else 1 - at.x
        ref = self.target.at[y, x, zz, at.me if core is None else core]
        if place >= 3:
            ref = ref.at[pl.ds((place - 3) * self.part, self.part)]
        return ref

    def half(self, place, zz, piece):
        return self.block(place, zz).at[pl.ds(piece * self.part, self.part)]

    def own(self):
        return self.target.at[self.at.y, self.at.x, self.at.z, self.at.me]

    def flat(self, source, target, index, zz, device):
        return remote(source, target, self.flat_sent.at[index, zz], self.flat_arrived.at[index, zz], device)

    def sides(self, source, zz, when=None):
        target = self.block(0, zz)
        self.sent.go(self.flat(source, target, 0, zz, self.at.next_x), when)
        self.sent.go(self.flat(source, target, 1, zz, self.at.next_y), when)

    def from_side(self, index, zz, when=None):
        at = self.at
        place = 1 + index
        ref = self.block(place, zz)
        copy = self.flat(ref, ref, index, zz, (at.next_x, at.next_y)[index])
        copy.wait_recv() if when is None else pl.when(when)(copy.wait_recv)
        ref = self.half(place, zz, index)
        self.sent.go(self.flat(ref, ref, 2 + index, zz, (at.next_y, at.next_x)[index]), when)

    def from_across(self, index, zz, when=None):
        ref = self.block(3 + index, zz)
        copy = self.flat(ref, ref, 2 + index, zz, (self.at.next_y, self.at.next_x)[index])
        copy.wait_recv() if when is None else pl.when(when)(copy.wait_recv)

    def line(self, source, place, zz, up, when):
        at = self.at
        ref = self.block(place, zz)
        copy = remote(
            ref if source is None else source,
            ref,
            self.line_sent.at[int(up), place, zz],
            self.line_arrived.at[place, zz],
            at.above if up else at.below,
        )
        self.sent.go(copy, (at.has_above if up else at.has_below) & when)

    def both_ways(self, place, source=None):
        for up in (True, False):
            self.line(source, place, self.at.z, up, True)

    def from_line(self, step, up, place, onward):
        at = self.at
        zz = at.z - step if up else at.z + step
        valid = zz >= 0 if up else zz < at.nz
        zz = jnp.clip(zz, 0, at.nz - 1)
        ref = self.block(place, zz)
        copy = remote(
            ref,
            ref,
            self.line_sent.at[int(up), place, zz],
            self.line_arrived.at[place, zz],
            at.below if up else at.above,
        )
        pl.when(valid)(copy.wait_recv)
        self.line(None, place, zz, up, valid)
        if onward:
            self.sides(ref, zz, valid)

    def levels(self, step):
        at = self.at
        if step == 0:
            return [(at.z, None)]
        places = ((at.z - step, at.z >= step), (at.z + step, at.z + step < at.nz))
        return [(jnp.clip(zz, 0, at.nz - 1), valid) for zz, valid in places]

    def hand_copy(self, zz, core):
        ref = self.target.at[:, :, zz, core]
        return remote(ref, ref, self.core_sent.at[zz], self.core_arrived.at[zz], self.at.core)

    def hand_over(self, step):
        for zz, valid in self.levels(step):
            self.sent.go(self.hand_copy(zz, self.at.me), valid)

    def finish(self):
        for zz in range(self.at.nz):
            self.hand_copy(zz, 1 - self.at.me).wait_recv()


    def begin_line(self):
        self.both_ways(0, self.source)

    def begin_sides(self):
        self.sides(self.source, self.at.z)

    def level_sides(self, step):
        for zz, valid in self.levels(step):
            self.sides(self.block(0, zz), zz, valid)

    def sides_at(self, step):
        for zz, valid in self.levels(step):
            for index in range(2):
                self.from_side(index, zz, valid)

    def corners(self, step):
        for zz, valid in self.levels(step):
            for index in range(2):
                self.from_across(index, zz, valid)


    def plane(self, place):
        z = self.at.z
        if place < 3:
            self.from_side(place - 1, z)
        else:
            self.from_across(place - 3, z)
        self.both_ways(place)


def begin_kernel(
    nz,
    own_ref,
    partner_ref,
    starts_ref,
    seq_ref,
    wq_ref,
    wk_ref,
    wv_ref,
    gain_ref,
    wa_ref,
    wg_ref,
    wu_ref,
    x_ref,
    cot_ref,
    ck_ref,
    cv_ref,
    first_ref,
    a_ref,
    b_ref,
    xs_ref,
    cots_ref,
    qkv_ref,
    att_out,
    kmem_out,
    vmem_out,
    lse_ref,
    cos_ref,
    sin_ref,
    all_ref,
    xv_ref,
    n1_ref,
    y_ref,
    cotbuf,
    near_ref,
    far_ref,
    stage_ref,
    kmem_ref,
    vmem_ref,
    att_ref,
    acc_ref,
    shift_ref,
    total_ref,
    wide_ref,
    loaded,
    stored,
    csent,
    carrived,
    far_sent,
    far_arrived,
    far_csent,
    far_carrived,
    *refs,
):
    at = Place(nz)
    me, x, y, z = at.me, at.x, at.y, at.z
    keys = ck_ref.shape[1]
    width = all_ref.shape[-1]
    units = wg_ref.shape[1]
    tokens, model = n1_ref.shape
    half = model // 2
    sent = Sent()
    n = Spread.BUFFERS
    first = Spread(at, sent, None, all_ref, refs[:n])
    late = Spread(at, sent, wa_ref, a_ref, refs[n : 2 * n])
    wide = Spread(at, sent, wide_ref, b_ref, refs[2 * n :])
    span = [pl.ds(0, keys), pl.ds(keys, keys)]
    caches = (ck_ref, cv_ref)

    def local(source, target, semaphore):
        return pltpu.make_async_copy(source, target, semaphore)

    loads = [
        local(source, target, loaded.at[i])
        for i, (source, target) in enumerate(
            (
                (wq_ref, first.own().at[:, pl.ds(0, half)]),
                (x_ref.at[me], xv_ref.at[me]),
                (cot_ref.at[me], cotbuf),
                (ck_ref.at[me], near_ref.at[me, span[0]]),
                (cv_ref.at[me], near_ref.at[me, span[1]]),
                (wa_ref, late.own()),
                (wk_ref, first.own().at[:, pl.ds(half, half)]),
                (wv_ref, first.own().at[:, pl.ds(2 * half, half)]),
                (gain_ref, first.own().at[:, pl.ds(3 * half, LANES)]),
                (wg_ref, wide_ref.at[:, pl.ds(0, units)]),
                (wu_ref, wide_ref.at[:, pl.ds(units, units)]),
            )
        )
    ]
    stores = [
        local(source, target, stored.at[i])
        for i, (source, target) in enumerate(
            (
                (cotbuf, cots_ref.at[me]),
                (xv_ref, xs_ref),
                (all_ref, first_ref),
                (y_ref, qkv_ref),
                (kmem_ref, kmem_out),
                (vmem_ref, vmem_out),
                (att_ref, att_out),
            )
        )
    ]
    placed = local(wide_ref, wide.own(), stored.at[7])
    for copy in loads:
        copy.start()
    at.barrier([at.core, at.next_x, at.next_y, at.above, at.below])
    exchange = [
        remote(source, target, csent.at[i], carrived.at[i], at.core)
        for i, (source, target) in enumerate(
            (
                (x_ref.at[1 - me], xv_ref.at[me]),
                (ck_ref.at[1 - me], near_ref.at[me, span[0]]),
                (cv_ref.at[1 - me], near_ref.at[me, span[1]]),
                (cot_ref.at[1 - me], cots_ref.at[me]),
            )
        )
    ]

    def landing(source, turn, kv):
        return far_ref.at[source, me, span[kv]] if turn == 0 else stage_ref.at[source, kv]

    def cache_copy(line, turn, kv):
        index = (line, turn * 2 + kv)
        return remote(
            caches[kv].at[me if turn == 0 else 1 - me],
            landing(line, turn, kv),
            far_sent.at[index],
            far_arrived.at[index],
            (at.next_x, at.next_y)[line],
        )

    def corner_copy(turn, kv):
        source, device = (0, at.next_y) if turn == 0 else (1, at.next_x)
        index = (2, turn * 2 + kv)
        return remote(
            landing(source, turn, kv), landing(2, turn, kv), far_sent.at[index], far_arrived.at[index], device
        )

    def hand_over(source, kv):
        return remote(
            stage_ref.at[source, kv],
            far_ref.at[source, me, span[kv]],
            far_csent.at[source, kv],
            far_carrived.at[source, kv],
            at.core,
        )

    def from_lines(spread, step, places, onward):
        for place in places:
            for up in (True, False):
                spread.from_line(step, up, place, onward)


    for i in (0, 6, 7, 8):
        loads[i].wait()
    first.begin_line()
    first.begin_sides()
    late.begin_line()
    for i in (9, 10):
        loads[i].wait()
    placed.start()
    wide.begin_line()
    wide.begin_sides()
    sent.go(exchange[0])

    place_in = lax.broadcasted_iota(jnp.int32, (tokens, HEAD_DIM), 0).astype(F32)
    lane = lax.broadcasted_iota(jnp.int32, (1, HEAD_DIM), 1)
    turns = lax.rem(lane, HEAD_DIM // 2).astype(F32) * (-2.0 * math.log(10000.0) / HEAD_DIM)
    angles = place_in * jnp.exp(turns)
    cos_ref[...] = jnp.cos(angles)
    sin_ref[...] = jnp.where(lane < HEAD_DIM // 2, -1.0, 1.0) * jnp.sin(angles)

    from_lines(first, 1, (0,), True)
    wide.plane(1)
    wide.plane(2)
    first.sides_at(0)
    from_lines(first, 2, (0,), True)
    from_lines(late, 1, (0,), False)
    wide.plane(3)
    wide.plane(4)
    placed.wait()
    wide.hand_over(0)
    first.sides_at(1)
    for kv in range(2):
        sent.go(cache_copy(0, 0, kv))
        sent.go(cache_copy(1, 1, kv))
    from_lines(first, 3, (0,), True)
    from_lines(late, 2, (0,), False)
    first.sides_at(2)
    for kv in range(2):
        sent.go(cache_copy(0, 1, kv))
        sent.go(cache_copy(1, 0, kv))
    for copy in exchange[1:]:
        sent.go(copy)
    first.sides_at(3)
    from_lines(late, 3, (0,), False)
    from_lines(wide, 1, range(3), False)
    loads[2].wait()
    stores[0].start()
    loads[1].wait()
    exchange[0].wait_recv()
    stores[1].start()
    for step in range(nz):
        first.corners(step)
        first.hand_over(step)
    first.finish()
    stores[2].start()
    from_lines(wide, 1, range(3, 5), False)
    wide.hand_over(1)

    gains = all_ref[:, :, :, 0, :, pl.ds(width - LANES, LANES)].reshape(model, LANES).astype(F32)
    gain = jnp.transpose(gains)[0:1, :]

    def norm(rows):
        normal, _ = normal_of(features(xv_ref, rows).astype(F32))
        n1_ref[rows, :] = (normal * gain).astype(BF)

    chunks(tokens, norm)

    def project(i, carry):
        m, h = i // 2, i % 2
        lanes = pl.ds(pl.multiple_of(m * half, half), half)
        value = nn(n1_ref[...], all_ref[:, :, :, h, :, lanes].reshape(model, half))
        for head in range(half // HEAD_DIM):
            lanes = slice(head * HEAD_DIM, (head + 1) * HEAD_DIM)
            u = value[:, lanes]
            turned = u * cos_ref[...] + pltpu.roll(u, HEAD_DIM // 2, 1) * sin_ref[...]
            y_ref[m, h, :, lanes] = jnp.where(m < 2, turned, u).astype(BF)
        return carry

    lax.fori_loop(0, 6, project, 0)
    stores[3].start()


    for kv in range(2):
        cache_copy(0, 0, kv).wait_recv()
        sent.go(corner_copy(0, kv))
        cache_copy(1, 1, kv).wait_recv()
        sent.go(corner_copy(1, kv))
        sent.go(hand_over(1, kv))
    late.begin_sides()
    for step in range(1, nz):
        late.level_sides(step)
    for copy in loads[3:5]:
        copy.wait()
    for copy in exchange[1:3]:
        copy.wait_recv()

    def choose(index_ref, first_row):
        for b in range(QBLKS):
            for j in range(OWN_K):
                index = index_ref[me, b, j]
                rows = pl.ds(first_row + j * MEM_BLK, MEM_BLK)
                for h in range(2):
                    for offset, ref in ((0, kmem_ref), (keys, vmem_ref)):
                        block = near_ref[h, pl.ds(offset, MEM_BLK), :]
                        for c in range(1, keys // MEM_BLK):
                            other = near_ref[h, pl.ds(offset + c * MEM_BLK, MEM_BLK), :]
                            block = jnp.where(index == c, other, block)
                        ref[h, b, rows, :] = block

    choose(own_ref, 0)
    heads = half // HEAD_DIM
    near_rows = slice(0, OWN_K * MEM_BLK)
    far_rows = slice(OWN_K * MEM_BLK, (OWN_K + PART_K) * MEM_BLK)

    def place(i):
        h, column = i // heads, i % heads
        return h, column, pl.ds(pl.multiple_of(column * HEAD_DIM, HEAD_DIM), HEAD_DIM)

    def without_partner(i, carry):
        h, column, lanes = place(i)

        def store(rows, shift, total, acc):
            acc_ref[i, :, rows] = acc
            shift_ref[i, :, rows] = shift
            total_ref[i, :, rows] = total

        attend_head(
            lambda m, rows: y_ref[m, h, rows, lanes],
            lambda b: (kmem_ref[h, b, near_rows, lanes], vmem_ref[h, b, near_rows, lanes]),
            [starts_ref[me, b] for b in range(QBLKS)],
            store,
        )
        return carry

    def with_partner(i, carry):
        h, column, lanes = place(i)
        for b in range(QBLKS):
            rows = pl.ds(b * QROWS, QROWS)
            shift, total, acc = attend_rows(
                [(kmem_ref[h, b, far_rows, lanes], vmem_ref[h, b, far_rows, lanes], None)],
                y_ref[0, h, rows, lanes],
            )
            before = shift_ref[i, :, rows]
            top = jnp.maximum(shift, before)
            now, then = jnp.exp2(shift - top), jnp.exp2(before - top)
            total = total * now + total_ref[i, :, rows] * then
            acc = acc * now + acc_ref[i, :, rows] * then
            att_ref[h, rows, lanes] = jnp.transpose(acc / total).astype(BF)
            lse_ref[h, column, :, rows] = top + jnp.log2(total)
        return carry

    lax.fori_loop(0, heads, without_partner, 0)
    from_lines(wide, 2, range(3), False)
    for kv in range(2):
        cache_copy(0, 1, kv).wait_recv()
        sent.go(hand_over(0, kv))
        cache_copy(1, 0, kv).wait_recv()
    lax.fori_loop(heads, 2 * heads, without_partner, 0)
    from_lines(wide, 2, range(3, 5), False)
    wide.hand_over(2)
    late.sides_at(0)
    for kv in range(2):
        corner_copy(1, kv).wait_recv()
        sent.go(hand_over(2, kv))
        corner_copy(0, kv).wait_recv()
    for source in range(3):
        for kv in range(2):
            remote(
                stage_ref.at[source, kv],
                far_ref.at[source, 1 - me, span[kv]],
                far_csent.at[source, kv],
                far_carrived.at[source, kv],
                at.core,
            ).wait_recv()
    source = seq_ref[me]
    across = (1 - y) * 2 + 1 - x
    near_y = (1 - y) * 2 + x
    at_most = SEQ_DEV * nz

    def comes_from(place):
        return (source >= place * at_most) & (source < (place + 1) * at_most)

    def take(i, carry):
        rows = pl.ds(pl.multiple_of(i * MEM_BLK, MEM_BLK), MEM_BLK)
        for h in range(2):
            block = jnp.where(comes_from(near_y), far_ref[1, h, rows, :], far_ref[0, h, rows, :])
            near_ref[h, rows, :] = jnp.where(comes_from(across), far_ref[2, h, rows, :], block)
        return carry

    lax.fori_loop(0, 2 * keys // MEM_BLK, take, 0)
    choose(partner_ref, OWN_K * MEM_BLK)
    stores[4].start()
    stores[5].start()
    lax.fori_loop(0, 2 * heads, with_partner, 0)
    stores[6].start()
    late.sides_at(1)
    loads[5].wait()
    late.corners(0)
    late.hand_over(0)
    from_lines(wide, 3, range(5), False)
    wide.hand_over(3)
    late.sides_at(2)
    late.corners(1)
    late.hand_over(1)
    late.sides_at(3)
    for step in range(2, nz):
        late.corners(step)
        late.hand_over(step)
    late.finish()
    wide.finish()
    exchange[3].wait_recv()
    for copy in stores:
        copy.wait()
    sent.wait()


def begin(own, partner, starts, seq, wq, wk, wv, gains, wa, wg, wu, x, cot, cache_keys, cache_values, nz):
    dma = pltpu.SemaphoreType.DMA
    _, tokens, half = x.shape
    keys = cache_keys.shape[1]
    full = jax.ShapeDtypeStruct((2, tokens, half), BF)
    rows, units = wg.shape
    gathered = lambda width: (2, 2, nz, 2, rows, width)
    whole_array = lambda width: jax.ShapeDtypeStruct(gathered(width), BF)
    first = 3 * half + LANES
    vmem = pl.BlockSpec(memory_space=pltpu.VMEM)
    table = jax.ShapeDtypeStruct((tokens, HEAD_DIM), F32)
    heads = 2 * half // HEAD_DIM
    memory = (2, QBLKS, (OWN_K + PART_K) * MEM_BLK, half)
    return pl.pallas_call(
        functools.partial(begin_kernel, nz),
        in_specs=[pl.BlockSpec(memory_space=pltpu.SMEM)] * 4 + [HBM] * 11,
        out_specs=[HBM] * 9 + [vmem] * 3,
        out_shape=[
            whole_array(first),
            whole_array(wa.shape[1]),
            whole_array(2 * units),
            full,
            full,
            jax.ShapeDtypeStruct((3, 2, tokens, half), BF),
            full,
            jax.ShapeDtypeStruct(memory, BF),
            jax.ShapeDtypeStruct(memory, BF),
            jax.ShapeDtypeStruct((2, half // HEAD_DIM, 1, tokens), F32),
            table,
            table,
        ],
        scratch_shapes=[
            pltpu.VMEM(gathered(first), BF),
            pltpu.VMEM((2, tokens, half), BF),
            pltpu.VMEM((tokens, 2 * half), BF),
            pltpu.VMEM((3, 2, tokens, half), BF),
            pltpu.VMEM((tokens, half), BF),
            pltpu.VMEM((2, 2 * keys, half), BF),
            pltpu.VMEM((3, 2, 2 * keys, half), BF),
            pltpu.VMEM((3, 2, keys, half), BF),
            pltpu.VMEM(memory, BF),
            pltpu.VMEM(memory, BF),
            pltpu.VMEM((2, tokens, half), BF),
            pltpu.VMEM((heads, HEAD_DIM, tokens), F32),
            pltpu.VMEM((heads, 1, tokens), F32),
            pltpu.VMEM((heads, 1, tokens), F32),
            pltpu.VMEM((rows, 2 * units), BF),
            dma((11,)),
            dma((8,)),
            dma((4,)),
            dma((4,)),
            dma((3, 4)),
            dma((3, 4)),
            dma((3, 2)),
            dma((3, 2)),
        ]
        + Spread.scratch(nz) * 3,
        compiler_params=comm_params(0),
        name="begin",
    )(own, partner, starts, seq, wq, wk, wv, gains, wa, wg, wu, x, cot, cache_keys, cache_values)


class Sums:
    BUFFERS = 10

    @staticmethod
    def last(halved):
        return 4 if halved else 3

    @staticmethod
    def scratch(parts, rows, tiles, nz, halved, taken=False):
        dma = pltpu.SemaphoreType.DMA
        slab = rows // 4
        pairs = pltpu.VMEM((1, 1, 16, LANES) if taken else (2, parts, rows, LANES), BF)
        return [
            pairs,
            pairs,
            pltpu.VMEM((tiles, parts, rows, LANES), BF),
            pltpu.VMEM((tiles, 2, parts, slab // 2, LANES) if halved else (tiles, 1, parts, slab, LANES), BF),
            pltpu.VMEM((tiles, 2, parts, slab, LANES), BF),
            pltpu.VMEM((tiles, nz - 1, parts, slab // nz, LANES), BF),
            dma((tiles, 5)),
            dma((tiles, 5)),
            dma((tiles, nz - 1)),
            dma((tiles, nz - 1)),
        ]

    def __init__(self, at, halved, refs, left=0):
        (
            self.mine,
            self.other,
            self.total,
            self.diag,
            self.side,
            self.hop,
            self.sent,
            self.arrived,
            self.hop_sent,
            self.hop_arrived,
        ) = refs
        self.at, self.halved = at, halved
        self.tiles, _, self.rows, _ = self.total.shape
        self.left, self.early = left, self.tiles - left
        self.slab = self.rows // 4
        self.block = self.slab // at.nz

    def span(self, y, x, first=0, size=None):
        start = pl.multiple_of((y * 2 + x) * self.slab + first, self.block)
        return pl.ds(start, self.slab if size is None else size)

    def copy(self, j, span, target, index, device):
        return remote(
            self.total.at[j, :, span], target, self.sent.at[j, index], self.arrived.at[j, index], device
        )

    def core_copy(self, j):
        return remote(
            self.other.at[j % 2],
            self.total.at[j],
            self.sent.at[j, 0],
            self.arrived.at[j, 0],
            self.at.core,
        )

    def diag_copies(self, j):
        at, part = self.at, self.slab // 2
        y, x = 1 - at.y, 1 - at.x
        if not self.halved:
            return [self.copy(j, self.span(y, x), self.diag.at[j, 0], 1, at.corner())]
        return [
            self.copy(j, self.span(y, x, i * part, part), self.diag.at[j, i], 1 + i, device)
            for i, device in enumerate((at.next_x, at.next_y))
        ]

    def side_copies(self, j):
        at = self.at
        return [
            self.copy(j, self.span(at.y, 1 - at.x), self.side.at[j, 0], 3, at.next_x),
            self.copy(j, self.span(1 - at.y, at.x), self.side.at[j, 1], 4, at.next_y),
        ]

    def hop_copies(self, j):
        at = self.at
        copies = []
        for by in range(1, at.nz):
            device = at.level(by)
            copies.append(
                remote(
                    self.total.at[j, :, self.span(at.y, at.x, device[2] * self.block, self.block)],
                    self.hop.at[j, by - 1],
                    self.hop_sent.at[j, by - 1],
                    self.hop_arrived.at[j, by - 1],
                    device,
                )
            )
        return copies

    def add(self, j, span, *values):
        total = self.total[j, :, span, :].astype(F32)
        for value in values:
            total = total + value.astype(F32)
        self.total[j, :, span, :] = total.astype(BF)

    def start(self, j):
        self.core_copy(j).start()

    def after_core(self, j):
        self.core_copy(j).wait()

        def body(rows):
            self.add(j, rows, self.mine[j % 2, :, rows, :])

        chunks(self.rows, body)

    def begin(self, j):
        for copy in self.diag_copies(j):
            copy.start()
        if not self.halved:
            for copy in self.side_copies(j):
                copy.start()

    def after_diag(self, j):
        at, part = self.at, self.slab // 2
        for copy in self.diag_copies(j):
            copy.wait()
        self.add(j, self.span(1 - at.y, at.x, 0, part), self.diag[j, 0])
        self.add(j, self.span(at.y, 1 - at.x, part, part), self.diag[j, 1])
        for copy in self.side_copies(j):
            copy.start()

    def after_side(self, j):
        at = self.at
        for copy in self.side_copies(j):
            copy.wait()
        values = [self.side[j, 0], self.side[j, 1]]
        if not self.halved:
            for copy in self.diag_copies(j):
                copy.wait()
            values.append(self.diag[j, 0])
        self.add(j, self.span(at.y, at.x), *values)
        for copy in self.hop_copies(j):
            copy.start()

    def result(self, j):
        at = self.at
        for copy in self.hop_copies(j):
            copy.wait()
        value = self.total[j, :, self.span(at.y, at.x, at.z * self.block, self.block), :].astype(F32)
        for by in range(at.nz - 1):
            value = value + self.hop[j, by].astype(F32)
        return value

    def advance(self, step, store, leave=None, taken=False):
        def on(behind, body, first, last):
            j = step - behind
            pl.when((j >= first) & (j < last))(lambda: body(jnp.clip(j, first, last - 1)))

        def summed(j):
            self.after_core(j)
            self.begin(j)

        def left(j):
            self.after_core(j)
            leave(self.total[j])

        if not taken:
            on(1, summed, 0, self.early)
        if self.left:
            on(1, left, self.early, self.tiles)
        if self.halved:
            on(2, self.after_diag, 0, self.early)
        on(self.last(self.halved) - 1, self.after_side, 0, self.early)
        on(self.last(self.halved), lambda j: store(self.result(j)), 0, self.early)


class Norms:
    BUFFERS = 7

    @staticmethod
    def scratch(model, nz):
        dma = pltpu.SemaphoreType.DMA
        return [
            pltpu.VMEM((4, 8, model // 4), F32),
            pltpu.VMEM((8, 8, model // 4), F32),
            pltpu.VMEM((nz, 8, LANES), F32),
            dma((7,)),
            dma((7,)),
            dma((nz - 1,)),
            dma((nz - 1,)),
        ]

    def __init__(self, at, refs):
        self.at = at
        self.own, self.parts, self.level, self.sent, self.arrived, self.hop_sent, self.hop_arrived = refs

    def plane_copies(self):
        at = self.at
        me = at.y * 4 + at.x * 2 + at.me
        return [
            remote(self.own.at[device[0]], self.parts.at[me], self.sent.at[i], self.arrived.at[i], device)
            for i, device in enumerate(at.plane())
        ]

    def hop_copies(self):
        at = self.at
        me = at.y * 4 + at.x * 2 + at.me
        copies = []
        for by in range(1, at.nz):
            device = at.level(by)
            lanes = pl.ds(pl.multiple_of(device[2] // 2 * LANES, LANES), LANES)
            copies.append(
                remote(
                    self.own.at[0, :, lanes],
                    self.level.at[at.z],
                    self.hop_sent.at[by - 1],
                    self.hop_arrived.at[by - 1],
                    device,
                )
            )
        return copies

    def start(self, rows):
        at = self.at
        width = self.own.shape[2]
        for d in range(4):
            self.own[d] = rows[:, d * width : (d + 1) * width]
        self.parts[at.y * 4 + at.x * 2 + at.me] = self.own[at.y * 2 + at.x]
        for copy in self.plane_copies():
            copy.start()

    def after_plane(self):
        at = self.at
        for copy in self.plane_copies():
            copy.wait()
        total = self.parts[0]
        for i in range(1, 8):
            total = total + self.parts[i]
        self.own[0] = total
        lanes = pl.ds(pl.multiple_of(at.z // 2 * LANES, LANES), LANES)
        self.level[at.z] = self.own[0, :, lanes]
        for copy in self.hop_copies():
            copy.start()

    def result(self):
        for copy in self.hop_copies():
            copy.wait()
        total = self.level[0]
        for i in range(1, self.at.nz):
            total = total + self.level[i]
        return total


class Unsummed:
    class Tile:
        def __init__(self, ref):
            self.ref = ref

        def __setitem__(self, index, value):
            self.ref[index[1:]] = value

    def __init__(self, mine, other):
        self.mine, self.other = Unsummed.Tile(mine), Unsummed.Tile(other)

    def start(self, j):
        pass

    def advance(self, step, store, leave=None):
        pass


def features(ref, rows):
    return jnp.concatenate([ref[0, rows, :], ref[1, rows, :]], axis=1)


def pair(ref, model):
    return jnp.concatenate(
        [ref[:, 0].reshape(model, LANES), ref[:, 1].reshape(model, LANES)], axis=1
    )


def normal_of(x):
    inverse = lax.rsqrt(jnp.mean(x * x, axis=1, keepdims=True) + EPSILON)
    return x * inverse, inverse


def norm_back(normal, inverse, gain, grad):
    scaled = grad * gain
    return inverse * (scaled - normal * jnp.mean(scaled * normal, axis=1, keepdims=True))


def qkv_kernel(x_ref, gain_ref, w_ref, cos_ref, sin_ref, out_ref, n1_ref):
    part = pl.program_id(0)
    tokens, model = n1_ref.shape

    @pl.when((part == 0) & (pl.program_id(1) == 0))
    def _():
        def norm(rows):
            normal, _ = normal_of(features(x_ref, rows).astype(F32))
            n1_ref[rows, :] = (normal * gain_ref[...]).astype(BF)

        chunks(tokens, norm)

    def project(rows):
        y = nn(n1_ref[rows, :], w_ref[...].reshape(model, -1))
        cosine, sine = cos_ref[rows, :], sin_ref[rows, :]
        for h in range(y.shape[1] // HEAD_DIM):
            lanes = slice(h * HEAD_DIM, (h + 1) * HEAD_DIM)
            u = y[:, lanes]
            turned = u * cosine + pltpu.roll(u, HEAD_DIM // 2, 1) * sine
            out_ref[rows, lanes] = jnp.where(part < 2, turned, u).astype(BF)

    chunks(tokens, project, tokens)


def project_qkv(x, gain, gathered, cosine, sine):
    halves, tokens, half = x.shape
    groups, _, rows, _ = gathered.shape
    return pl.pallas_call(
        qkv_kernel,
        grid=(3, halves),
        in_specs=[
            whole(x.shape),
            whole(gain.shape),
            pl.BlockSpec((groups, None, rows, half), lambda m, h: (0, h, 0, m)),
            whole(cosine.shape),
            whole(sine.shape),
        ],
        out_specs=pl.BlockSpec((None, None, tokens, half), lambda m, h: (m, h, 0, 0)),
        out_shape=jax.ShapeDtypeStruct((3, halves, tokens, half), BF),
        scratch_shapes=[pltpu.VMEM((tokens, halves * half), BF)],
        compiler_params=params(),
        name="project_qkv",
    )(x, gain, gathered, cosine, sine)


def fill_memory(idx_ref, near_ref, far_ref, offset, mem_ref):
    for b in range(QBLKS):
        for j in range(OWN_K + PART_K):
            ref, at = (near_ref, b * OWN_K + j) if j < OWN_K else (far_ref, QBLKS * OWN_K + b * PART_K + j - OWN_K)
            start = pl.multiple_of(idx_ref[at] * MEM_BLK, MEM_BLK) + offset
            mem_ref[b, j * MEM_BLK : (j + 1) * MEM_BLK, :] = ref[pl.ds(start, MEM_BLK), :]


def masked(scores, start):
    keys, queries = scores.shape
    at = lax.broadcasted_iota(jnp.int32, (1, queries), 1)
    limit = jnp.where((at >= start) & (at < start + PIC), start + PIC - 1, at)
    key = lax.broadcasted_iota(jnp.int32, (keys, queries), 0)
    return jnp.where(key <= limit, scores, NEG)


SCALE = LOG2E / math.sqrt(HEAD_DIM)


def attend_rows(parts, q):
    scores = []
    for keys, values, mask in parts:
        s = nt(keys, q)
        scores.append((s if mask is None else masked(s, *mask), values))
    top = functools.reduce(jnp.maximum, [jnp.max(s, axis=0, keepdims=True) for s, _ in scores])
    shift = top * SCALE
    total = jnp.zeros_like(top)
    acc = jnp.zeros((HEAD_DIM, q.shape[0]), F32)
    for s, values in scores:
        e = jnp.exp2(s * SCALE - shift)
        total = total + jnp.sum(e, axis=0, keepdims=True)
        acc = acc + tn(values, e.astype(BF))
    return shift, total, acc


def attend_head(part, memory, starts, store):
    for b in range(QBLKS):
        rows = slice(b * QROWS, (b + 1) * QROWS)
        parts = []
        for n in range(b + 1):
            span = slice(n * QROWS, (n + 1) * QROWS)
            mask = (starts[b] - b * QROWS,) if n == b else None
            parts.append((part(1, span), part(2, span), mask))
        parts.append(memory(b) + (None,))
        store(rows, *attend_rows(parts, part(0, rows)))


def attend_kernel(
    idx_ref, q_ref, k_ref, v_ref, near_ref, far_ref, out_ref, lse_ref, kmem_ref, vmem_ref
):
    keys = near_ref.shape[0] // 2
    fill_memory(idx_ref, near_ref, far_ref, 0, kmem_ref)
    fill_memory(idx_ref, near_ref, far_ref, keys, vmem_ref)
    refs = (q_ref, k_ref, v_ref)

    def store(rows, shift, total, acc):
        out_ref[rows, :] = jnp.transpose(acc / total).astype(BF)
        lse_ref[:, rows] = shift + jnp.log2(total)

    attend_head(
        lambda m, rows: refs[m][rows, :],
        lambda b: (kmem_ref[b], vmem_ref[b]),
        [idx_ref[QBLKS * (OWN_K + PART_K) + b] for b in range(QBLKS)],
        store,
    )


def attend(idx, qkv, near, far):
    _, halves, tokens, half = qkv.shape
    here = half // HEAD_DIM
    cached = near.shape[1]
    memory = (OWN_K + PART_K) * MEM_BLK
    column = lambda m: pl.BlockSpec(
        (None, None, tokens, HEAD_DIM), lambda h, idx: (m, h // here, 0, h % here)
    )
    cache = pl.BlockSpec((None, cached, HEAD_DIM), lambda h, idx: (h // here, 0, h % here))
    which = QBLKS * (OWN_K + PART_K) + QBLKS
    partner = pl.BlockSpec(
        (None, None, cached, HEAD_DIM), lambda h, idx: (idx[which], h // here, 0, h % here)
    )
    chosen = pl.BlockSpec((None, QBLKS, memory, HEAD_DIM), lambda h, idx: (h // here, 0, 0, h % here))
    chosen_shape = jax.ShapeDtypeStruct((halves, QBLKS, memory, half), BF)
    return pl.pallas_call(
        attend_kernel,
        grid_spec=pltpu.PrefetchScalarGridSpec(
            num_scalar_prefetch=1,
            grid=(halves * here,),
            in_specs=[column(0), column(1), column(2), cache, partner],
            out_specs=[
                pl.BlockSpec((None, tokens, HEAD_DIM), lambda h, idx: (h // here, 0, h % here)),
                pl.BlockSpec((None, None, 1, tokens), lambda h, idx: (h // here, h % here, 0, 0)),
                chosen,
                chosen,
            ],
        ),
        out_shape=[
            jax.ShapeDtypeStruct((halves, tokens, half), BF),
            jax.ShapeDtypeStruct((halves, here, 1, tokens), F32),
            chosen_shape,
            chosen_shape,
        ],
        compiler_params=params(),
        name="attend",
    )(idx, qkv, qkv, qkv, near, far)


def split_store(me, value, mine_ref, other_ref, index):
    low, high = value[:, :LANES], value[:, LANES:]
    mine_ref[index] = jnp.where(me == 0, low, high)
    other_ref[index] = jnp.where(me == 0, high, low)


def send_halves(at, buffer, out_ref, local, sent, arrived):
    tokens = buffer.shape[1]
    rows = pl.ds(pl.multiple_of(at.me * tokens, tokens), tokens)
    return (
        pltpu.make_async_copy(buffer.at[at.me], out_ref.at[rows], local),
        remote(buffer.at[1 - at.me], out_ref.at[rows], sent, arrived, at.core),
    )


def feed_kernel(
    nz,
    steps,
    x_ref,
    att_ref,
    cot_ref,
    gain_ref,
    wo_ref,
    wg_ref,
    wu_ref,
    wd_ref,
    ghid_ref,
    gn2_ref,
    *refs,
):
    if nz:
        out_ref, grad_ref, down_ref, late_ref, *refs = refs
    else:
        result_ref, mine_ref, other_ref, *refs = refs
    hid_ref, n2_ref, n2t_ref, cott_ref, acc_ref, dn_ref, a_ref, dg_ref, du_ref, *refs = refs
    tokens, model = hid_ref.shape
    half = model // 2
    step = pl.program_id(0)
    me = lax.axis_index("row")
    copies = []
    if nz:
        at = Place(nz)
        result_ref, local, sent, arrived, *refs = refs
        sums = Sums(at, True, refs, LATE)
        copies = send_halves(at, result_ref, out_ref, local.at[0], sent.at[0], arrived.at[0])
    else:
        sums = Unsummed(mine_ref, other_ref)

    def wo_half(h):
        return wo_ref[:, h].reshape(model, half)

    @pl.when(step == 0)
    def _():
        if nz:
            at.barrier([at.core, at.next_x, at.next_y] + at.levels())

        def start(rows):
            hidden = features(x_ref, rows).astype(F32)
            for h in range(2):
                hidden = hidden + nt(att_ref[h, rows, :], wo_half(h))
            hid_ref[rows, :] = hidden
            normal, _ = normal_of(hidden)
            n2_ref[rows, :] = (normal * gain_ref[...]).astype(BF)
            n2t_ref[:, rows] = jnp.transpose(n2_ref[rows, :])
            cott_ref[:, rows] = jnp.transpose(features(cot_ref, rows))
            acc_ref[rows, :] = jnp.zeros((CHUNK, model), F32)
            dn_ref[rows, :] = jnp.zeros((CHUNK, model), F32)

        chunks(tokens, start)

    def store(value):
        grad_ref[...] = value[:2]
        down_ref[...] = value[2]

    def leave(value):
        late_ref[...] = value

    def forward_back(rows):
        n2 = n2_ref[rows, :]
        gating = nn(n2, pair(wg_ref, model))
        upward = nn(n2, pair(wu_ref, model))
        gactive = nn(features(cot_ref, rows), pair(wd_ref, model))
        sigmoid = 1.0 / (1.0 + jnp.exp(-gating))
        silu = gating * sigmoid
        a_ref[rows, :] = (silu * upward).astype(BF)
        dg_ref[rows, :] = (gactive * upward * (sigmoid + silu * (1.0 - sigmoid))).astype(BF)
        du_ref[rows, :] = (gactive * silu).astype(BF)
        acc_ref[rows, :] += nt(a_ref[rows, :], pair(wd_ref, model))
        dn_ref[rows, :] += nt(dg_ref[rows, :], pair(wg_ref, model)) + nt(
            du_ref[rows, :], pair(wu_ref, model)
        )

    @pl.when(step < steps)
    def _():
        chunks(tokens, forward_back, tokens)
        slot = step % 2

        def weights(rows):
            n2t = n2t_ref[rows, :]
            for p, value in enumerate(
                (nn(n2t, dg_ref[...]), nn(n2t, du_ref[...]), nn(cott_ref[rows, :], a_ref[...]))
            ):
                split_store(me, value.astype(BF), sums.mine, sums.other, (slot, p, rows))

        chunks(model, weights, model)
        sums.start(step)

    sums.advance(step, store, leave)

    @pl.when(step == (steps if nz else steps - 1))
    def _():
        gn2_ref[...] = jnp.zeros_like(gn2_ref)

        def finish(rows):
            hidden = hid_ref[rows, :]
            result = (hidden + acc_ref[rows, :]).astype(BF)
            result_ref[0, rows, :] = result[:, :half]
            result_ref[1, rows, :] = result[:, half:]
            normal, inverse = normal_of(hidden)
            dn = dn_ref[rows, :]
            gn2_ref[...] += jnp.sum(dn * normal, axis=0, keepdims=True)
            ghid_ref[rows, :] = features(cot_ref, rows).astype(F32) + norm_back(
                normal, inverse, gain_ref[...], dn
            )

        chunks(tokens, finish)
        for copy in copies:
            copy.start()

    if nz:

        @pl.when(step == pl.num_programs(0) - 1)
        def _():
            for copy in copies:
                copy.wait()


def feed(x, attended, cotangent, gain, narrow, wide, units, nz):
    halves, tokens, half = x.shape
    model = halves * half
    groups, _, rows, _ = wide.shape
    steps = units // LANES
    tile = lambda at: pl.BlockSpec(
        (groups, halves, rows, LANES),
        lambda j: (0, 0, 0, at // LANES + jnp.minimum(j, steps - 1)),
    )
    big = lambda dtype: pltpu.VMEM((tokens, model), dtype)
    small = pltpu.VMEM((tokens, 2 * LANES), BF)
    early = steps - LATE
    last = Sums.last(True)
    dma = pltpu.SemaphoreType.DMA((1,))
    if nz:
        out_specs = [
            HBM,
            pl.BlockSpec((2, rows, LANES), lambda j: (0, 0, jnp.clip(j - last, 0, early - 1))),
            pl.BlockSpec((rows, LANES), lambda j: (0, jnp.clip(j - last, 0, early - 1))),
            pl.BlockSpec((3, model, LANES), lambda j: (0, 0, jnp.clip(j - 1 - early, 0, LATE - 1))),
        ]
        out_shape = [
            jax.ShapeDtypeStruct((halves * tokens, half), BF),
            jax.ShapeDtypeStruct((2, rows, units), F32),
            jax.ShapeDtypeStruct((rows, units), F32),
            jax.ShapeDtypeStruct((3, model, LATE * LANES), BF),
        ]
        more = [pltpu.VMEM(x.shape, BF), dma, dma, dma] + Sums.scratch(3, model, steps, nz, True)
    else:
        grads = pl.BlockSpec((3, model, LANES), lambda j: (0, 0, j))
        out_specs = [once(x.shape), grads, grads]
        grads = jax.ShapeDtypeStruct((3, model, units), BF)
        out_shape = [jax.ShapeDtypeStruct(x.shape, BF), grads, grads]
        more = []
    return pl.pallas_call(
        functools.partial(feed_kernel, nz, steps),
        grid=(max(steps + 1, early + last) if nz else steps,),
        in_specs=[
            once(x.shape),
            once(x.shape),
            once(x.shape),
            once(gain.shape),
            pl.BlockSpec(
                (groups, halves, rows, half),
                lambda j: (0, 0, 0, 0),
                pipeline_mode=pl.Buffered(1),
            ),
            tile(0),
            tile(units),
            tile(half),
        ],
        out_specs=[once((tokens, model)), once(gain.shape)] + out_specs,
        out_shape=[
            jax.ShapeDtypeStruct((tokens, model), F32),
            jax.ShapeDtypeStruct(gain.shape, F32),
        ]
        + out_shape,
        scratch_shapes=[big(F32), big(BF), big(BF), big(BF), big(F32), big(F32), small, small, small]
        + more,
        compiler_params=comm_params(1) if nz else params(),
        name="feed",
    )(x, attended, cotangent, gain, narrow, wide, wide, narrow)


def back_kernel(
    nz,
    steps,
    starts_ref,
    qkv_ref,
    kmem_ref,
    vmem_ref,
    att_ref,
    lse_ref,
    wo_ref,
    wq_ref,
    wk_ref,
    wv_ref,
    x_ref,
    gain_ref,
    ghid_ref,
    gn2_ref,
    cos_ref,
    sin_ref,
    *refs,
):
    if nz:
        left_ref, _, _, out_ref, grad_ref, gout_ref, late_ref, down_ref, norms_ref, *refs = refs
    else:
        result_ref, mine_ref, other_ref, gn1_ref, *refs = refs
    gmix_ref, gmixt_ref, n1t_ref, dn_ref, gatt_ref, g_ref, dk_ref, dv_ref, *refs = refs
    tokens, model = ghid_ref.shape
    half = model // 2
    step = pl.program_id(0)
    me = lax.axis_index("row")
    copies = []
    if nz:
        at = Place(nz)
        result_ref, local, sent, arrived, *refs = refs
        sums = Sums(at, True, refs[: Sums.BUFFERS])
        late = Sums(at, True, refs[Sums.BUFFERS : 2 * Sums.BUFFERS])
        norms = Norms(at, refs[2 * Sums.BUFFERS :])
        copies = send_halves(at, result_ref, out_ref, local.at[0], sent.at[0], arrived.at[0])
    else:
        sums = Unsummed(mine_ref, other_ref)
    scale = LOG2E / math.sqrt(HEAD_DIM)
    plain = 1.0 / math.sqrt(HEAD_DIM)

    @pl.when(step == 0)
    def _():
        if nz:
            at.barrier(at.plane() + at.levels())

        def start(rows):
            normal, _ = normal_of(features(x_ref, rows).astype(F32))
            n1t_ref[:, rows] = jnp.transpose((normal * gain_ref[...]).astype(BF))
            gmix_ref[rows, :] = ghid_ref[rows, :].astype(BF)
            gmixt_ref[:, rows] = jnp.transpose(gmix_ref[rows, :])
            dn_ref[rows, :] = jnp.zeros((CHUNK, model), F32)

        chunks(tokens, start)

    def store(value):
        grad_ref[...] = value[:3]
        gout_ref[...] = value[3]

    def store_late(value):
        late_ref[...] = value[:2]
        down_ref[...] = value[2]

    if nz:

        @pl.when(step < LATE)
        def _():
            late.total[step] = left_ref[...]
            late.begin(step)

    def unturn(g, rows):
        return g * cos_ref[rows, :] - pltpu.roll(g, HEAD_DIM // 2, 1) * sin_ref[rows, :]

    def one_head(hh, carry):
        dk_ref[...] = jnp.zeros_like(dk_ref)
        dv_ref[...] = jnp.zeros_like(dv_ref)
        for b in range(QBLKS):
            start = starts_ref[me, b] - b * QROWS

            rows = slice(b * QROWS, (b + 1) * QROWS)
            q = qkv_ref[0, hh, rows, :]
            do = gatt_ref[hh, rows, :]
            lse = lse_ref[hh, 0, :, rows]
            dots = jnp.transpose(do.astype(F32) * att_ref[hh, rows, :].astype(F32))
            dot = jnp.sum(dots, axis=0, keepdims=True)
            dq = jnp.zeros((HEAD_DIM, QROWS), F32)
            for n in range(b + 2):
                span = slice(n * QROWS, (n + 1) * QROWS)
                if n <= b:
                    k, v = qkv_ref[1, hh, span, :], qkv_ref[2, hh, span, :]
                else:
                    k, v = kmem_ref[hh, b], vmem_ref[hh, b]
                s = nt(k, q)
                if n == b:
                    s = masked(s, start)
                share = jnp.exp2(s * scale - lse)
                ds = (share * (nt(v, do) - dot)).astype(BF)
                if n <= b:
                    dv_ref[span, :] += nn(share.astype(BF), do)
                    dk_ref[span, :] += nn(ds, q)
                dq = dq + tn(k, ds)
            g_ref[0, hh, rows, :] = unturn(jnp.transpose(dq) * plain, rows).astype(BF)

        def finish(rows):
            g_ref[1, hh, rows, :] = unturn(dk_ref[rows, :] * plain, rows).astype(BF)
            g_ref[2, hh, rows, :] = dv_ref[rows, :].astype(BF)

        chunks(tokens, finish)
        return carry

    @pl.when(step < steps)
    def _():
        def grad_attended(rows):
            value = nn(gmix_ref[rows, :], pair(wo_ref, model)).astype(BF)
            gatt_ref[0, rows, :] = value[:, :LANES]
            gatt_ref[1, rows, :] = value[:, LANES:]

        chunks(tokens, grad_attended, tokens)

    sums.advance(step, store)
    if nz:
        late.advance(step + 1, store_late, taken=True)

    @pl.when(step < steps)
    def _():
        lax.fori_loop(0, 2, one_head, 0)
        slot = step % 2

        def weights(rows):
            n1t = n1t_ref[rows, :]
            for p in range(3):
                value = nn(n1t, jnp.concatenate([g_ref[p, 0], g_ref[p, 1]], axis=1))
                split_store(me, value.astype(BF), sums.mine, sums.other, (slot, p, rows))
            value = nn(gmixt_ref[rows, :], jnp.concatenate([att_ref[0], att_ref[1]], axis=1))
            split_store(me, value.astype(BF), sums.mine, sums.other, (slot, 3, rows))

        chunks(model, weights, model)
        sums.start(step)

        def inward(rows):
            total = dn_ref[rows, :]
            for p, ref in enumerate((wq_ref, wk_ref, wv_ref)):
                g = jnp.concatenate([g_ref[p, 0, rows, :], g_ref[p, 1, rows, :]], axis=1)
                total = total + nt(g, pair(ref, model))
            dn_ref[rows, :] = total

        chunks(tokens, inward, tokens)

    @pl.when(step == (steps if nz else steps - 1))
    def _():
        def finish(rows, carry):
            normal, inverse = normal_of(features(x_ref, rows).astype(F32))
            dn = dn_ref[rows, :]
            value = (ghid_ref[rows, :] + norm_back(normal, inverse, gain_ref[...], dn)).astype(BF)
            result_ref[0, rows, :] = value[:, :half]
            result_ref[1, rows, :] = value[:, half:]
            return carry + jnp.sum(dn * normal, axis=0, keepdims=True)

        gn1 = lax.fori_loop(
            0,
            tokens // CHUNK,
            lambda i, c: finish(pl.ds(pl.multiple_of(i * CHUNK, CHUNK), CHUNK), c),
            jnp.zeros((1, model), F32),
        )
        for copy in copies:
            copy.start()
        if not nz:
            gn1_ref[...] = gn1
            return
        row = lax.broadcasted_iota(jnp.int32, (8, model), 0)
        norms.start(jnp.where(row == 0, gn1, jnp.where(row == 1, gn2_ref[...], 0.0)))

    if nz:

        @pl.when(step == steps + 1)
        def _():
            norms.after_plane()

        @pl.when(step == steps + 2)
        def _():
            norms_ref[...] = norms.result()

        @pl.when(step == pl.num_programs(0) - 1)
        def _():
            for copy in copies:
                copy.wait()


def back(starts, qkv, kmem, vmem, attended, lse, first, narrow, x, gain, ghid, gn2, cosine, sine, nz, *left):
    halves, tokens, half = x.shape
    model = halves * half
    groups, _, rows, _ = first.shape
    steps = half // HEAD_DIM
    memory = kmem.shape[2]
    now = lambda j: jnp.minimum(j, steps - 1)
    tile = lambda at: pl.BlockSpec(
        (groups, halves, rows, LANES), lambda j: (0, 0, 0, at // LANES + now(j))
    )
    chosen = pl.BlockSpec((halves, QBLKS, memory, HEAD_DIM), lambda j: (0, 0, 0, now(j)))
    big = lambda dtype: pltpu.VMEM((tokens, model), dtype)
    last = Sums.last(True)
    dma = pltpu.SemaphoreType.DMA((1,))
    aliases = {}
    if nz:
        early = left[1].shape[2] // LANES - LATE
        aliases = {17: 3, 18: 4}
        out_specs = [
            HBM,
            pl.BlockSpec((3, rows, LANES), lambda j: (0, 0, jnp.clip(j - last, 0, steps - 1))),
            pl.BlockSpec((rows, LANES), lambda j: (0, jnp.clip(j - last, 0, steps - 1))),
            pl.BlockSpec((2, rows, LANES), lambda j: (0, 0, early + jnp.clip(j - 3, 0, LATE - 1))),
            pl.BlockSpec((rows, LANES), lambda j: (0, early + jnp.clip(j - 3, 0, LATE - 1))),
            once((8, LANES)),
        ]
        out_shape = [
            jax.ShapeDtypeStruct((halves * tokens, half), BF),
            jax.ShapeDtypeStruct((3, rows, half), F32),
            jax.ShapeDtypeStruct((rows, half), F32),
            jax.ShapeDtypeStruct(left[1].shape, F32),
            jax.ShapeDtypeStruct(left[2].shape, F32),
            jax.ShapeDtypeStruct((8, LANES), F32),
        ]
        more = (
            [pltpu.VMEM(x.shape, BF), dma, dma, dma]
            + Sums.scratch(4, model, steps, nz, True)
            + Sums.scratch(3, model, LATE, nz, True, True)
            + Norms.scratch(model, nz)
        )
        left_spec = [pl.BlockSpec((3, model, LANES), lambda j: (0, 0, jnp.minimum(j, LATE - 1))), HBM, HBM]
    else:
        grads = pl.BlockSpec((4, model, LANES), lambda j: (0, 0, j))
        out_specs = [once(x.shape), grads, grads, once(gain.shape)]
        grads = jax.ShapeDtypeStruct((4, model, half), BF)
        out_shape = [jax.ShapeDtypeStruct(x.shape, BF), grads, grads]
        out_shape.append(jax.ShapeDtypeStruct(gain.shape, F32))
        more = []
        left_spec = []
    return pl.pallas_call(
        functools.partial(back_kernel, nz, steps),
        grid=(steps + last if nz else steps,),
        in_specs=[
            pl.BlockSpec(memory_space=pltpu.SMEM),
            pl.BlockSpec((3, halves, tokens, HEAD_DIM), lambda j: (0, 0, 0, now(j))),
            chosen,
            chosen,
            pl.BlockSpec((halves, tokens, HEAD_DIM), lambda j: (0, 0, now(j))),
            pl.BlockSpec((halves, 1, 1, tokens), lambda j: (0, now(j), 0, 0)),
            tile(0),
            tile(0),
            tile(half),
            tile(2 * half),
            once(x.shape),
            once(gain.shape),
            once(ghid.shape),
            once(gain.shape),
            once(cosine.shape),
            once(sine.shape),
        ]
        + left_spec,
        out_specs=out_specs,
        out_shape=out_shape,
        scratch_shapes=[big(BF), big(BF), big(BF), big(F32)]
        + [
            pltpu.VMEM((halves, tokens, HEAD_DIM), BF),
            pltpu.VMEM((3, halves, tokens, HEAD_DIM), BF),
            pltpu.VMEM((tokens, HEAD_DIM), F32),
            pltpu.VMEM((tokens, HEAD_DIM), F32),
        ]
        + more,
        input_output_aliases=aliases,
        compiler_params=comm_params(2) if nz else params(),
        name="back",
    )(
        starts,
        qkv,
        kmem,
        vmem,
        attended,
        lse,
        narrow,
        first,
        first,
        first,
        x,
        gain,
        ghid,
        gn2,
        cosine,
        sine,
        *left,
    )


def swap(value):
    return lax.ppermute(value, "row", [(0, 1), (1, 0)])


def in_order(mine, got, me):
    return jnp.where(me == 0, jnp.stack([mine, got]), jnp.stack([got, mine]))


def own_sequence(value, me):
    take = lambda i: lax.dynamic_index_in_dim(value, i, 0, keepdims=False)
    return in_order(take(me), swap(take(1 - me)), me)


def own_features(value, me):
    return own_sequence(value, me).reshape(-1, value.shape[2])


def summed(mine, other):
    total = mine.astype(F32) + swap(other).astype(F32)
    return lax.psum_scatter(total, ("dp", "col"), scatter_dimension=1, tiled=True)


def on_device(
    inputs,
    w_query,
    w_key,
    w_value,
    w_out,
    w_gate,
    w_up,
    w_down,
    norm_one,
    norm_two,
    cache_keys,
    cache_values,
    own_index,
    partner_index,
    picture_start,
    partner_seq,
    cotangent,
):
    me = lax.axis_index("row")
    nz = lax.axis_size("col")
    chips = lax.axis_size("dp") * nz
    half = inputs.shape[1]
    model = 2 * half
    units = w_gate.shape[1]
    rows = w_query.shape[0]

    gains = jnp.pad(jnp.stack([norm_one, norm_two], axis=1), ((0, 0), (0, LANES - 2)))
    narrow = jnp.concatenate([w_out.T, w_down.T], axis=1)
    tokens = inputs.reshape(SEQ_DEV, SEQ_LEN, half)
    upstream = cotangent.reshape(SEQ_DEV, SEQ_LEN, half)
    lines = lax.axis_size("dp") == 4 and nz * rows == 2 * LANES and rows * 2 == LANES
    if lines:
        first, narrow, wide, x, cot, qkv, attended, kmem, vmem, lse, cosine, sine = begin(
            own_index,
            partner_index,
            picture_start,
            partner_seq,
            w_query,
            w_key,
            w_value,
            gains,
            narrow,
            w_gate,
            w_up,
            tokens,
            upstream,
            cache_keys,
            cache_values,
            nz,
        )
    else:
        spread = lambda w: lax.all_gather(w, ("dp", "col", "row"), axis=0, tiled=True)
        first = spread(jnp.concatenate([w_query, w_key, w_value, gains], axis=1))
        narrow, wide = spread(narrow), spread(jnp.concatenate([w_gate, w_up], axis=1))
        x, cot = own_sequence(tokens, me), own_sequence(upstream, me)
        near = own_sequence(jnp.concatenate([cache_keys, cache_values], axis=1), me)
        far = lax.all_gather(near, "dp", axis=0)
        cosine, sine = rotary_tables()
        pick = lambda table: lax.dynamic_index_in_dim(table, me, 0, keepdims=False).reshape(-1)
        source = lax.dynamic_index_in_dim(partner_seq, me, 0) // SEQ_DEV // nz
        idx = jnp.concatenate([pick(own_index), pick(partner_index), pick(picture_start), source])
    first, narrow, wide = [w.reshape(chips, 2, rows, -1) for w in (first, narrow, wide)]
    gains = first[:, 0, :, 3 * half : 3 * half + 2].reshape(model, 2).astype(F32)
    gain_one, gain_two = gains[:, 0].reshape(1, model), gains[:, 1].reshape(1, model)
    if not lines:
        qkv = project_qkv(x, gain_one, first, cosine, sine)
        attended, lse, kmem, vmem = attend(idx, qkv, near, far)
    hops = nz if lines else 0
    ghid, gn2, *fed = feed(
        x, attended, cot, gain_two, narrow, wide, units, hops
    )
    left = [fed[3], fed[1], fed[2]] if lines else []
    backed = back(
        picture_start,
        qkv,
        kmem,
        vmem,
        attended,
        lse,
        first,
        narrow,
        x,
        gain_one,
        ghid,
        gn2,
        cosine,
        sine,
        hops,
        *left,
    )
    if lines:
        out = fed[0]
        input_grad, model_grads, grad_out, feed_grads, grad_down, norms = backed
        grad_out, grad_down = grad_out.T, grad_down.T
        grad_gate, grad_up = feed_grads[0], feed_grads[1]
        norms = lax.dynamic_slice_in_dim(norms[:2], lax.axis_index("col") % 2 * rows, rows, 1).T
    else:
        out, input_grad = own_features(fed[0], me), own_features(backed[0], me)
        feed_grads, model_grads = summed(*fed[1:]), summed(*backed[1:3])
        norms = jnp.concatenate([backed[3], gn2], axis=0).T
        norms = lax.psum_scatter(norms, ("dp", "col"), scatter_dimension=0, tiled=True)
        norms = lax.psum(norms, "row")
        grad_out, grad_down = model_grads[3].T, feed_grads[2].T
        grad_gate, grad_up = feed_grads[0], feed_grads[1]
    return (
        out,
        input_grad,
        model_grads[0],
        model_grads[1],
        model_grads[2],
        grad_out,
        grad_gate,
        grad_up,
        grad_down,
        norms[:, 0],
        norms[:, 1],
    )


def solution(mesh):
    tokens = P(("dp", "col"), "row")
    down = P("row", ("dp", "col"))
    gain = P(("dp", "col"))
    cache = P(("dp", "col"), None, "row")
    index = P(("dp", "col"), None, None)
    weights = (tokens, tokens, tokens, down, tokens, tokens, down)
    return jax.shard_map(
        on_device,
        mesh=mesh,
        in_specs=(tokens,)
        + weights
        + (gain, gain, cache, cache, index, index, P(("dp", "col"), None), gain, tokens),
        out_specs=(tokens, tokens) + weights + (gain, gain),
        check_vma=False,
    )
```
